128 devices in a mesh: gx: 4 (over x_lo, core), gy: 8 (over z, x_hi), gz: 4 (over y).
Axes of the slice: x: 4 (x_hi: 2, x_lo: 2; x = x_hi * 2 + x_lo), y: 4, z: 4, core: 2. Of those that a mesh axis runs over, the one named last changes fastest.
Arguments:
- load: float32 [3, 128, 256, 512], P(None, 'gz', 'gy', 'gx'), may hold values from -6 to 6
- labels: int32 [128, 256, 512], P('gz', 'gy', 'gx'), may hold values from 0 to 15
- mask: int32 [128, 256, 512], P('gz', 'gy', 'gx'), may hold values 0 or 1
- table: float32 [16], replicated, may hold values from 0.25 to 2
Outputs:
- displacement: float32 [3, 128, 256, 512], P(None, 'gz', 'gy', 'gx')
- residual: float32 [3, 128, 256, 512], P(None, 'gz', 'gy', 'gx')
The draws below stay inside these ranges and needn't reach their ends.
All inputs are finite; a program needn't handle non-finite values. No bound on the sum of `mask` on one device may be relied on, other than what follows from the above.
Results may differ from the reference program's by a relative error of at most 0.0003.
Values sent between devices are 32-bit elements; how exact they have to be, the bound alone decides.
A program may use at most 128 MiB of HBM per device.

```python
import math
import jax
import jax.numpy as jnp
from jax import lax

BRICK = 32
INTERSECTION = 4
MATERIALS = 16
SWEEPS = 2
NZ = 128
NY = 256
NX = 512


def draw_load(key, part):
    shape = (3, NZ, NY, NX)
    first = jax.random.fold_in(jax.random.fold_in(key, 11), 0)
    return jnp.clip(jax.random.normal(first, shape, jnp.float32), -6.0, 6.0)


def place_ends(values, stream_key, smallest, largest):
    spot = [jax.random.randint(jax.random.fold_in(stream_key, axis), (), 0, length) for axis, length in enumerate(values.shape)]
    longest = values.shape.index(max(values.shape))
    neighbour = spot[:longest] + [(spot[longest] + 1) % values.shape[longest]] + spot[longest + 1:]
    return values.at[tuple(spot)].set(smallest).at[tuple(neighbour)].set(largest)


def setup_inputs(seed: int = 0) -> dict:
    splits = jax.random.split(jax.random.key(seed), 5)
    load = draw_load(jax.random.fold_in(splits[4], 71), 0)
    labels = place_ends(jax.random.randint(splits[1], (NZ, NY, NX), 0, MATERIALS), jax.random.fold_in(splits[1], 1), 0, MATERIALS - 1).astype(jnp.int32)
    mask = place_ends((jax.random.randint(splits[2], (NZ, NY, NX), 0, 4) < 3).astype(jnp.int32), jax.random.fold_in(splits[2], 1), 0, 1)
    table = jnp.clip(jnp.exp(jax.random.uniform(splits[3], (MATERIALS,), jnp.float32, math.log(0.25), math.log(2.0))), 0.25, 2.0)
    return dict(load=load, labels=labels, mask=mask, table=table)


LAMBDA_RATIO = 2.0
SIGMA_SHIFT = 0.1
REF_MODULUS = 1.5
VOID_MODULUS = 0.1
HIGHEST = lax.Precision.HIGHEST

def stiffness_ratio(component, direction):
    return LAMBDA_RATIO if component == direction else 1.0

def sine_table(length):
    grid = jnp.arange(1, length + 1, dtype=jnp.float32)
    return jnp.sqrt(2.0 / (length + 1)) * jnp.sin(jnp.pi * grid[:, None] * grid[None, :] / (length + 1))

def eigen_values(length):
    grid = jnp.arange(1, length + 1, dtype=jnp.float32)
    return 2.0 - 2.0 * jnp.cos(jnp.pi * grid / (length + 1))

def ramp_weights(length, margin):
    position = jnp.arange(length, dtype=jnp.float32)
    rising = (position + 0.5) / (2 * margin)
    falling = (length - 0.5 - position) / (2 * margin)
    return jnp.minimum(jnp.minimum(rising, falling), 1.0)

def operator_core(padded_field, padded_modulus):
    centre_modulus = padded_modulus[1:-1, 1:-1, 1:-1]
    centre = padded_field[:, 1:-1, 1:-1, 1:-1]
    results = []
    for component in range(3):
        total = SIGMA_SHIFT * centre_modulus * centre[component]
        for direction in range(3):
            for offset in (0, 2):
                window = [slice(1, -1), slice(1, -1), slice(1, -1)]
                window[direction] = slice(offset, offset + centre_modulus.shape[direction])
                window = tuple(window)
                face = 0.5 * (centre_modulus + padded_modulus[window])
                total = total + stiffness_ratio(component, direction) * face * (centre[component] - padded_field[component][window])
        results.append(total)
    return jnp.stack(results)

def apply_operator(field, modulus):
    padded_field = jnp.pad(field, ((0, 0), (1, 1), (1, 1), (1, 1)))
    padded_modulus = jnp.pad(modulus, 1)
    return operator_core(padded_field, padded_modulus)

def transform_all(values, along_x, along_rest):
    values = jnp.einsum('czyx,xk->czyk', values, along_x, precision=HIGHEST)
    values = jnp.einsum('czyx,yk->czkx', values, along_rest, precision=HIGHEST)
    return jnp.einsum('czyx,zk->ckyx', values, along_rest, precision=HIGHEST)

def reference(load, labels, mask, table):
    modulus = jnp.where(mask == 1, jnp.take(table, labels), VOID_MODULUS)
    length = BRICK + 2 * INTERSECTION
    sine = sine_table(length)
    eigen = eigen_values(length)
    denominators = jnp.stack([REF_MODULUS * (stiffness_ratio(component, 0) * eigen[:, None, None] + stiffness_ratio(component, 1) * eigen[None, :, None] + stiffness_ratio(component, 2) * eigen[None, None, :] + SIGMA_SHIFT) for component in range(3)])
    ramp = ramp_weights(length, INTERSECTION)
    weight_cube = ramp[:, None, None] * ramp[None, :, None] * ramp[None, None, :]
    rows_y = NY // BRICK
    rows_x = NX // BRICK
    number_bricks = NZ // BRICK * rows_y * rows_x
    solution = jnp.zeros_like(load)
    residual = load
    for sweep in range(SWEEPS):
        padded = jnp.pad(residual, ((0, 0), (INTERSECTION, INTERSECTION), (INTERSECTION, INTERSECTION), (INTERSECTION, INTERSECTION)))

        def add_brick(total, number, padded=padded):
            layer = number // (rows_y * rows_x)
            column_y = number // rows_x % rows_y
            column_x = number % rows_x
            starts = (jnp.int32(0), (layer * BRICK).astype(jnp.int32), (column_y * BRICK).astype(jnp.int32), (column_x * BRICK).astype(jnp.int32))
            piece = lax.dynamic_slice(padded, starts, (3, length, length, length))
            solved = transform_all(transform_all(piece * weight_cube, sine, sine) / denominators, sine, sine)
            current = lax.dynamic_slice(total, starts, (3, length, length, length))
            return (lax.dynamic_update_slice(total, current + solved, starts), None)
        summed, _ = lax.scan(add_brick, jnp.zeros_like(padded), jnp.arange(number_bricks, dtype=jnp.int32))
        correction = summed[:, INTERSECTION:-INTERSECTION, INTERSECTION:-INTERSECTION, INTERSECTION:-INTERSECTION]
        solution = solution + correction
        residual = residual - apply_operator(correction, modulus)
    return (solution, residual)
```

```python
import jax
import jax.numpy as jnp
import numpy as np
from jax import lax
from jax.experimental import pallas as pl
from jax.experimental.pallas import tpu as pltpu
from jax.sharding import PartitionSpec as P

BRICK = 32
MARGIN = 4
SWEEPS = 2
LENGTH = BRICK + 2 * MARGIN
LANES = 128
WIDE = 256
ROWS = LENGTH * LENGTH
PADDED = 1664
CHUNKS = PADDED // LANES
OWNED = BRICK * LENGTH
LAMBDA_RATIO = 2.0
SIGMA_SHIFT = 0.1
REF_MODULUS = 1.5
VOID_MODULUS = 0.1
MESH = pl.DeviceIdType.MESH
PHASES = 9
AY, AZ, AX, BX, BZ, BY, CY, CZ, CX = range(PHASES)
AXIS = {AY: "gy", AZ: "gz", AX: "gx", BX: "gx", BZ: "gz", BY: "gy", CY: "gy", CZ: "gz", CX: "gx"}
F32 = jnp.float32
BF16 = jnp.bfloat16


def ratio(component, direction):
    return LAMBDA_RATIO if component == direction else 1.0


def halves(values):
    high = values.astype(BF16)
    return high, (values - high.astype(F32)).astype(BF16)


def constants():
    grid = np.arange(1, LENGTH + 1, dtype=np.float64)
    sine = np.sqrt(2.0 / (LENGTH + 1)) * np.sin(np.pi * grid[:, None] * grid[None, :] / (LENGTH + 1))
    eigen = 2.0 - 2.0 * np.cos(np.pi * grid / (LENGTH + 1))
    spot = np.arange(LENGTH, dtype=np.float64)
    ramp = np.minimum(np.minimum((spot + 0.5) / (2 * MARGIN), (LENGTH - 0.5 - spot) / (2 * MARGIN)), 1.0)
    ramped = ramp[:, None] * sine
    place = np.concatenate([np.arange(MARGIN, MARGIN + BRICK), np.arange(MARGIN), np.arange(MARGIN + BRICK, LENGTH)])
    forward = ramped[place].T
    backward = sine.T[place]
    count = LANES // BRICK
    wide_x = LANES + 2 * MARGIN
    forward_x = np.zeros((wide_x, WIDE))
    backward_x = np.zeros((WIDE, wide_x))
    for brick in range(count):
        rows = slice(brick * BRICK, brick * BRICK + LENGTH)
        columns = slice(brick * LENGTH, (brick + 1) * LENGTH)
        forward_x[rows, columns] = ramped
        backward_x[columns, rows] = sine
    into = np.zeros((WIDE, WIDE))
    into[:LANES] = forward_x[MARGIN:MARGIN + LANES]
    into[LANES:LANES + MARGIN] = forward_x[:MARGIN]
    into[LANES + MARGIN:LANES + 2 * MARGIN] = forward_x[MARGIN + LANES:]
    out = backward_x[:, MARGIN:MARGIN + LANES]
    edge = np.concatenate([backward_x[:, :MARGIN], backward_x[:, MARGIN + LANES:]], axis=1).T
    eigen_x = np.zeros((1, WIDE))
    eigen_x[0, : count * LENGTH] = np.tile(eigen, count)
    eigen_lanes = np.broadcast_to(eigen[:, None], (LENGTH, WIDE))
    take4 = np.zeros((8, LANES))
    take1 = np.zeros((8, LANES))
    for i in range(MARGIN):
        take4[i, i] = 1.0
        take4[MARGIN + i, LANES - MARGIN + i] = 1.0
    take1[0, 0] = 1.0
    take1[1, LANES - 1] = 1.0

    def split(matrix, stack):
        matrix = matrix.astype(np.float32)
        high = matrix.astype(BF16)
        low = (matrix - high.astype(np.float32)).astype(BF16)
        return np.concatenate([high, low], axis=0) if stack else (high, low)

    return (
        split(forward, True),
        split(backward, True),
        *split(into, False),
        *split(out, False),
        split(edge, True),
        eigen_x.astype(np.float32),
        np.ascontiguousarray(eigen_lanes).astype(np.float32),
        take4.astype(BF16),
        take1.astype(BF16),
    ), eigen


def dot(a, b):
    return jnp.dot(a, b, preferred_element_type=F32)


def dot_nt(a, b):
    return lax.dot_general(a, b, (((1,), (1,)), ((), ())), preferred_element_type=F32)


def apply_left(stacked, values):
    size = LENGTH
    high, low = halves(values)
    both = dot(stacked, high)
    return both[:size] + both[size:] + dot(stacked[:size], low)


def kernel(
    load, labels, mask, table,
    fwd, bwd, into_hi, into_lo, out_hi, out_lo, edge, eigen_x, eigen_rows, take4, take1,
    disp, resid,
    modulus, faces, w, xs, xr, b1a, b1b, b2a, b2b, zb, fs, fr, zr, ys, yr, corr, rinv,
    cys, cyr, czs, czr, cxs, cxr,
    send_sem, recv_sem,
):
    index = {a: lax.axis_index(a) for a in ("gx", "gy", "gz")}
    count = {a: lax.axis_size(a) for a in ("gx", "gy", "gz")}
    lower = {a: lax.rem(index[a] + count[a] - 1, count[a]) for a in index}
    upper = {a: lax.rem(index[a] + 1, count[a]) for a in index}
    has_lower = {a: index[a] > 0 for a in index}
    has_upper = {a: index[a] < count[a] - 1 for a in index}

    barrier = pltpu.get_barrier_semaphore()
    for a in ("gx", "gy", "gz"):
        pl.semaphore_signal(barrier, inc=1, device_id={a: lower[a]}, device_id_type=MESH)
        pl.semaphore_signal(barrier, inc=1, device_id={a: upper[a]}, device_id_type=MESH)
    pl.semaphore_wait(barrier, 6)

    def copies(slot, phase, down, up):
        a = AXIS[phase]
        made = []
        for side, (source, target), device in ((0, down, lower[a]), (1, up, upper[a])):
            number = (slot * PHASES + phase) * 2 + side
            made.append(pltpu.make_async_remote_copy(
                src_ref=source, dst_ref=target,
                send_sem=send_sem.at[number], recv_sem=recv_sem.at[number],
                device_id={a: device}, device_id_type=MESH,
            ))
        return made

    pending = {}

    def send(slot, phase, down, up):
        made = copies(slot, phase, down, up)
        for copy in made:
            copy.start()
        pending[slot, phase] = made

    def arrive(slot, phase):
        for copy in pending[slot, phase]:
            copy.wait_recv()

    def keep(flag, values):
        return jnp.where(flag, values, 0.0)

    def face_columns(values):
        flat = values.reshape(BRICK * BRICK, LANES)
        high, low = halves(flat)
        return dot_nt(take1[...], high) + dot_nt(take1[...], low)

    def halo_send(slot, values):
        cys[slot, 0] = values[:, 0, :]
        cys[slot, 1] = values[:, BRICK - 1, :]
        czs[slot, 0] = values[0]
        czs[slot, 1] = values[BRICK - 1]
        cxs[slot] = face_columns(values)
        send(slot, CY, (cys.at[slot, 0], cyr.at[slot, 1]), (cys.at[slot, 1], cyr.at[slot, 0]))
        send(slot, CZ, (czs.at[slot, 0], czr.at[slot, 1]), (czs.at[slot, 1], czr.at[slot, 0]))
        send(slot, CX, (cxs.at[slot], cxr.at[slot, 1]), (cxs.at[slot], cxr.at[slot, 0]))

    def halo_get(slot):
        for phase in (CY, CZ, CX):
            arrive(slot, phase)
        low_y = keep(has_lower["gy"], cyr[slot, 0])
        high_y = keep(has_upper["gy"], cyr[slot, 1])
        low_z = keep(has_lower["gz"], czr[slot, 0])
        high_z = keep(has_upper["gz"], czr[slot, 1])
        left = keep(has_lower["gx"], cxr[slot, 0, 1:2, :])
        right = keep(has_upper["gx"], cxr[slot, 1, 0:1, :])
        side = jnp.concatenate([left, jnp.zeros((LANES - 2, BRICK * BRICK), F32), right], axis=0)
        side = jnp.concatenate(
            [jnp.transpose(side[:, i * LANES:(i + 1) * LANES]) for i in range(8)], axis=0
        ).reshape(BRICK, BRICK, LANES)
        return low_y, high_y, low_z, high_z, side

    def shifts(values, halo):
        low_y, high_y, low_z, high_z, side = halo
        lane = lax.broadcasted_iota(jnp.int32, values.shape, 2)
        yield jnp.concatenate([low_z[None], values[:-1]], axis=0)
        yield jnp.concatenate([values[1:], high_z[None]], axis=0)
        yield jnp.concatenate([low_y[:, None, :], values[:, :-1]], axis=1)
        yield jnp.concatenate([values[:, 1:], high_y[:, None, :]], axis=1)
        yield jnp.where(lane == 0, side, jnp.roll(values, 1, axis=2))
        yield jnp.where(lane == LANES - 1, side, jnp.roll(values, -1, axis=2))

    def a_start(s, c):
        slot = s * 3 + c
        values = w[slot, 0:OWNED, :].reshape(BRICK, LENGTH, LANES)
        ys[slot, 0] = values[:, 0:MARGIN, :]
        ys[slot, 1] = values[:, BRICK - MARGIN:BRICK, :]
        send(slot, AY, (ys.at[slot, 0], yr.at[slot, 1]), (ys.at[slot, 1], yr.at[slot, 0]))

    def a_z(s, c):
        slot = s * 3 + c
        arrive(slot, AY)
        low = keep(has_lower["gy"], yr[slot, 0])
        high = keep(has_upper["gy"], yr[slot, 1])
        for z in range(BRICK):
            w[slot, z * LENGTH + BRICK:(z + 1) * LENGTH, :] = jnp.concatenate([low[z], high[z]], axis=0)
        first, last = MARGIN * LENGTH, OWNED - MARGIN * LENGTH
        send(
            slot, AZ,
            (w.at[slot, pl.ds(0, first)], w.at[slot, pl.ds(OWNED + first, first)]),
            (w.at[slot, pl.ds(last, first)], w.at[slot, pl.ds(OWNED, first)]),
        )

    def a_x(s, c):
        slot = s * 3 + c
        arrive(slot, AZ)
        part = MARGIN * LENGTH
        low = w[slot, OWNED:OWNED + part, :]
        w[slot, OWNED:OWNED + part, :] = keep(has_lower["gz"], low)
        high = w[slot, OWNED + part:ROWS, :]
        w[slot, OWNED + part:ROWS, :] = keep(has_upper["gz"], high)

        def chunk(i, carry):
            at = pl.ds(pl.multiple_of(i * LANES, LANES), LANES)
            high, low = halves(w[slot, at, :])
            xs[slot, :, at] = dot_nt(take4[...], high) + dot_nt(take4[...], low)
            return carry

        lax.fori_loop(0, CHUNKS, chunk, 0)
        send(slot, AX, (xs.at[slot], xr.at[slot, 1]), (xs.at[slot], xr.at[slot, 0]))

    def solve(s, c):
        slot = s * 3 + c
        arrive(slot, AX)

        def forward_x(i, carry):
            at = pl.ds(pl.multiple_of(i * LANES, LANES), LANES)
            left = keep(has_lower["gx"], xr[slot, 0, MARGIN:, at])
            right = keep(has_upper["gx"], xr[slot, 1, :MARGIN, at])
            side = jnp.transpose(jnp.concatenate([left, right, jnp.zeros((LANES - 8, LANES), F32)], axis=0))
            high, low = halves(jnp.concatenate([w[slot, at, :], side], axis=1))
            out = dot(high, into_hi[...]) + dot(low, into_hi[...]) + dot(high, into_lo[...])
            b1a[at, :] = out[:, :LANES]
            b1b[at, :] = out[:, LANES:]
            return carry

        lax.fori_loop(0, CHUNKS, forward_x, 0)

        def forward_y(i, carry):
            for k in range(4):
                z = i * 4 + k
                at = pl.ds(pl.multiple_of(z * LENGTH, 8), LENGTH)
                out = apply_left(fwd[...], jnp.concatenate([b1a[at, :], b1b[at, :]], axis=1))
                b2a[pl.ds(z, LENGTH, stride=LENGTH), :] = out[:, :LANES]
                b2b[pl.ds(z, LENGTH, stride=LENGTH), :] = out[:, LANES:]
            return carry

        lax.fori_loop(0, LENGTH // 4, forward_y, 0)

        def solve_z(i, carry):
            for k in range(4):
                y = i * 4 + k
                at = pl.ds(pl.multiple_of(y * LENGTH, 8), LENGTH)
                out = apply_left(fwd[...], jnp.concatenate([b2a[at, :], b2b[at, :]], axis=1))
                out = apply_left(bwd[...], out * rinv[c, at, :])
                b1a[pl.ds(y, LENGTH, stride=LENGTH), :] = out[:, :LANES]
                b1b[pl.ds(y, LENGTH, stride=LENGTH), :] = out[:, LANES:]
            return carry

        lax.fori_loop(0, LENGTH // 4, solve_z, 0)

        def backward_y(i, carry):
            for k in range(4):
                z = i * 4 + k
                at = pl.ds(pl.multiple_of(z * LENGTH, 8), LENGTH)
                out = apply_left(bwd[...], jnp.concatenate([b1a[at, :], b1b[at, :]], axis=1))
                b2a[at, :] = out[:, :LANES]
                b2b[at, :] = out[:, LANES:]
            return carry

        lax.fori_loop(0, LENGTH // 4, backward_y, 0)

        def backward_x(i, carry):
            at = pl.ds(pl.multiple_of(i * LANES, LANES), LANES)
            high, low = halves(jnp.concatenate([b2a[at, :], b2b[at, :]], axis=1))
            zb[slot, at, :] = dot(high, out_hi[...]) + dot(low, out_hi[...]) + dot(high, out_lo[...])
            both = dot_nt(edge[...], high)
            fs[slot, :, at] = both[:8] + both[8:] + dot_nt(edge[0:8, :], low)
            return carry

        lax.fori_loop(0, CHUNKS, backward_x, 0)
        send(slot, BX, (fs.at[slot], fr.at[slot, 1]), (fs.at[slot], fr.at[slot, 0]))

    def b_z(s, c):
        slot = s * 3 + c
        arrive(slot, BX)

        def chunk(i, carry):
            at = pl.ds(pl.multiple_of(i * LANES, LANES), LANES)
            left = keep(has_lower["gx"], fr[slot, 0, MARGIN:, at])
            right = keep(has_upper["gx"], fr[slot, 1, :MARGIN, at])
            side = jnp.concatenate([left, jnp.zeros((LANES - 8, LANES), F32), right], axis=0)
            zb[slot, at, :] += jnp.transpose(side)
            return carry

        lax.fori_loop(0, CHUNKS, chunk, 0)
        part = MARGIN * LENGTH
        send(
            slot, BZ,
            (zb.at[slot, pl.ds(OWNED, part)], zr.at[slot, 1]),
            (zb.at[slot, pl.ds(OWNED + part, part)], zr.at[slot, 0]),
        )

    def b_y(s, c):
        slot = s * 3 + c
        arrive(slot, BZ)
        part = MARGIN * LENGTH
        zb[slot, 0:part, :] += keep(has_lower["gz"], zr[slot, 0])
        zb[slot, OWNED - part:OWNED, :] += keep(has_upper["gz"], zr[slot, 1])
        other = slot + 6
        for z in range(BRICK):
            rows = zb[slot, z * LENGTH + BRICK:(z + 1) * LENGTH, :]
            ys[other, 0, z] = rows[:MARGIN]
            ys[other, 1, z] = rows[MARGIN:]
        send(slot, BY, (ys.at[other, 0], yr.at[other, 1]), (ys.at[other, 1], yr.at[other, 0]))

    def c_start(s, c):
        slot = s * 3 + c
        arrive(slot, BY)
        other = slot + 6
        low = keep(has_lower["gy"], yr[other, 0])
        high = keep(has_upper["gy"], yr[other, 1])
        own = zb[slot, 0:OWNED, :].reshape(BRICK, LENGTH, LANES)[:, :BRICK]
        blank = jnp.zeros((BRICK, MARGIN, LANES), F32)
        own = jnp.concatenate([
            own[:, :8] + jnp.concatenate([low, blank], axis=1),
            own[:, 8:24],
            own[:, 24:] + jnp.concatenate([blank, high], axis=1),
        ], axis=1)
        corr[slot] = own
        halo_send(slot, own)
        if s == 0:
            disp[c] = own
        else:
            disp[c] += own

    def update(s, c):
        slot = s * 3 + c
        halo = halo_get(slot)
        values = corr[slot]
        total = SIGMA_SHIFT * modulus[...] * values
        for number, moved in enumerate(shifts(values, halo)):
            total = total + (ratio(c, number // 2) * 0.5) * faces[number] * (values - moved)
        if s == 0:
            old = load[c]
        else:
            old = w[slot, 0:OWNED, :].reshape(BRICK, LENGTH, LANES)[:, :BRICK]
        new = old - total
        if s == SWEEPS - 1:
            resid[c] = new
        else:
            for z in range(BRICK):
                w[slot + 3, z * LENGTH:z * LENGTH + BRICK, :] = new[z]

    for c in range(3):
        for z in range(BRICK):
            w[c, z * LENGTH:z * LENGTH + BRICK, :] = load[c, z]
    for slot in range(6):
        w[slot, ROWS:, :] = jnp.zeros((PADDED - ROWS, LANES), F32)
    for c in range(3):
        a_start(0, c)

    def look(z, carry):
        picked = labels[z]
        value = jnp.zeros(picked.shape, F32)
        for number in range(table.shape[0]):
            value = jnp.where(picked == number, table[number], value)
        modulus[z] = jnp.where(mask[z] == 1, value, VOID_MODULUS)
        return carry

    lax.fori_loop(0, BRICK, look, 0)
    halo_send(6, modulus[...])

    for c in range(3):
        def invert(y, carry, c=c):
            at = pl.ds(pl.multiple_of(y * LENGTH, 8), LENGTH)
            rinv[c, at, :] = 1.0 / (REF_MODULUS * (
                ratio(c, 0) * eigen_rows[...]
                + ratio(c, 1) * eigen_rows[pl.ds(y, 1), :]
                + ratio(c, 2) * eigen_x[...]
                + SIGMA_SHIFT
            ))
            return carry

        lax.fori_loop(0, LENGTH, invert, 0)

    own = modulus[...]
    for number, moved in enumerate(shifts(own, halo_get(6))):
        faces[number] = own + moved

    for s in range(SWEEPS):
        for stage in (a_z, a_x, solve, b_z, b_y, c_start, update):
            for c in range(3):
                stage(s, c)
                if stage is update and s < SWEEPS - 1:
                    a_start(s + 1, c)

    for made in pending.values():
        for copy in made:
            copy.wait_send()


def local(load, labels, mask, table):
    tables, _ = constants()
    vmem = pl.BlockSpec(memory_space=pltpu.VMEM)
    smem = pl.BlockSpec(memory_space=pltpu.SMEM)
    slots = 3 * SWEEPS
    field = jax.ShapeDtypeStruct(load.shape, F32)
    block = (BRICK, BRICK, LANES)
    return pl.pallas_call(
        kernel,
        out_shape=(field, field),
        in_specs=[vmem, vmem, vmem, smem] + [vmem] * len(tables),
        out_specs=(vmem, vmem),
        scratch_shapes=[
            pltpu.VMEM(block, F32),
            pltpu.VMEM((6,) + block, F32),
            pltpu.VMEM((slots, PADDED, LANES), F32),
            pltpu.VMEM((slots, 8, PADDED), F32),
            pltpu.VMEM((slots, 2, 8, PADDED), F32),
            pltpu.VMEM((PADDED, LANES), F32),
            pltpu.VMEM((PADDED, LANES), F32),
            pltpu.VMEM((PADDED, LANES), F32),
            pltpu.VMEM((PADDED, LANES), F32),
            pltpu.VMEM((slots, PADDED, LANES), F32),
            pltpu.VMEM((slots, 8, PADDED), F32),
            pltpu.VMEM((slots, 2, 8, PADDED), F32),
            pltpu.VMEM((slots, 2, MARGIN * LENGTH, LANES), F32),
            pltpu.VMEM((2 * slots, 2, BRICK, MARGIN, LANES), F32),
            pltpu.VMEM((2 * slots, 2, BRICK, MARGIN, LANES), F32),
            pltpu.VMEM((slots,) + block, F32),
            pltpu.VMEM((3, ROWS, WIDE), F32),
            pltpu.VMEM((slots + 1, 2, BRICK, LANES), F32),
            pltpu.VMEM((slots + 1, 2, BRICK, LANES), F32),
            pltpu.VMEM((slots + 1, 2, BRICK, LANES), F32),
            pltpu.VMEM((slots + 1, 2, BRICK, LANES), F32),
            pltpu.VMEM((slots + 1, 8, BRICK * BRICK), F32),
            pltpu.VMEM((slots + 1, 2, 8, BRICK * BRICK), F32),
            pltpu.SemaphoreType.DMA(((slots + 1) * PHASES * 2,)),
            pltpu.SemaphoreType.DMA(((slots + 1) * PHASES * 2,)),
        ],
        compiler_params=pltpu.CompilerParams(
            collective_id=0, has_side_effects=True, vmem_limit_bytes=62 * 1024 * 1024
        ),
    )(load, labels, mask, table, *tables)


def solution(mesh):
    placed = (P(None, "gz", "gy", "gx"), P("gz", "gy", "gx"), P("gz", "gy", "gx"), P())
    return jax.shard_map(
        local,
        mesh=mesh,
        in_specs=placed,
        out_specs=(P(None, "gz", "gy", "gx"), P(None, "gz", "gy", "gx")),
        check_vma=False,
    )
```

```python
import jax
import jax.numpy as jnp
import numpy as np
from jax import lax
from jax.experimental import pallas as pl
from jax.experimental.pallas import tpu as pltpu
from jax.sharding import PartitionSpec as P

BRICK = 32
MARGIN = 4
SWEEPS = 2
LENGTH = BRICK + 2 * MARGIN
LANES = 128
WIDE = 256
ROWS = LENGTH * LENGTH
PADDED = 1664
CHUNKS = PADDED // LANES
OWNED = BRICK * LENGTH
LAMBDA_RATIO = 2.0
SIGMA_SHIFT = 0.1
REF_MODULUS = 1.5
VOID_MODULUS = 0.1
MESH = pl.DeviceIdType.MESH
UNROLL = 5
PHASES = 9
AY, AZ, AX, BX, BZ, BY, CY, CZ, CX = range(PHASES)
AXIS = {AY: "gy", AZ: "gz", AX: "gx", BX: "gx", BZ: "gz", BY: "gy", CY: "gy", CZ: "gz", CX: "gx"}
F32 = jnp.float32
BF16 = jnp.bfloat16


def ratio(component, direction):
    return LAMBDA_RATIO if component == direction else 1.0


def halves(values):
    high = values.astype(BF16)
    return high, (values - high.astype(F32)).astype(BF16)


def constants():
    grid = np.arange(1, LENGTH + 1, dtype=np.float64)
    sine = np.sqrt(2.0 / (LENGTH + 1)) * np.sin(np.pi * grid[:, None] * grid[None, :] / (LENGTH + 1))
    eigen = 2.0 - 2.0 * np.cos(np.pi * grid / (LENGTH + 1))
    spot = np.arange(LENGTH, dtype=np.float64)
    ramp = np.minimum(np.minimum((spot + 0.5) / (2 * MARGIN), (LENGTH - 0.5 - spot) / (2 * MARGIN)), 1.0)
    ramped = ramp[:, None] * sine
    place = np.concatenate([np.arange(MARGIN, MARGIN + BRICK), np.arange(MARGIN), np.arange(MARGIN + BRICK, LENGTH)])
    forward = ramped[place].T
    backward = sine.T[place]
    count = LANES // BRICK
    wide_x = LANES + 2 * MARGIN
    forward_x = np.zeros((wide_x, WIDE))
    backward_x = np.zeros((WIDE, wide_x))
    for brick in range(count):
        rows = slice(brick * BRICK, brick * BRICK + LENGTH)
        columns = slice(brick * LENGTH, (brick + 1) * LENGTH)
        forward_x[rows, columns] = ramped
        backward_x[columns, rows] = sine
    edge = slice(LANES, LANES + 2 * MARGIN)
    into = forward_x[MARGIN:MARGIN + LANES]
    into_edge = np.concatenate([forward_x[:MARGIN], forward_x[MARGIN + LANES:]])
    out = np.zeros((WIDE, WIDE))
    out[:, :LANES] = backward_x[:, MARGIN:MARGIN + LANES]
    out[:, edge] = np.concatenate([backward_x[:, :MARGIN], backward_x[:, MARGIN + LANES:]], axis=1)
    rest = count * LENGTH - LANES
    eigen_x = np.zeros((1, WIDE))
    eigen_x[0, : count * LENGTH] = np.tile(eigen, count)
    eigen_lanes = np.broadcast_to(eigen[:, None], (LENGTH, WIDE))

    def high(matrix):
        return matrix.astype(np.float32).astype(BF16).astype(np.float64)

    def low(matrix):
        return matrix - high(matrix)

    def pair(matrix):
        zero = np.zeros((LENGTH, LENGTH))
        both = np.block([[matrix, zero], [zero, matrix]])
        return np.concatenate([high(both), high(both), low(both)], axis=1)

    def tall(*parts):
        blank = np.zeros((2 * LANES - sum(p.shape[0] for p in parts), WIDE))
        return np.concatenate(parts + (blank,))

    head, tail = out[:LANES], out[LANES:LANES + rest]
    return [m.astype(BF16) for m in (
        pair(forward),
        pair(backward),
        tall(high(into), high(into)),
        tall(low(into), high(into_edge), high(into_edge), low(into_edge)),
        tall(high(head), high(head)),
        tall(low(head), high(tail), high(tail), low(tail)),
    )] + [eigen_x.astype(np.float32), np.ascontiguousarray(eigen_lanes).astype(np.float32)]


def dot(a, b):
    return jnp.dot(a, b, preferred_element_type=F32)


def triple(values):
    high, low = halves(values)
    return jnp.concatenate([high, low, high], axis=0)


def kernel(
    load, labels, mask, table,
    fwd, bwd, into_1, into_2, out_1, out_2, eigen_x, eigen_rows,
    disp, resid,
    modulus, faces, w, xs, xr, b1a, b1b, b2a, b2b, zb, fs, fr, zr, ys, yr, corr, rinv,
    cys, cyr, czs, czr, cxs, cxr,
    send_sem, recv_sem,
):
    index = {a: lax.axis_index(a) for a in ("gx", "gy", "gz")}
    count = {a: lax.axis_size(a) for a in ("gx", "gy", "gz")}
    lower = {a: lax.rem(index[a] + count[a] - 1, count[a]) for a in index}
    upper = {a: lax.rem(index[a] + 1, count[a]) for a in index}
    has_lower = {a: index[a] > 0 for a in index}
    has_upper = {a: index[a] < count[a] - 1 for a in index}

    barrier = pltpu.get_barrier_semaphore()
    for a in ("gx", "gy", "gz"):
        pl.semaphore_signal(barrier, inc=1, device_id={a: lower[a]}, device_id_type=MESH)
        pl.semaphore_signal(barrier, inc=1, device_id={a: upper[a]}, device_id_type=MESH)
    pl.semaphore_wait(barrier, 6)

    def copies(slot, phase, down, up):
        a = AXIS[phase]
        made = []
        for side, (source, target), device in ((0, down, lower[a]), (1, up, upper[a])):
            number = (slot * PHASES + phase) * 2 + side
            made.append(pltpu.make_async_remote_copy(
                src_ref=source, dst_ref=target,
                send_sem=send_sem.at[number], recv_sem=recv_sem.at[number],
                device_id={a: device}, device_id_type=MESH,
            ))
        return made

    pending = {}

    def send(slot, phase, down, up):
        made = copies(slot, phase, down, up)
        for copy in made:
            copy.start()
        pending[slot, phase] = made

    def arrive(slot, phase):
        for copy in pending[slot, phase]:
            copy.wait_recv()

    def keep(flag, values):
        return jnp.where(flag, values, 0.0)

    lanes = lax.broadcasted_iota(jnp.int32, (LANES, LANES), 1)

    def face_columns(values):
        flat = values.reshape(BRICK * BRICK, LANES)
        total = jnp.zeros((LANES, LANES), F32)
        for i in range(8):
            part = pltpu.roll(flat[i * LANES:(i + 1) * LANES], 2 * i + 1, 1)
            total = jnp.where((lanes == 2 * i) | (lanes == 2 * i + 1), part, total)
        return jnp.transpose(total)[:16]

    def halo_send(slot, values):
        cys[slot, 0] = values[:, 0, :]
        cys[slot, 1] = values[:, BRICK - 1, :]
        czs[slot, 0] = values[0]
        czs[slot, 1] = values[BRICK - 1]
        cxs[slot] = face_columns(values)
        send(slot, CY, (cys.at[slot, 0], cyr.at[slot, 1]), (cys.at[slot, 1], cyr.at[slot, 0]))
        send(slot, CZ, (czs.at[slot, 0], czr.at[slot, 1]), (czs.at[slot, 1], czr.at[slot, 0]))
        send(slot, CX, (cxs.at[slot], cxr.at[slot, 1]), (cxs.at[slot], cxr.at[slot, 0]))

    def halo_get(slot):
        for phase in (CY, CZ, CX):
            arrive(slot, phase)
        low_y = keep(has_lower["gy"], cyr[slot, 0])
        high_y = keep(has_upper["gy"], cyr[slot, 1])
        low_z = keep(has_lower["gz"], czr[slot, 0])
        high_z = keep(has_upper["gz"], czr[slot, 1])
        left = keep(has_lower["gx"], cxr[slot, 0])
        right = keep(has_upper["gx"], cxr[slot, 1])
        odd = lax.rem(lax.broadcasted_iota(jnp.int32, (16, LANES), 0), 2) == 1
        both = jnp.where(odd, pltpu.roll(left, 1, 0), pltpu.roll(right, 15, 0))
        side = jnp.transpose(jnp.concatenate([both, jnp.zeros((LANES - 16, LANES), F32)], axis=0))
        side = jnp.concatenate(
            [pltpu.roll(side, LANES - 1 - 2 * i, 1) for i in range(8)], axis=0
        ).reshape(BRICK, BRICK, LANES)
        return low_y, high_y, low_z, high_z, side

    def shifts(values, halo):
        low_y, high_y, low_z, high_z, side = halo
        lane = lax.broadcasted_iota(jnp.int32, values.shape, 2)
        yield jnp.concatenate([low_z[None], values[:-1]], axis=0)
        yield jnp.concatenate([values[1:], high_z[None]], axis=0)
        yield jnp.concatenate([low_y[:, None, :], values[:, :-1]], axis=1)
        yield jnp.concatenate([values[:, 1:], high_y[:, None, :]], axis=1)
        yield jnp.where(lane == 0, side, pltpu.roll(values, 1, 2))
        yield jnp.where(lane == LANES - 1, side, pltpu.roll(values, LANES - 1, 2))

    def a_start(s, c):
        slot = s * 3 + c
        values = w[slot, 0:OWNED, :].reshape(BRICK, LENGTH, LANES)
        ys[slot, 0] = values[:, 0:MARGIN, :]
        ys[slot, 1] = values[:, BRICK - MARGIN:BRICK, :]
        send(slot, AY, (ys.at[slot, 0], yr.at[slot, 1]), (ys.at[slot, 1], yr.at[slot, 0]))

    def a_z(s, c):
        slot = s * 3 + c
        arrive(slot, AY)
        low = keep(has_lower["gy"], yr[slot, 0])
        high = keep(has_upper["gy"], yr[slot, 1])
        for z in range(BRICK):
            w[slot, z * LENGTH + BRICK:(z + 1) * LENGTH, :] = jnp.concatenate([low[z], high[z]], axis=0)
        first, last = MARGIN * LENGTH, OWNED - MARGIN * LENGTH
        send(
            slot, AZ,
            (w.at[slot, pl.ds(0, first)], w.at[slot, pl.ds(OWNED + first, first)]),
            (w.at[slot, pl.ds(last, first)], w.at[slot, pl.ds(OWNED, first)]),
        )

    def a_x(s, c):
        slot = s * 3 + c
        arrive(slot, AZ)
        part = MARGIN * LENGTH
        low = w[slot, OWNED:OWNED + part, :]
        w[slot, OWNED:OWNED + part, :] = keep(has_lower["gz"], low)
        high = w[slot, OWNED + part:ROWS, :]
        w[slot, OWNED + part:ROWS, :] = keep(has_upper["gz"], high)

        total = jnp.zeros((LANES, LANES), F32)
        for i in range(CHUNKS):
            part = pltpu.roll(w[slot, i * LANES:(i + 1) * LANES, :], 8 * i + MARGIN, 1)
            total = jnp.where((lanes >= 8 * i) & (lanes < 8 * i + 8), part, total)
        total = jnp.transpose(total)[:CHUNKS * 8].reshape(CHUNKS, 8, LANES)
        xs[slot, 0] = total[:, MARGIN:]
        xs[slot, 1] = total[:, :MARGIN]
        send(slot, AX, (xs.at[slot, 0], xr.at[slot, 1]), (xs.at[slot, 1], xr.at[slot, 0]))

    def solve(s, c):
        slot = s * 3 + c
        arrive(slot, AX)

        near = jnp.concatenate([keep(has_lower["gx"], xr[slot, 0]), keep(has_upper["gx"], xr[slot, 1])], axis=1)
        high = near.astype(BF16).astype(F32)
        near = jnp.concatenate([high, near - high, high], axis=1)
        sides = []
        for first in range(0, CHUNKS, 5):
            rows = near[first:first + 5].reshape(-1, LANES)
            blank = jnp.zeros((LANES - rows.shape[0], LANES), F32)
            sides.append(jnp.transpose(jnp.concatenate([rows, blank], axis=0)))
        for i in range(CHUNKS):
            at = pl.ds(i * LANES, LANES)
            side = sides[i // 5]
            if i % 5:
                side = pltpu.roll(side, LANES - 24 * (i % 5), 1)
            high, low = halves(w[slot, at, :])
            out = dot(jnp.concatenate([high, low], axis=1), into_1[...])
            out += dot(jnp.concatenate([high, side.astype(BF16)], axis=1), into_2[...])
            b1a[at, :] = out[:, :LANES]
            b1b[at, :] = out[:, LANES:]

        def transform(matrix, source, target, strided, scale=None):
            def body(i, carry):
                outs = []
                for k in range(UNROLL):
                    at = pl.ds(pl.multiple_of((i * UNROLL + k) * 2 * LENGTH, 8), 2 * LENGTH)
                    values = jnp.concatenate([source[0][at, :], source[1][at, :]], axis=1)
                    outs.append(dot(matrix[...], triple(values)))
                for k in range(UNROLL):
                    at = pl.ds(pl.multiple_of((i * UNROLL + k) * 2 * LENGTH, 8), 2 * LENGTH)
                    out = outs[k]
                    if scale is not None:
                        out = out * scale[c, at, :]
                    for half in range(2):
                        part = out[:, half * LANES:(half + 1) * LANES]
                        if strided:
                            for which in range(2):
                                spot = pl.ds((i * UNROLL + k) * 2 + which, LENGTH, stride=LENGTH)
                                target[half][spot, :] = part[which * LENGTH:(which + 1) * LENGTH]
                        else:
                            target[half][at, :] = part
                return carry

            lax.fori_loop(0, LENGTH // 2 // UNROLL, body, 0)

        one, two = (b1a, b1b), (b2a, b2b)
        transform(fwd, one, two, True)
        transform(fwd, two, one, False, rinv)
        transform(bwd, one, two, True)
        transform(bwd, two, one, False)

        margin = jnp.zeros((LANES, LANES), F32)
        for i in range(CHUNKS):
            at = pl.ds(i * LANES, LANES)
            high, low = halves(b1a[at, :])
            tail = b1b[at, :]
            tail_high = tail.astype(BF16).astype(F32)
            packed = tail_high + pltpu.roll(tail - tail_high, 32, 1) + pltpu.roll(tail_high, 64, 1)
            out = dot(jnp.concatenate([high, low], axis=1), out_1[...])
            out += dot(jnp.concatenate([high, packed.astype(BF16)], axis=1), out_2[...])
            zb[slot, at, :] = out[:, :LANES]
            part = out[:, LANES:]
            margin += pltpu.roll(part, 8 * i, 1) if i else part
        margin = jnp.transpose(margin)[:CHUNKS * 8].reshape(CHUNKS, 8, LANES)
        fs[slot, 0] = margin[:, :MARGIN]
        fs[slot, 1] = margin[:, MARGIN:]
        send(slot, BX, (fs.at[slot, 0], fr.at[slot, 1]), (fs.at[slot, 1], fr.at[slot, 0]))

    def b_z(s, c):
        slot = s * 3 + c
        arrive(slot, BX)

        near = jnp.concatenate([keep(has_upper["gx"], fr[slot, 1]), keep(has_lower["gx"], fr[slot, 0])], axis=1)
        blank = jnp.zeros((LANES - CHUNKS * 8, LANES), F32)
        side = jnp.transpose(jnp.concatenate([near.reshape(CHUNKS * 8, LANES), blank], axis=0))
        edge = (lanes < MARGIN) | (lanes >= LANES - MARGIN)
        for i in range(CHUNKS):
            at = pl.ds(i * LANES, LANES)
            zb[slot, at, :] += jnp.where(edge, pltpu.roll(side, LANES - 8 * i - MARGIN, 1), 0.0)

        part = MARGIN * LENGTH
        send(
            slot, BZ,
            (zb.at[slot, pl.ds(OWNED, part)], zr.at[slot, 1]),
            (zb.at[slot, pl.ds(OWNED + part, part)], zr.at[slot, 0]),
        )

    def b_y(s, c):
        slot = s * 3 + c
        arrive(slot, BZ)
        part = MARGIN * LENGTH
        zb[slot, 0:part, :] += keep(has_lower["gz"], zr[slot, 0])
        zb[slot, OWNED - part:OWNED, :] += keep(has_upper["gz"], zr[slot, 1])
        other = slot + 6
        for z in range(BRICK):
            rows = zb[slot, z * LENGTH + BRICK:(z + 1) * LENGTH, :]
            ys[other, 0, z] = rows[:MARGIN]
            ys[other, 1, z] = rows[MARGIN:]
        send(slot, BY, (ys.at[other, 0], yr.at[other, 1]), (ys.at[other, 1], yr.at[other, 0]))

    def c_start(s, c):
        slot = s * 3 + c
        arrive(slot, BY)
        other = slot + 6
        low = keep(has_lower["gy"], yr[other, 0])
        high = keep(has_upper["gy"], yr[other, 1])
        own = zb[slot, 0:OWNED, :].reshape(BRICK, LENGTH, LANES)[:, :BRICK]
        blank = jnp.zeros((BRICK, MARGIN, LANES), F32)
        own = jnp.concatenate([
            own[:, :8] + jnp.concatenate([low, blank], axis=1),
            own[:, 8:24],
            own[:, 24:] + jnp.concatenate([blank, high], axis=1),
        ], axis=1)
        corr[slot] = own
        halo_send(slot, own)
        if s == 0:
            disp[c] = own
        else:
            disp[c] += own

    def update(s, c):
        slot = s * 3 + c
        halo = halo_get(slot)
        values = corr[slot]
        total = SIGMA_SHIFT * modulus[...] * values
        for number, moved in enumerate(shifts(values, halo)):
            total = total + (ratio(c, number // 2) * 0.5) * faces[number] * (values - moved)
        if s == 0:
            old = load[c]
        else:
            old = w[slot, 0:OWNED, :].reshape(BRICK, LENGTH, LANES)[:, :BRICK]
        new = old - total
        if s == SWEEPS - 1:
            resid[c] = new
        else:
            for z in range(BRICK):
                w[slot + 3, z * LENGTH:z * LENGTH + BRICK, :] = new[z]

    for c in range(3):
        for z in range(BRICK):
            w[c, z * LENGTH:z * LENGTH + BRICK, :] = load[c, z]
    for slot in range(6):
        w[slot, ROWS:, :] = jnp.zeros((PADDED - ROWS, LANES), F32)
    for c in range(3):
        a_start(0, c)

    def look(z, carry):
        picked = labels[z]
        value = jnp.zeros(picked.shape, F32)
        for number in range(table.shape[0]):
            value = jnp.where(picked == number, table[number], value)
        modulus[z] = jnp.where(mask[z] == 1, value, VOID_MODULUS)
        return carry

    lax.fori_loop(0, BRICK, look, 0)
    halo_send(6, modulus[...])

    for c in range(3):
        def invert(y, carry, c=c):
            at = pl.ds(pl.multiple_of(y * LENGTH, 8), LENGTH)
            rinv[c, at, :] = 1.0 / (REF_MODULUS * (
                ratio(c, 0) * eigen_rows[...]
                + ratio(c, 1) * eigen_rows[pl.ds(y, 1), :]
                + ratio(c, 2) * eigen_x[...]
                + SIGMA_SHIFT
            ))
            return carry

        lax.fori_loop(0, LENGTH, invert, 0)

    own = modulus[...]
    for number, moved in enumerate(shifts(own, halo_get(6))):
        faces[number] = own + moved

    for s in range(SWEEPS):
        for stage in (a_z, a_x, solve, b_z, b_y, c_start, update):
            for c in range(3):
                stage(s, c)
                if stage is update and s < SWEEPS - 1:
                    a_start(s + 1, c)

    for made in pending.values():
        for copy in made:
            copy.wait_send()


def local(load, labels, mask, table):
    tables = constants()
    vmem = pl.BlockSpec(memory_space=pltpu.VMEM)
    smem = pl.BlockSpec(memory_space=pltpu.SMEM)
    slots = 3 * SWEEPS
    field = jax.ShapeDtypeStruct(load.shape, F32)
    block = (BRICK, BRICK, LANES)
    return pl.pallas_call(
        kernel,
        out_shape=(field, field),
        in_specs=[vmem, vmem, vmem, smem] + [vmem] * len(tables),
        out_specs=(vmem, vmem),
        scratch_shapes=[
            pltpu.VMEM(block, F32),
            pltpu.VMEM((6,) + block, F32),
            pltpu.VMEM((slots, PADDED, LANES), F32),
            pltpu.VMEM((slots, 2, CHUNKS, MARGIN, LANES), F32),
            pltpu.VMEM((slots, 2, CHUNKS, MARGIN, LANES), F32),
            pltpu.VMEM((PADDED, LANES), F32),
            pltpu.VMEM((PADDED, LANES), F32),
            pltpu.VMEM((PADDED, LANES), F32),
            pltpu.VMEM((PADDED, LANES), F32),
            pltpu.VMEM((slots, PADDED, LANES), F32),
            pltpu.VMEM((slots, 2, CHUNKS, MARGIN, LANES), F32),
            pltpu.VMEM((slots, 2, CHUNKS, MARGIN, LANES), F32),
            pltpu.VMEM((slots, 2, MARGIN * LENGTH, LANES), F32),
            pltpu.VMEM((2 * slots, 2, BRICK, MARGIN, LANES), F32),
            pltpu.VMEM((2 * slots, 2, BRICK, MARGIN, LANES), F32),
            pltpu.VMEM((slots,) + block, F32),
            pltpu.VMEM((3, ROWS, WIDE), F32),
            pltpu.VMEM((slots + 1, 2, BRICK, LANES), F32),
            pltpu.VMEM((slots + 1, 2, BRICK, LANES), F32),
            pltpu.VMEM((slots + 1, 2, BRICK, LANES), F32),
            pltpu.VMEM((slots + 1, 2, BRICK, LANES), F32),
            pltpu.VMEM((slots + 1, 16, LANES), F32),
            pltpu.VMEM((slots + 1, 2, 16, LANES), F32),
            pltpu.SemaphoreType.DMA(((slots + 1) * PHASES * 2,)),
            pltpu.SemaphoreType.DMA(((slots + 1) * PHASES * 2,)),
        ],
        compiler_params=pltpu.CompilerParams(
            collective_id=0, has_side_effects=True, vmem_limit_bytes=62 * 1024 * 1024
        ),
    )(load, labels, mask, table, *tables)


def solution(mesh):
    placed = (P(None, "gz", "gy", "gx"), P("gz", "gy", "gx"), P("gz", "gy", "gx"), P())
    return jax.shard_map(
        local,
        mesh=mesh,
        in_specs=placed,
        out_specs=(P(None, "gz", "gy", "gx"), P(None, "gz", "gy", "gx")),
        check_vma=False,
    )
```

```python
import jax
import jax.numpy as jnp
import numpy as np
from jax import lax
from jax.experimental import pallas as pl
from jax.experimental.pallas import tpu as pltpu
from jax.sharding import PartitionSpec as P

BRICK = 32
MARGIN = 4
SWEEPS = 2
LENGTH = BRICK + 2 * MARGIN
LANES = 128
WIDE = 256
ROWS = LENGTH * LENGTH
PADDED = 1664
CHUNKS = PADDED // LANES
OWNED = BRICK * LENGTH
LAMBDA_RATIO = 2.0
SIGMA_SHIFT = 0.1
REF_MODULUS = 1.5
VOID_MODULUS = 0.1
MESH = pl.DeviceIdType.MESH
UNROLL = 5
PHASES = 9
AY, AZ, AX, BX, BZ, BY, CY, CZ, CX = range(PHASES)
AXIS = {AY: "gy", AZ: "gz", AX: "gx", BX: "gx", BZ: "gz", BY: "gy", CY: "gy", CZ: "gz", CX: "gx"}
ORDER = (
    (0, 0, "a_z"), (0, 1, "a_z"), (0, 0, "a_x"), (0, 2, "a_z"), (0, 0, "s1"), (0, 1, "a_x"), (0, 0, "s2"),
    (0, 2, "a_x"), (0, 0, "s3"), (0, 1, "s1"), (0, 0, "b_z"), (0, 1, "s2"), (0, 1, "s3"), (0, 0, "b_y"),
    (0, 2, "s1"), (0, 1, "b_z"), (0, 2, "s2"), (0, 2, "s3"), (0, 0, "c_start"), (0, 1, "b_y"), (0, 2, "b_z"),
    (0, 0, "update"), (0, 1, "c_start"), (0, 2, "b_y"), (0, 1, "update"), (1, 0, "a_z"), (0, 2, "c_start"),
    (1, 0, "a_x"), (1, 1, "a_z"), (0, 2, "update"), (1, 0, "s1"), (1, 1, "a_x"), (1, 0, "s2"), (1, 0, "s3"),
    (1, 2, "a_z"), (1, 1, "s1"), (1, 0, "b_z"), (1, 1, "s2"), (1, 2, "a_x"), (1, 1, "s3"), (1, 0, "b_y"),
    (1, 2, "s1"), (1, 1, "b_z"), (1, 2, "s2"), (1, 2, "s3"), (1, 0, "c_start"), (1, 1, "b_y"), (1, 2, "b_z"),
    (1, 0, "update"), (1, 2, "b_y"), (1, 1, "c_start"), (1, 2, "c_start"), (1, 1, "update"), (1, 2, "update"),
)
F32 = jnp.float32
BF16 = jnp.bfloat16


def ratio(component, direction):
    return LAMBDA_RATIO if component == direction else 1.0


def halves(values):
    high = values.astype(BF16)
    return high, (values - high.astype(F32)).astype(BF16)


def constants():
    grid = np.arange(1, LENGTH + 1, dtype=np.float64)
    sine = np.sqrt(2.0 / (LENGTH + 1)) * np.sin(np.pi * grid[:, None] * grid[None, :] / (LENGTH + 1))
    eigen = 2.0 - 2.0 * np.cos(np.pi * grid / (LENGTH + 1))
    spot = np.arange(LENGTH, dtype=np.float64)
    ramp = np.minimum(np.minimum((spot + 0.5) / (2 * MARGIN), (LENGTH - 0.5 - spot) / (2 * MARGIN)), 1.0)
    ramped = ramp[:, None] * sine
    place = np.concatenate([np.arange(MARGIN, MARGIN + BRICK), np.arange(MARGIN), np.arange(MARGIN + BRICK, LENGTH)])
    forward = ramped[place].T
    backward = sine.T[place]
    count = LANES // BRICK
    wide_x = LANES + 2 * MARGIN
    forward_x = np.zeros((wide_x, WIDE))
    backward_x = np.zeros((WIDE, wide_x))
    for brick in range(count):
        rows = slice(brick * BRICK, brick * BRICK + LENGTH)
        columns = slice(brick * LENGTH, (brick + 1) * LENGTH)
        forward_x[rows, columns] = ramped
        backward_x[columns, rows] = sine
    edge = slice(LANES, LANES + 2 * MARGIN)
    into = forward_x[MARGIN:MARGIN + LANES]
    into_edge = np.concatenate([forward_x[:MARGIN], forward_x[MARGIN + LANES:]])
    out = np.zeros((WIDE, WIDE))
    out[:, :LANES] = backward_x[:, MARGIN:MARGIN + LANES]
    out[:, edge] = np.concatenate([backward_x[:, :MARGIN], backward_x[:, MARGIN + LANES:]], axis=1)
    rest = count * LENGTH - LANES
    eigen_x = np.zeros((1, WIDE))
    eigen_x[0, : count * LENGTH] = np.tile(eigen, count)
    eigen_lanes = np.broadcast_to(eigen[:, None], (LENGTH, WIDE))

    def high(matrix):
        return matrix.astype(np.float32).astype(BF16).astype(np.float64)

    def low(matrix):
        return matrix - high(matrix)

    def pair(matrix):
        zero = np.zeros((LENGTH, LENGTH))
        both = np.block([[matrix, zero], [zero, matrix]])
        return np.concatenate([high(both), high(both), low(both)], axis=1)

    def tall(*parts):
        blank = np.zeros((2 * LANES - sum(p.shape[0] for p in parts), WIDE))
        return np.concatenate(parts + (blank,))

    head, tail = out[:LANES], out[LANES:LANES + rest]
    return [m.astype(BF16) for m in (
        pair(forward),
        pair(backward),
        tall(high(into), high(into)),
        tall(low(into), high(into_edge), high(into_edge), low(into_edge)),
        tall(high(head), high(head)),
        tall(low(head), high(tail), high(tail), low(tail)),
    )] + [eigen_x.astype(np.float32), np.ascontiguousarray(eigen_lanes).astype(np.float32)]


def dot(a, b):
    return jnp.dot(a, b, preferred_element_type=F32)


def triple(values):
    high, low = halves(values)
    return jnp.concatenate([high, low, high], axis=0)


def kernel(
    load, labels, mask, table,
    fwd, bwd, into_1, into_2, out_1, out_2, eigen_x, eigen_rows,
    disp, resid,
    modulus, faces, w, xs, xr, b1a, b1b, b2a, b2b, zb, fs, fr, zr, ys, yr, corr, rinv,
    cys, cyr, czs, czr, cxs, cxr,
    send_sem, recv_sem,
):
    index = {a: lax.axis_index(a) for a in ("gx", "gy", "gz")}
    count = {a: lax.axis_size(a) for a in ("gx", "gy", "gz")}
    lower = {a: lax.rem(index[a] + count[a] - 1, count[a]) for a in index}
    upper = {a: lax.rem(index[a] + 1, count[a]) for a in index}
    has_lower = {a: index[a] > 0 for a in index}
    has_upper = {a: index[a] < count[a] - 1 for a in index}

    barrier = pltpu.get_barrier_semaphore()
    for a in ("gx", "gy", "gz"):
        pl.semaphore_signal(barrier, inc=1, device_id={a: lower[a]}, device_id_type=MESH)
        pl.semaphore_signal(barrier, inc=1, device_id={a: upper[a]}, device_id_type=MESH)
    pl.semaphore_wait(barrier, 6)

    def copies(slot, phase, down, up):
        a = AXIS[phase]
        made = []
        for side, (source, target), device in ((0, down, lower[a]), (1, up, upper[a])):
            number = (slot * PHASES + phase) * 2 + side
            made.append(pltpu.make_async_remote_copy(
                src_ref=source, dst_ref=target,
                send_sem=send_sem.at[number], recv_sem=recv_sem.at[number],
                device_id={a: device}, device_id_type=MESH,
            ))
        return made

    pending = {}

    def send(slot, phase, down, up):
        made = copies(slot, phase, down, up)
        for copy in made:
            copy.start()
        pending[slot, phase] = made

    def arrive(slot, phase):
        for copy in pending[slot, phase]:
            copy.wait_recv()

    def keep(flag, values):
        return jnp.where(flag, values, 0.0)

    lanes = lax.broadcasted_iota(jnp.int32, (LANES, LANES), 1)

    def face_columns(values):
        flat = values.reshape(BRICK * BRICK, LANES)
        total = jnp.zeros((LANES, LANES), F32)
        for i in range(8):
            part = pltpu.roll(flat[i * LANES:(i + 1) * LANES], 2 * i + 1, 1)
            total = jnp.where((lanes == 2 * i) | (lanes == 2 * i + 1), part, total)
        return jnp.transpose(total)[:16]

    def halo_send(slot, values):
        cys[slot, 0] = values[:, 0, :]
        cys[slot, 1] = values[:, BRICK - 1, :]
        czs[slot, 0] = values[0]
        czs[slot, 1] = values[BRICK - 1]
        cxs[slot] = face_columns(values)
        send(slot, CY, (cys.at[slot, 0], cyr.at[slot, 1]), (cys.at[slot, 1], cyr.at[slot, 0]))
        send(slot, CZ, (czs.at[slot, 0], czr.at[slot, 1]), (czs.at[slot, 1], czr.at[slot, 0]))
        send(slot, CX, (cxs.at[slot], cxr.at[slot, 1]), (cxs.at[slot], cxr.at[slot, 0]))

    def halo_get(slot):
        for phase in (CY, CZ, CX):
            arrive(slot, phase)
        low_y = keep(has_lower["gy"], cyr[slot, 0])
        high_y = keep(has_upper["gy"], cyr[slot, 1])
        low_z = keep(has_lower["gz"], czr[slot, 0])
        high_z = keep(has_upper["gz"], czr[slot, 1])
        left = keep(has_lower["gx"], cxr[slot, 0])
        right = keep(has_upper["gx"], cxr[slot, 1])
        odd = lax.rem(lax.broadcasted_iota(jnp.int32, (16, LANES), 0), 2) == 1
        both = jnp.where(odd, pltpu.roll(left, 1, 0), pltpu.roll(right, 15, 0))
        side = jnp.transpose(jnp.concatenate([both, jnp.zeros((LANES - 16, LANES), F32)], axis=0))
        side = jnp.concatenate(
            [pltpu.roll(side, LANES - 1 - 2 * i, 1) for i in range(8)], axis=0
        ).reshape(BRICK, BRICK, LANES)
        return low_y, high_y, low_z, high_z, side

    def shifts(values, halo):
        low_y, high_y, low_z, high_z, side = halo
        lane = lax.broadcasted_iota(jnp.int32, values.shape, 2)
        yield jnp.concatenate([low_z[None], values[:-1]], axis=0)
        yield jnp.concatenate([values[1:], high_z[None]], axis=0)
        yield jnp.concatenate([low_y[:, None, :], values[:, :-1]], axis=1)
        yield jnp.concatenate([values[:, 1:], high_y[:, None, :]], axis=1)
        yield jnp.where(lane == 0, side, pltpu.roll(values, 1, 2))
        yield jnp.where(lane == LANES - 1, side, pltpu.roll(values, LANES - 1, 2))

    def a_start(s, c):
        slot = s * 3 + c
        if s == 0:
            values = load[c]
        else:
            values = w[slot, 0:OWNED, :].reshape(BRICK, LENGTH, LANES)
        ys[slot, 0] = values[:, 0:MARGIN, :]
        ys[slot, 1] = values[:, BRICK - MARGIN:BRICK, :]
        send(slot, AY, (ys.at[slot, 0], yr.at[slot, 1]), (ys.at[slot, 1], yr.at[slot, 0]))

    def a_z(s, c):
        slot = s * 3 + c
        arrive(slot, AY)
        low = keep(has_lower["gy"], yr[slot, 0])
        high = keep(has_upper["gy"], yr[slot, 1])
        for z in range(BRICK):
            w[slot, z * LENGTH + BRICK:(z + 1) * LENGTH, :] = jnp.concatenate([low[z], high[z]], axis=0)
        first, last = MARGIN * LENGTH, OWNED - MARGIN * LENGTH
        send(
            slot, AZ,
            (w.at[slot, pl.ds(0, first)], w.at[slot, pl.ds(OWNED + first, first)]),
            (w.at[slot, pl.ds(last, first)], w.at[slot, pl.ds(OWNED, first)]),
        )

    def a_x(s, c):
        slot = s * 3 + c
        arrive(slot, AZ)
        part = MARGIN * LENGTH
        low = w[slot, OWNED:OWNED + part, :]
        w[slot, OWNED:OWNED + part, :] = keep(has_lower["gz"], low)
        high = w[slot, OWNED + part:ROWS, :]
        w[slot, OWNED + part:ROWS, :] = keep(has_upper["gz"], high)

        total = jnp.zeros((LANES, LANES), F32)
        for i in range(CHUNKS):
            part = pltpu.roll(w[slot, i * LANES:(i + 1) * LANES, :], 8 * i + MARGIN, 1)
            total = jnp.where((lanes >= 8 * i) & (lanes < 8 * i + 8), part, total)
        total = jnp.transpose(total)[:CHUNKS * 8].reshape(CHUNKS, 8, LANES)
        xs[slot, 0] = total[:, MARGIN:]
        xs[slot, 1] = total[:, :MARGIN]
        send(slot, AX, (xs.at[slot, 0], xr.at[slot, 1]), (xs.at[slot, 1], xr.at[slot, 0]))

    one, two = (b1a, b1b), (b2a, b2b)

    def transform(matrix, source, target, strided, scale=None):
        def body(i, carry):
            outs = []
            for k in range(UNROLL):
                at = pl.ds(pl.multiple_of((i * UNROLL + k) * 2 * LENGTH, 8), 2 * LENGTH)
                values = jnp.concatenate([source[0][at, :], source[1][at, :]], axis=1)
                outs.append(dot(matrix[...], triple(values)))
            for k in range(UNROLL):
                at = pl.ds(pl.multiple_of((i * UNROLL + k) * 2 * LENGTH, 8), 2 * LENGTH)
                out = outs[k]
                if scale is not None:
                    out = out * scale[at, :]
                for half in range(2):
                    part = out[:, half * LANES:(half + 1) * LANES]
                    if strided:
                        for which in range(2):
                            spot = pl.ds((i * UNROLL + k) * 2 + which, LENGTH, stride=LENGTH)
                            target[half][spot, :] = part[which * LENGTH:(which + 1) * LENGTH]
                    else:
                        target[half][at, :] = part
            return carry

        lax.fori_loop(0, LENGTH // 2 // UNROLL, body, 0)

    def s1(s, c):
        slot = s * 3 + c
        arrive(slot, AX)

        near = jnp.concatenate([keep(has_lower["gx"], xr[slot, 0]), keep(has_upper["gx"], xr[slot, 1])], axis=1)
        high = near.astype(BF16).astype(F32)
        near = jnp.concatenate([high, near - high, high], axis=1)
        sides = []
        for first in range(0, CHUNKS, 5):
            rows = near[first:first + 5].reshape(-1, LANES)
            blank = jnp.zeros((LANES - rows.shape[0], LANES), F32)
            sides.append(jnp.transpose(jnp.concatenate([rows, blank], axis=0)))
        for i in range(CHUNKS):
            at = pl.ds(i * LANES, LANES)
            side = sides[i // 5]
            if i % 5:
                side = pltpu.roll(side, LANES - 24 * (i % 5), 1)
            high, low = halves(w[slot, at, :])
            out = dot(jnp.concatenate([high, low], axis=1), into_1[...])
            out += dot(jnp.concatenate([high, side.astype(BF16)], axis=1), into_2[...])
            b1a[at, :] = out[:, :LANES]
            b1b[at, :] = out[:, LANES:]

        transform(fwd, one, two, True)

    def s2(s, c):
        transform(fwd, two, one, False, rinv.at[c])
        transform(bwd, one, two, True)

    def s3(s, c):
        slot = s * 3 + c
        transform(bwd, two, one, False)

        margin = jnp.zeros((LANES, LANES), F32)
        for i in range(CHUNKS):
            at = pl.ds(i * LANES, LANES)
            high, low = halves(b1a[at, :])
            tail = b1b[at, :]
            tail_high = tail.astype(BF16).astype(F32)
            packed = tail_high + pltpu.roll(tail - tail_high, 32, 1) + pltpu.roll(tail_high, 64, 1)
            out = dot(jnp.concatenate([high, low], axis=1), out_1[...])
            out += dot(jnp.concatenate([high, packed.astype(BF16)], axis=1), out_2[...])
            zb[slot, at, :] = out[:, :LANES]
            part = out[:, LANES:]
            margin += pltpu.roll(part, 8 * i, 1) if i else part
        margin = jnp.transpose(margin)[:CHUNKS * 8].reshape(CHUNKS, 8, LANES)
        fs[slot, 0] = margin[:, :MARGIN]
        fs[slot, 1] = margin[:, MARGIN:]
        send(slot, BX, (fs.at[slot, 0], fr.at[slot, 1]), (fs.at[slot, 1], fr.at[slot, 0]))

    def b_z(s, c):
        slot = s * 3 + c
        arrive(slot, BX)

        near = jnp.concatenate([keep(has_upper["gx"], fr[slot, 1]), keep(has_lower["gx"], fr[slot, 0])], axis=1)
        blank = jnp.zeros((LANES - CHUNKS * 8, LANES), F32)
        side = jnp.transpose(jnp.concatenate([near.reshape(CHUNKS * 8, LANES), blank], axis=0))
        edge = (lanes < MARGIN) | (lanes >= LANES - MARGIN)
        for i in range(CHUNKS):
            at = pl.ds(i * LANES, LANES)
            zb[slot, at, :] += jnp.where(edge, pltpu.roll(side, LANES - 8 * i - MARGIN, 1), 0.0)

        part = MARGIN * LENGTH
        send(
            slot, BZ,
            (zb.at[slot, pl.ds(OWNED, part)], zr.at[slot, 1]),
            (zb.at[slot, pl.ds(OWNED + part, part)], zr.at[slot, 0]),
        )

    def b_y(s, c):
        slot = s * 3 + c
        arrive(slot, BZ)
        part = MARGIN * LENGTH
        zb[slot, 0:part, :] += keep(has_lower["gz"], zr[slot, 0])
        zb[slot, OWNED - part:OWNED, :] += keep(has_upper["gz"], zr[slot, 1])
        other = slot + 6
        for z in range(BRICK):
            rows = zb[slot, z * LENGTH + BRICK:(z + 1) * LENGTH, :]
            ys[other, 0, z] = rows[:MARGIN]
            ys[other, 1, z] = rows[MARGIN:]
        send(slot, BY, (ys.at[other, 0], yr.at[other, 1]), (ys.at[other, 1], yr.at[other, 0]))

    def c_start(s, c):
        slot = s * 3 + c
        arrive(slot, BY)
        other = slot + 6
        low = keep(has_lower["gy"], yr[other, 0])
        high = keep(has_upper["gy"], yr[other, 1])
        own = zb[slot, 0:OWNED, :].reshape(BRICK, LENGTH, LANES)[:, :BRICK]
        blank = jnp.zeros((BRICK, MARGIN, LANES), F32)
        own = jnp.concatenate([
            own[:, :8] + jnp.concatenate([low, blank], axis=1),
            own[:, 8:24],
            own[:, 24:] + jnp.concatenate([blank, high], axis=1),
        ], axis=1)
        corr[slot] = own
        halo_send(slot, own)
        if s == 0:
            disp[c] = own
        else:
            disp[c] += own

    def update(s, c):
        slot = s * 3 + c
        halo = halo_get(slot)
        values = corr[slot]
        total = SIGMA_SHIFT * modulus[...] * values
        for number, moved in enumerate(shifts(values, halo)):
            total = total + (ratio(c, number // 2) * 0.5) * faces[number] * (values - moved)
        if s == 0:
            old = load[c]
        else:
            old = w[slot, 0:OWNED, :].reshape(BRICK, LENGTH, LANES)[:, :BRICK]
        new = old - total
        if s == SWEEPS - 1:
            resid[c] = new
        else:
            for z in range(BRICK):
                w[slot + 3, z * LENGTH:z * LENGTH + BRICK, :] = new[z]

    for c in range(3):
        a_start(0, c)
    for c in range(3):
        for z in range(BRICK):
            w[c, z * LENGTH:z * LENGTH + BRICK, :] = load[c, z]
    for slot in range(6):
        w[slot, ROWS:, :] = jnp.zeros((PADDED - ROWS, LANES), F32)

    def look(z, carry):
        picked = labels[z]
        value = jnp.zeros(picked.shape, F32)
        for number in range(table.shape[0]):
            value = jnp.where(picked == number, table[number], value)
        modulus[z] = jnp.where(mask[z] == 1, value, VOID_MODULUS)
        return carry

    lax.fori_loop(0, BRICK, look, 0)
    halo_send(6, modulus[...])

    for c in range(3):
        def invert(y, carry, c=c):
            at = pl.ds(pl.multiple_of(y * LENGTH, 8), LENGTH)
            rinv[c, at, :] = 1.0 / (REF_MODULUS * (
                ratio(c, 0) * eigen_rows[...]
                + ratio(c, 1) * eigen_rows[pl.ds(y, 1), :]
                + ratio(c, 2) * eigen_x[...]
                + SIGMA_SHIFT
            ))
            return carry

        lax.fori_loop(0, LENGTH, invert, 0)

    own = modulus[...]
    for number, moved in enumerate(shifts(own, halo_get(6))):
        faces[number] = own + moved

    stages = dict(a_z=a_z, a_x=a_x, s1=s1, s2=s2, s3=s3, b_z=b_z, b_y=b_y, c_start=c_start, update=update)
    for s, c, name in ORDER:
        stages[name](s, c)
        if name == "update" and s < SWEEPS - 1:
            a_start(s + 1, c)

    for made in pending.values():
        for copy in made:
            copy.wait_send()


def local(load, labels, mask, table):
    tables = constants()
    vmem = pl.BlockSpec(memory_space=pltpu.VMEM)
    smem = pl.BlockSpec(memory_space=pltpu.SMEM)
    slots = 3 * SWEEPS
    field = jax.ShapeDtypeStruct(load.shape, F32)
    block = (BRICK, BRICK, LANES)
    return pl.pallas_call(
        kernel,
        out_shape=(field, field),
        in_specs=[vmem, vmem, vmem, smem] + [vmem] * len(tables),
        out_specs=(vmem, vmem),
        scratch_shapes=[
            pltpu.VMEM(block, F32),
            pltpu.VMEM((6,) + block, F32),
            pltpu.VMEM((slots, PADDED, LANES), F32),
            pltpu.VMEM((slots, 2, CHUNKS, MARGIN, LANES), F32),
            pltpu.VMEM((slots, 2, CHUNKS, MARGIN, LANES), F32),
            pltpu.VMEM((PADDED, LANES), F32),
            pltpu.VMEM((PADDED, LANES), F32),
            pltpu.VMEM((PADDED, LANES), F32),
            pltpu.VMEM((PADDED, LANES), F32),
            pltpu.VMEM((slots, PADDED, LANES), F32),
            pltpu.VMEM((slots, 2, CHUNKS, MARGIN, LANES), F32),
            pltpu.VMEM((slots, 2, CHUNKS, MARGIN, LANES), F32),
            pltpu.VMEM((slots, 2, MARGIN * LENGTH, LANES), F32),
            pltpu.VMEM((2 * slots, 2, BRICK, MARGIN, LANES), F32),
            pltpu.VMEM((2 * slots, 2, BRICK, MARGIN, LANES), F32),
            pltpu.VMEM((slots,) + block, F32),
            pltpu.VMEM((3, ROWS, WIDE), F32),
            pltpu.VMEM((slots + 1, 2, BRICK, LANES), F32),
            pltpu.VMEM((slots + 1, 2, BRICK, LANES), F32),
            pltpu.VMEM((slots + 1, 2, BRICK, LANES), F32),
            pltpu.VMEM((slots + 1, 2, BRICK, LANES), F32),
            pltpu.VMEM((slots + 1, 16, LANES), F32),
            pltpu.VMEM((slots + 1, 2, 16, LANES), F32),
            pltpu.SemaphoreType.DMA(((slots + 1) * PHASES * 2,)),
            pltpu.SemaphoreType.DMA(((slots + 1) * PHASES * 2,)),
        ],
        compiler_params=pltpu.CompilerParams(
            collective_id=0, has_side_effects=True, vmem_limit_bytes=62 * 1024 * 1024
        ),
    )(load, labels, mask, table, *tables)


def solution(mesh):
    placed = (P(None, "gz", "gy", "gx"), P("gz", "gy", "gx"), P("gz", "gy", "gx"), P())
    return jax.shard_map(
        local,
        mesh=mesh,
        in_specs=placed,
        out_specs=(P(None, "gz", "gy", "gx"), P(None, "gz", "gy", "gx")),
        check_vma=False,
    )
```

```python
import jax
import jax.numpy as jnp
import numpy as np
from jax import lax
from jax.experimental import pallas as pl
from jax.experimental.pallas import tpu as pltpu
from jax.sharding import PartitionSpec as P

BRICK = 32
MARGIN = 4
SWEEPS = 2
LENGTH = BRICK + 2 * MARGIN
LANES = 128
WIDE = 256
ROWS = LENGTH * LENGTH
PADDED = 1664
CHUNKS = PADDED // LANES
OWNED = BRICK * LENGTH
LAMBDA_RATIO = 2.0
SIGMA_SHIFT = 0.1
REF_MODULUS = 1.5
VOID_MODULUS = 0.1
MESH = pl.DeviceIdType.MESH
UNROLL = 5
PHASES = 10
AY, AZ, AE, AX, BX, BZ, BY, CY, CZ, CX = range(PHASES)
AXIS = ("gy", "gz", "gz", "gx", "gx", "gz", "gy", "gy", "gz", "gx")
PLANES = 42
ORDER = (
    (0, 0, "a_z"), (0, 1, "a_z"), (0, 0, "a_x"), (0, 1, "a_x"), (0, 0, "s1"), (0, 2, "a_z"), (0, 0, "s2"),
    (0, 0, "s3"), (0, 1, "s1"), (0, 1, "s2"), (0, 0, "stiff"), (0, 0, "b_z"), (0, 1, "s3"), (0, 2, "a_x"),
    (0, 0, "b_y"), (0, 1, "b_z"), (0, 2, "s1"), (0, 2, "s2"), (0, 2, "s3"), (0, 1, "b_y"), (0, 0, "c_start"),
    (0, 2, "b_z"), (0, 0, "update"), (0, 1, "c_start"), (0, 2, "b_y"), (0, 1, "update"), (1, 0, "a_z"),
    (0, 2, "c_start"), (1, 0, "a_x"), (1, 1, "a_z"), (0, 2, "update"), (1, 0, "s1"), (1, 1, "a_x"), (1, 0, "s2"),
    (1, 0, "s3"), (1, 2, "a_z"), (1, 1, "s1"), (1, 1, "s2"), (1, 2, "a_x"), (1, 1, "s3"), (1, 0, "b_z"),
    (1, 2, "s1"), (1, 2, "s2"), (1, 0, "b_y"), (1, 1, "b_z"), (1, 2, "s3"), (1, 1, "b_y"), (1, 2, "b_z"),
    (1, 0, "c_start"), (1, 2, "b_y"), (1, 1, "c_start"), (1, 0, "update"), (1, 1, "update"), (1, 2, "c_start"),
    (1, 2, "update"),
)
F32 = jnp.float32
BF16 = jnp.bfloat16


def ratio(component, direction):
    return LAMBDA_RATIO if component == direction else 1.0


def halves(values):
    high = values.astype(BF16)
    return high, (values - high.astype(F32)).astype(BF16)


def constants():
    grid = np.arange(1, LENGTH + 1, dtype=np.float64)
    sine = np.sqrt(2.0 / (LENGTH + 1)) * np.sin(np.pi * grid[:, None] * grid[None, :] / (LENGTH + 1))
    eigen = 2.0 - 2.0 * np.cos(np.pi * grid / (LENGTH + 1))
    spot = np.arange(LENGTH, dtype=np.float64)
    ramp = np.minimum(np.minimum((spot + 0.5) / (2 * MARGIN), (LENGTH - 0.5 - spot) / (2 * MARGIN)), 1.0)
    ramped = ramp[:, None] * sine
    place = np.concatenate([np.arange(MARGIN, MARGIN + BRICK), np.arange(MARGIN), np.arange(MARGIN + BRICK, LENGTH)])
    forward = ramped[place].T
    backward = sine.T[place]
    count = LANES // BRICK
    wide_x = LANES + 2 * MARGIN
    forward_x = np.zeros((wide_x, WIDE))
    backward_x = np.zeros((WIDE, wide_x))
    for brick in range(count):
        rows = slice(brick * BRICK, brick * BRICK + LENGTH)
        columns = slice(brick * LENGTH, (brick + 1) * LENGTH)
        forward_x[rows, columns] = ramped
        backward_x[columns, rows] = sine
    edge = slice(LANES, LANES + 2 * MARGIN)
    into = forward_x[MARGIN:MARGIN + LANES]
    into_edge = np.concatenate([forward_x[:MARGIN], forward_x[MARGIN + LANES:]])
    out = np.zeros((WIDE, WIDE))
    out[:, :LANES] = backward_x[:, MARGIN:MARGIN + LANES]
    out[:, edge] = np.concatenate([backward_x[:, :MARGIN], backward_x[:, MARGIN + LANES:]], axis=1)
    rest = count * LENGTH - LANES
    eigen_x = np.zeros((1, WIDE))
    eigen_x[0, : count * LENGTH] = np.tile(eigen, count)
    eigen_lanes = np.broadcast_to(eigen[:, None], (LENGTH, WIDE))

    def high(matrix):
        return matrix.astype(np.float32).astype(BF16).astype(np.float64)

    def low(matrix):
        return matrix - high(matrix)

    def pair(matrix):
        zero = np.zeros((LENGTH, LENGTH))
        both = np.block([[matrix, zero], [zero, matrix]])
        return np.concatenate([high(both), high(both), low(both)], axis=1)

    def tall(*parts):
        blank = np.zeros((2 * LANES - sum(p.shape[0] for p in parts), WIDE))
        return np.concatenate(parts + (blank,))

    head, tail = out[:LANES], out[LANES:LANES + rest]
    return [m.astype(BF16) for m in (
        pair(forward),
        pair(backward),
        tall(high(into), high(into)),
        tall(low(into), high(into_edge), high(into_edge), low(into_edge)),
        tall(high(head), high(head)),
        tall(low(head), high(tail), high(tail), low(tail)),
    )] + [eigen_x.astype(np.float32), np.ascontiguousarray(eigen_lanes).astype(np.float32)]


def dot(a, b):
    return jnp.dot(a, b, preferred_element_type=F32)


def triple(values):
    high, low = halves(values)
    return jnp.concatenate([high, low, high], axis=0)


def kernel(
    load, labels, mask, table,
    fwd, bwd, into_1, into_2, out_1, out_2, eigen_x, eigen_rows,
    disp, resid,
    modulus, faces, w, xs, xr, b1a, b1b, b2a, b2b, zb, fs, fr, zr, ys, yr, corr, rinv,
    cys, cyr, czs, czr, cxs, cxr,
    done, send_sem, recv_sem, out_sem,
):
    index = {a: lax.axis_index(a) for a in ("gx", "gy", "gz")}
    count = {a: lax.axis_size(a) for a in ("gx", "gy", "gz")}
    lower = {a: lax.rem(index[a] + count[a] - 1, count[a]) for a in index}
    upper = {a: lax.rem(index[a] + 1, count[a]) for a in index}
    has_lower = {a: index[a] > 0 for a in index}
    has_upper = {a: index[a] < count[a] - 1 for a in index}

    barrier = pltpu.get_barrier_semaphore()
    for a in ("gx", "gy", "gz"):
        pl.semaphore_signal(barrier, inc=1, device_id={a: lower[a]}, device_id_type=MESH)
        pl.semaphore_signal(barrier, inc=1, device_id={a: upper[a]}, device_id_type=MESH)

    def copies(slot, phase, down, up):
        a = AXIS[phase]
        made = []
        for side, (source, target), device in ((0, down, lower[a]), (1, up, upper[a])):
            number = (slot * PHASES + phase) * 2 + side
            made.append(pltpu.make_async_remote_copy(
                src_ref=source, dst_ref=target,
                send_sem=send_sem.at[number], recv_sem=recv_sem.at[number],
                device_id={a: device}, device_id_type=MESH,
            ))
        return made

    pending = {}

    def send(slot, phase, down, up):
        made = copies(slot, phase, down, up)
        for copy in made:
            copy.start()
        pending[slot, phase] = made

    def arrive(slot, phase):
        for copy in pending[slot, phase]:
            copy.wait_recv()

    def flat(ref, slot):
        return ref.at[slot].reshape(PLANES * LENGTH, LANES)

    def keep(flag, values):
        return jnp.where(flag, values, 0.0)

    lanes = lax.broadcasted_iota(jnp.int32, (LANES, LANES), 1)

    def face_columns(values):
        flat = values.reshape(BRICK * BRICK, LANES)
        total = jnp.zeros((LANES, LANES), F32)
        for i in range(8):
            part = pltpu.roll(flat[i * LANES:(i + 1) * LANES], 2 * i + 1, 1)
            total = jnp.where((lanes == 2 * i) | (lanes == 2 * i + 1), part, total)
        return jnp.transpose(total)[:16]

    def y_pack(slot, values):
        cys[slot, 0] = values[:, 0, :]
        cys[slot, 1] = values[:, BRICK - 1, :]

    def y_send(slot):
        send(slot, CY, (cys.at[slot, 0], cyr.at[slot, 1]), (cys.at[slot, 1], cyr.at[slot, 0]))

    def xz_pack(slot, values):
        czs[slot, 0] = values[0]
        czs[slot, 1] = values[BRICK - 1]
        cxs[slot] = face_columns(values)

    def xz_send(slot):
        send(slot, CZ, (czs.at[slot, 0], czr.at[slot, 1]), (czs.at[slot, 1], czr.at[slot, 0]))
        send(slot, CX, (cxs.at[slot], cxr.at[slot, 1]), (cxs.at[slot], cxr.at[slot, 0]))

    def halo_get(slot, low_y, high_y):
        for phase in (CZ, CX):
            arrive(slot, phase)
        low_z = keep(has_lower["gz"], czr[slot, 0])
        high_z = keep(has_upper["gz"], czr[slot, 1])
        left = keep(has_lower["gx"], cxr[slot, 0])
        right = keep(has_upper["gx"], cxr[slot, 1])
        odd = lax.rem(lax.broadcasted_iota(jnp.int32, (16, LANES), 0), 2) == 1
        both = jnp.where(odd, pltpu.roll(left, 1, 0), pltpu.roll(right, 15, 0))
        side = jnp.transpose(jnp.concatenate([both, jnp.zeros((LANES - 16, LANES), F32)], axis=0))
        side = jnp.concatenate(
            [pltpu.roll(side, LANES - 1 - 2 * i, 1) for i in range(8)], axis=0
        ).reshape(BRICK, BRICK, LANES)
        return low_y, high_y, low_z, high_z, side

    def shifts(values, halo):
        low_y, high_y, low_z, high_z, side = halo
        lane = lax.broadcasted_iota(jnp.int32, values.shape, 2)
        yield jnp.concatenate([low_z[None], values[:-1]], axis=0)
        yield jnp.concatenate([values[1:], high_z[None]], axis=0)
        yield jnp.concatenate([low_y[:, None, :], values[:, :-1]], axis=1)
        yield jnp.concatenate([values[:, 1:], high_y[:, None, :]], axis=1)
        yield jnp.where(lane == 0, side, pltpu.roll(values, 1, 2))
        yield jnp.where(lane == LANES - 1, side, pltpu.roll(values, LANES - 1, 2))

    def a_pack(s, c):
        slot = s * 3 + c
        if s == 0:
            values = load[c]
            w[slot, 0:BRICK, 0:BRICK, :] = values
        else:
            values = w[slot, 0:BRICK, 0:BRICK, :]
        ys[slot, 0] = values[:, 0:MARGIN, :]
        ys[slot, 1] = values[:, BRICK - MARGIN:BRICK, :]

    def z_planes(ref, slot, rows):
        def at(first):
            return ref.at[slot, pl.ds(first, MARGIN), rows]

        return (at(0), at(BRICK + MARGIN)), (at(BRICK - MARGIN), at(BRICK))

    def a_send(s, c):
        slot = s * 3 + c
        send(slot, AY, (ys.at[slot, 0], yr.at[slot, 1]), (ys.at[slot, 1], yr.at[slot, 0]))
        send(slot, AZ, *z_planes(w, slot, pl.ds(0, BRICK)))

    def a_z(s, c):
        slot = s * 3 + c
        arrive(slot, AY)
        low = keep(has_lower["gy"], yr[slot, 0])
        high = keep(has_upper["gy"], yr[slot, 1])
        w[slot, 0:BRICK, BRICK:LENGTH, :] = jnp.concatenate([low, high], axis=1)
        send(slot, AE, *z_planes(w, slot, pl.ds(BRICK, 2 * MARGIN)))

    def a_x(s, c):
        slot = s * 3 + c
        arrive(slot, AZ)
        arrive(slot, AE)
        low = w[slot, BRICK:BRICK + MARGIN]
        w[slot, BRICK:BRICK + MARGIN] = keep(has_lower["gz"], low)
        high = w[slot, BRICK + MARGIN:LENGTH]
        w[slot, BRICK + MARGIN:LENGTH] = keep(has_upper["gz"], high)
        rows = flat(w, slot)
        total = jnp.zeros((LANES, LANES), F32)
        for i in range(CHUNKS):
            part = pltpu.roll(rows[i * LANES:(i + 1) * LANES, :], 8 * i + MARGIN, 1)
            total = jnp.where((lanes >= 8 * i) & (lanes < 8 * i + 8), part, total)
        total = jnp.transpose(total)[:CHUNKS * 8].reshape(CHUNKS, 8, LANES)
        xs[slot, 0] = total[:, MARGIN:]
        xs[slot, 1] = total[:, :MARGIN]
        send(slot, AX, (xs.at[slot, 0], xr.at[slot, 1]), (xs.at[slot, 1], xr.at[slot, 0]))

    one, two = (b1a, b1b), (b2a, b2b)

    def transform(matrix, source, target, strided, scale=None):
        def body(i, carry):
            outs = []
            for k in range(UNROLL):
                at = pl.ds(pl.multiple_of((i * UNROLL + k) * 2 * LENGTH, 8), 2 * LENGTH)
                values = jnp.concatenate([source[0][at, :], source[1][at, :]], axis=1)
                outs.append(dot(matrix[...], triple(values)))
            for k in range(UNROLL):
                at = pl.ds(pl.multiple_of((i * UNROLL + k) * 2 * LENGTH, 8), 2 * LENGTH)
                out = outs[k]
                if scale is not None:
                    out = out * scale[at, :]
                for half in range(2):
                    part = out[:, half * LANES:(half + 1) * LANES]
                    if strided:
                        for which in range(2):
                            spot = pl.ds((i * UNROLL + k) * 2 + which, LENGTH, stride=LENGTH)
                            target[half][spot, :] = part[which * LENGTH:(which + 1) * LENGTH]
                    else:
                        target[half][at, :] = part
            return carry

        lax.fori_loop(0, LENGTH // 2 // UNROLL, body, 0)

    def s1(s, c):
        slot = s * 3 + c
        arrive(slot, AX)

        rows = flat(w, slot)
        near = jnp.concatenate([keep(has_lower["gx"], xr[slot, 0]), keep(has_upper["gx"], xr[slot, 1])], axis=1)
        high = near.astype(BF16).astype(F32)
        near = jnp.concatenate([high, near - high, high], axis=1)
        sides = []
        for first in range(0, CHUNKS, 5):
            group = near[first:first + 5].reshape(-1, LANES)
            blank = jnp.zeros((LANES - group.shape[0], LANES), F32)
            sides.append(jnp.transpose(jnp.concatenate([group, blank], axis=0)))
        for i in range(CHUNKS):
            at = pl.ds(i * LANES, LANES)
            side = sides[i // 5]
            if i % 5:
                side = pltpu.roll(side, LANES - 24 * (i % 5), 1)
            high, low = halves(rows[at, :])
            out = dot(jnp.concatenate([high, low], axis=1), into_1[...])
            out += dot(jnp.concatenate([high, side.astype(BF16)], axis=1), into_2[...])
            b1a[at, :] = out[:, :LANES]
            b1b[at, :] = out[:, LANES:]

        transform(fwd, one, two, True)

    def s2(s, c):
        transform(fwd, two, one, False, rinv.at[c])
        transform(bwd, one, two, True)

    def s3(s, c):
        slot = s * 3 + c
        transform(bwd, two, one, False)

        rows = flat(zb, slot)
        margin = jnp.zeros((LANES, LANES), F32)
        for i in range(CHUNKS):
            at = pl.ds(i * LANES, LANES)
            high, low = halves(b1a[at, :])
            tail = b1b[at, :]
            tail_high = tail.astype(BF16).astype(F32)
            packed = tail_high + pltpu.roll(tail - tail_high, 32, 1) + pltpu.roll(tail_high, 64, 1)
            out = dot(jnp.concatenate([high, low], axis=1), out_1[...])
            out += dot(jnp.concatenate([high, packed.astype(BF16)], axis=1), out_2[...])
            rows[at, :] = out[:, :LANES]
            part = out[:, LANES:]
            margin += pltpu.roll(part, 8 * i, 1) if i else part
        margin = jnp.transpose(margin)[:CHUNKS * 8].reshape(CHUNKS, 8, LANES)
        fs[slot, 0] = margin[:, :MARGIN]
        fs[slot, 1] = margin[:, MARGIN:]
        send(slot, BX, (fs.at[slot, 0], fr.at[slot, 1]), (fs.at[slot, 1], fr.at[slot, 0]))

    def b_z(s, c):
        slot = s * 3 + c
        arrive(slot, BX)

        near = jnp.concatenate([keep(has_upper["gx"], fr[slot, 1]), keep(has_lower["gx"], fr[slot, 0])], axis=1)
        blank = jnp.zeros((LANES - CHUNKS * 8, LANES), F32)
        side = jnp.transpose(jnp.concatenate([near.reshape(CHUNKS * 8, LANES), blank], axis=0))
        rows = flat(zb, slot)
        edge = (lanes < MARGIN) | (lanes >= LANES - MARGIN)
        for i in range(CHUNKS):
            at = pl.ds(i * LANES, LANES)
            rows[at, :] += jnp.where(edge, pltpu.roll(side, LANES - 8 * i - MARGIN, 1), 0.0)

        send(
            slot, BZ,
            (zb.at[slot, pl.ds(BRICK, MARGIN)], zr.at[slot, 1]),
            (zb.at[slot, pl.ds(BRICK + MARGIN, MARGIN)], zr.at[slot, 0]),
        )

    def b_y(s, c):
        slot = s * 3 + c
        arrive(slot, BZ)
        zb[slot, 0:MARGIN] += keep(has_lower["gz"], zr[slot, 0])
        zb[slot, BRICK - MARGIN:BRICK] += keep(has_upper["gz"], zr[slot, 1])
        other = slot + 3 * SWEEPS
        rows = zb[slot, 0:BRICK, BRICK:LENGTH, :]
        ys[other, 0] = rows[:, :MARGIN]
        ys[other, 1] = rows[:, MARGIN:]
        y_pack(slot, zb[slot, 0:BRICK, 0:BRICK, :])
        send(slot, BY, (ys.at[other, 0], yr.at[other, 1]), (ys.at[other, 1], yr.at[other, 0]))
        y_send(slot)

    def c_start(s, c):
        slot = s * 3 + c
        arrive(slot, BY)
        other = slot + 3 * SWEEPS
        low = keep(has_lower["gy"], yr[other, 0])
        high = keep(has_upper["gy"], yr[other, 1])
        own = zb[slot, 0:BRICK, 0:BRICK, :]
        blank = jnp.zeros((BRICK, MARGIN, LANES), F32)
        own = jnp.concatenate([
            own[:, :8] + jnp.concatenate([low, blank], axis=1),
            own[:, 8:24],
            own[:, 24:] + jnp.concatenate([blank, high], axis=1),
        ], axis=1)
        corr[slot] = own
        xz_pack(slot, own)
        xz_send(slot)
        if s == SWEEPS - 1:
            total = own
            for before in range(s):
                total = corr[before * 3 + c] + total
            done[0, c] = total
            store(0, c, disp)

    def store(which, c, target):
        copy = pltpu.make_async_copy(done.at[which, c], target.at[c], out_sem.at[which * 3 + c])
        copy.start()
        stores.append(copy)

    stores = []

    def update(s, c):
        slot = s * 3 + c
        arrive(slot, CY)
        margins = zb[slot, 0:BRICK, BRICK:LENGTH, :]
        halo = halo_get(
            slot,
            keep(has_lower["gy"], cyr[slot, 0] + margins[:, MARGIN - 1, :]),
            keep(has_upper["gy"], cyr[slot, 1] + margins[:, MARGIN, :]),
        )
        values = corr[slot]
        total = SIGMA_SHIFT * modulus[...] * values
        for number, moved in enumerate(shifts(values, halo)):
            total = total + (ratio(c, number // 2) * 0.5) * faces[number] * (values - moved)
        if s == SWEEPS - 1:
            done[1, c] = w[slot, 0:BRICK, 0:BRICK, :] - total
            store(1, c, resid)
        else:
            w[slot + 3, 0:BRICK, 0:BRICK, :] = w[slot, 0:BRICK, 0:BRICK, :] - total
            a_pack(s + 1, c)
            a_send(s + 1, c)

    def stiff(s, c):
        arrive(6, CY)
        own = modulus[...]
        low, high = keep(has_lower["gy"], cyr[6, 0]), keep(has_upper["gy"], cyr[6, 1])
        for number, moved in enumerate(shifts(own, halo_get(6, low, high))):
            faces[number] = own + moved

    for c in range(3):
        a_pack(0, c)
    for slot in range(6):
        w[slot, LENGTH:] = jnp.zeros((PLANES - LENGTH, LENGTH, LANES), F32)

    def look(z, carry):
        picked = labels[z]
        value = jnp.zeros(picked.shape, F32)
        for number in range(table.shape[0]):
            value = jnp.where(picked == number, table[number], value)
        modulus[z] = jnp.where(mask[z] == 1, value, VOID_MODULUS)
        return carry

    lax.fori_loop(0, BRICK, look, 0)
    y_pack(6, modulus[...])
    xz_pack(6, modulus[...])

    for c in range(3):
        def invert(y, carry, c=c):
            at = pl.ds(pl.multiple_of(y * LENGTH, 8), LENGTH)
            rinv[c, at, :] = 1.0 / (REF_MODULUS * (
                ratio(c, 0) * eigen_rows[...]
                + ratio(c, 1) * eigen_rows[pl.ds(y, 1), :]
                + ratio(c, 2) * eigen_x[...]
                + SIGMA_SHIFT
            ))
            return carry

        lax.fori_loop(0, LENGTH, invert, 0)

    pl.semaphore_wait(barrier, 6)
    for c in range(3):
        a_send(0, c)
    y_send(6)
    xz_send(6)

    stages = dict(a_z=a_z, a_x=a_x, s1=s1, s2=s2, s3=s3, b_z=b_z, b_y=b_y, c_start=c_start, update=update,
                  stiff=stiff)
    for s, c, name in ORDER:
        stages[name](s, c)

    for made in pending.values():
        for copy in made:
            copy.wait_send()
    for copy in stores:
        copy.wait()


def local(load, labels, mask, table):
    tables = constants()
    vmem = pl.BlockSpec(memory_space=pltpu.VMEM)
    smem = pl.BlockSpec(memory_space=pltpu.SMEM)
    slots = 3 * SWEEPS
    field = jax.ShapeDtypeStruct(load.shape, F32)
    block = (BRICK, BRICK, LANES)
    return pl.pallas_call(
        kernel,
        out_shape=(field, field),
        in_specs=[vmem, vmem, vmem, smem] + [vmem] * len(tables),
        out_specs=(pl.BlockSpec(memory_space=pl.ANY),) * 2,
        scratch_shapes=[
            pltpu.VMEM(block, F32),
            pltpu.VMEM((6,) + block, F32),
            pltpu.VMEM((slots, PLANES, LENGTH, LANES), F32),
            pltpu.VMEM((slots, 2, CHUNKS, MARGIN, LANES), F32),
            pltpu.VMEM((slots, 2, CHUNKS, MARGIN, LANES), F32),
            pltpu.VMEM((PADDED, LANES), F32),
            pltpu.VMEM((PADDED, LANES), F32),
            pltpu.VMEM((PADDED, LANES), F32),
            pltpu.VMEM((PADDED, LANES), F32),
            pltpu.VMEM((slots, PLANES, LENGTH, LANES), F32),
            pltpu.VMEM((slots, 2, CHUNKS, MARGIN, LANES), F32),
            pltpu.VMEM((slots, 2, CHUNKS, MARGIN, LANES), F32),
            pltpu.VMEM((slots, 2, MARGIN, LENGTH, LANES), F32),
            pltpu.VMEM((2 * slots, 2, BRICK, MARGIN, LANES), F32),
            pltpu.VMEM((2 * slots, 2, BRICK, MARGIN, LANES), F32),
            pltpu.VMEM((slots,) + block, F32),
            pltpu.VMEM((3, ROWS, WIDE), F32),
            pltpu.VMEM((slots + 1, 2, BRICK, LANES), F32),
            pltpu.VMEM((slots + 1, 2, BRICK, LANES), F32),
            pltpu.VMEM((slots + 1, 2, BRICK, LANES), F32),
            pltpu.VMEM((slots + 1, 2, BRICK, LANES), F32),
            pltpu.VMEM((slots + 1, 16, LANES), F32),
            pltpu.VMEM((slots + 1, 2, 16, LANES), F32),
            pltpu.VMEM((2, 3) + block, F32),
            pltpu.SemaphoreType.DMA(((slots + 1) * PHASES * 2,)),
            pltpu.SemaphoreType.DMA(((slots + 1) * PHASES * 2,)),
            pltpu.SemaphoreType.DMA((6,)),
        ],
        compiler_params=pltpu.CompilerParams(
            collective_id=0, has_side_effects=True, vmem_limit_bytes=62 * 1024 * 1024
        ),
    )(load, labels, mask, table, *tables)


def solution(mesh):
    placed = (P(None, "gz", "gy", "gx"), P("gz", "gy", "gx"), P("gz", "gy", "gx"), P())
    return jax.shard_map(
        local,
        mesh=mesh,
        in_specs=placed,
        out_specs=(P(None, "gz", "gy", "gx"), P(None, "gz", "gy", "gx")),
        check_vma=False,
    )
```

```python
import jax
import jax.numpy as jnp
import numpy as np
from jax import lax
from jax.experimental import pallas as pl
from jax.experimental.pallas import tpu as pltpu
from jax.sharding import PartitionSpec as P

BRICK = 32
MARGIN = 4
SWEEPS = 2
LENGTH = BRICK + 2 * MARGIN
LANES = 128
WIDE = 256
ROWS = LENGTH * LENGTH
PADDED = 1664
CHUNKS = PADDED // LANES
OWNED = BRICK * LENGTH
LAMBDA_RATIO = 2.0
SIGMA_SHIFT = 0.1
REF_MODULUS = 1.5
VOID_MODULUS = 0.1
MESH = pl.DeviceIdType.MESH
UNROLL = 5
PHASES = 9
AY, AZ, AX, BX, BZ, BY, CY, CZ, CX = range(PHASES)
AXIS = ("gy", "gz", "gx", "gx", "gz", "gy", "gy", "gz", "gx")
QUARTERS = ((0, 0), (0, 1), (1, 0), (1, 1))
PLANES = 42
ORDER = (
    (0, 0, "a_x"), (0, 1, "a_x"), (0, 0, "s1"), (0, 0, "s2"), (0, 2, "a_x"), (0, 0, "s3"), (0, 1, "s1"),
    (0, 1, "s2"), (0, 0, "stiff"), (0, 0, "b_x"), (0, 1, "s3"), (0, 2, "s1"), (0, 2, "s2"), (0, 1, "b_x"),
    (0, 2, "s3"), (0, 0, "c_start"), (0, 2, "b_x"), (0, 0, "update"), (0, 1, "c_start"), (0, 1, "update"),
    (0, 2, "c_start"), (1, 0, "a_x"), (0, 2, "update"), (1, 1, "a_x"), (1, 0, "s1"), (1, 0, "s2"), (1, 0, "s3"),
    (1, 2, "a_x"), (1, 1, "s1"), (1, 1, "s2"), (1, 0, "b_x"), (1, 1, "s3"), (1, 2, "s1"), (1, 2, "s2"),
    (1, 1, "b_x"), (1, 2, "s3"), (1, 0, "c_start"), (1, 2, "b_x"), (1, 0, "update"), (1, 1, "c_start"),
    (1, 1, "update"), (1, 2, "c_start"), (1, 2, "update"),
)
F32 = jnp.float32
BF16 = jnp.bfloat16


def ratio(component, direction):
    return LAMBDA_RATIO if component == direction else 1.0


def halves(values):
    high = values.astype(BF16)
    return high, (values - high.astype(F32)).astype(BF16)


def constants():
    grid = np.arange(1, LENGTH + 1, dtype=np.float64)
    sine = np.sqrt(2.0 / (LENGTH + 1)) * np.sin(np.pi * grid[:, None] * grid[None, :] / (LENGTH + 1))
    eigen = 2.0 - 2.0 * np.cos(np.pi * grid / (LENGTH + 1))
    spot = np.arange(LENGTH, dtype=np.float64)
    ramp = np.minimum(np.minimum((spot + 0.5) / (2 * MARGIN), (LENGTH - 0.5 - spot) / (2 * MARGIN)), 1.0)
    ramped = ramp[:, None] * sine
    place = np.concatenate([np.arange(MARGIN, MARGIN + BRICK), np.arange(MARGIN), np.arange(MARGIN + BRICK, LENGTH)])
    forward = ramped[place].T
    backward = sine.T[place]
    count = LANES // BRICK
    wide_x = LANES + 2 * MARGIN
    forward_x = np.zeros((wide_x, WIDE))
    backward_x = np.zeros((WIDE, wide_x))
    for brick in range(count):
        rows = slice(brick * BRICK, brick * BRICK + LENGTH)
        columns = slice(brick * LENGTH, (brick + 1) * LENGTH)
        forward_x[rows, columns] = ramped
        backward_x[columns, rows] = sine
    edge = slice(LANES, LANES + 2 * MARGIN)
    into = forward_x[MARGIN:MARGIN + LANES]
    into_edge = np.concatenate([forward_x[:MARGIN], forward_x[MARGIN + LANES:]])
    out = np.zeros((WIDE, WIDE))
    out[:, :LANES] = backward_x[:, MARGIN:MARGIN + LANES]
    out[:, edge] = np.concatenate([backward_x[:, :MARGIN], backward_x[:, MARGIN + LANES:]], axis=1)
    rest = count * LENGTH - LANES
    eigen_x = np.zeros((1, WIDE))
    eigen_x[0, : count * LENGTH] = np.tile(eigen, count)
    eigen_lanes = np.broadcast_to(eigen[:, None], (LENGTH, WIDE))

    def high(matrix):
        return matrix.astype(np.float32).astype(BF16).astype(np.float64)

    def low(matrix):
        return matrix - high(matrix)

    def pair(matrix):
        zero = np.zeros((LENGTH, LENGTH))
        both = np.block([[matrix, zero], [zero, matrix]])
        return np.concatenate([high(both), high(both), low(both)], axis=1)

    def tall(*parts):
        blank = np.zeros((2 * LANES - sum(p.shape[0] for p in parts), WIDE))
        return np.concatenate(parts + (blank,))

    head, tail = out[:LANES], out[LANES:LANES + rest]
    return [m.astype(BF16) for m in (
        pair(forward),
        pair(backward),
        tall(high(into), high(into)),
        tall(low(into), high(into_edge), high(into_edge), low(into_edge)),
        tall(high(head), high(head)),
        tall(low(head), high(tail), high(tail), low(tail)),
    )] + [eigen_x.astype(np.float32), np.ascontiguousarray(eigen_lanes).astype(np.float32)]


def dot(a, b):
    return jnp.dot(a, b, preferred_element_type=F32)


def triple(values):
    high, low = halves(values)
    return jnp.concatenate([high, low, high], axis=0)


def kernel(
    load, labels, mask, table,
    fwd, bwd, into_1, into_2, out_1, out_2, eigen_x, eigen_rows,
    disp, resid,
    modulus, faces, w, xs, xr, b1a, b1b, b2a, b2b, zb, fs, fr, zr, ys, yr, corr, rinv,
    cys, cyr, czs, czr, cxs, cxr,
    de, dr, send_sem, recv_sem, corner_send, corner_recv,
):
    index = {a: lax.axis_index(a) for a in ("gx", "gy", "gz")}
    count = {a: lax.axis_size(a) for a in ("gx", "gy", "gz")}
    lower = {a: lax.rem(index[a] + count[a] - 1, count[a]) for a in index}
    upper = {a: lax.rem(index[a] + 1, count[a]) for a in index}
    has_lower = {a: index[a] > 0 for a in index}
    has_upper = {a: index[a] < count[a] - 1 for a in index}

    barrier = pltpu.get_barrier_semaphore()
    for a in ("gx", "gy", "gz"):
        pl.semaphore_signal(barrier, inc=1, device_id={a: lower[a]}, device_id_type=MESH)
        pl.semaphore_signal(barrier, inc=1, device_id={a: upper[a]}, device_id_type=MESH)
    near = (lower, upper)
    for z, y in QUARTERS:
        pl.semaphore_signal(
            barrier, inc=1, device_id={"gz": near[z]["gz"], "gy": near[y]["gy"]}, device_id_type=MESH
        )

    def copies(slot, phase, down, up):
        a = AXIS[phase]
        made = []
        for side, (source, target), device in ((0, down, lower[a]), (1, up, upper[a])):
            number = (slot * PHASES + phase) * 2 + side
            made.append(pltpu.make_async_remote_copy(
                src_ref=source, dst_ref=target,
                send_sem=send_sem.at[number], recv_sem=recv_sem.at[number],
                device_id={a: device}, device_id_type=MESH,
            ))
        return made

    pending = {}

    def send(slot, phase, down, up):
        made = copies(slot, phase, down, up)
        for copy in made:
            copy.start()
        pending[slot, phase] = made

    def arrive(slot, phase):
        for copy in pending[slot, phase]:
            copy.wait_recv()

    def send_corners(slot, sources, size):
        made = []
        for quarter, (z, y) in enumerate(QUARTERS):
            number = slot * 4 + quarter
            made.append(pltpu.make_async_remote_copy(
                src_ref=sources[quarter], dst_ref=dr.at[slot, 3 - quarter, pl.ds(0, size)],
                send_sem=corner_send.at[number], recv_sem=corner_recv.at[slot * 4 + 3 - quarter],
                device_id={"gz": near[z]["gz"], "gy": near[y]["gy"]}, device_id_type=MESH,
            ))
        for copy in made:
            copy.start()
        pending[slot, "corner"] = made

    def arrive_corners(slot, size):
        blocks = []
        for copy in reversed(pending[slot, "corner"]):
            copy.wait_recv()
        for quarter, (z, y) in enumerate(QUARTERS):
            flag = (has_lower, has_upper)[z]["gz"] & (has_lower, has_upper)[y]["gy"]
            blocks.append(keep(flag, dr[slot, quarter, 0:size]))
        return blocks

    def flat(ref, slot):
        return ref.at[slot].reshape(PLANES * LENGTH, LANES)

    def keep(flag, values):
        return jnp.where(flag, values, 0.0)

    lanes = lax.broadcasted_iota(jnp.int32, (LANES, LANES), 1)

    def face_columns(values):
        flat = values.reshape(BRICK * BRICK, LANES)
        total = jnp.zeros((LANES, LANES), F32)
        for i in range(8):
            part = pltpu.roll(flat[i * LANES:(i + 1) * LANES], 2 * i + 1, 1)
            total = jnp.where((lanes == 2 * i) | (lanes == 2 * i + 1), part, total)
        return jnp.transpose(total)[:16]

    def y_pack(slot, values):
        cys[slot, 0] = values[:, 0, :]
        cys[slot, 1] = values[:, BRICK - 1, :]

    def y_send(slot):
        send(slot, CY, (cys.at[slot, 0], cyr.at[slot, 1]), (cys.at[slot, 1], cyr.at[slot, 0]))

    def xz_pack(slot, values):
        czs[slot, 0] = values[0]
        czs[slot, 1] = values[BRICK - 1]
        cxs[slot] = face_columns(values)

    def xz_send(slot):
        send(slot, CZ, (czs.at[slot, 0], czr.at[slot, 1]), (czs.at[slot, 1], czr.at[slot, 0]))
        send(slot, CX, (cxs.at[slot], cxr.at[slot, 1]), (cxs.at[slot], cxr.at[slot, 0]))

    def halo_get(slot, low_y, high_y):
        for phase in (CZ, CX):
            arrive(slot, phase)
        low_z = keep(has_lower["gz"], czr[slot, 0])
        high_z = keep(has_upper["gz"], czr[slot, 1])
        left = keep(has_lower["gx"], cxr[slot, 0])
        right = keep(has_upper["gx"], cxr[slot, 1])
        odd = lax.rem(lax.broadcasted_iota(jnp.int32, (16, LANES), 0), 2) == 1
        both = jnp.where(odd, pltpu.roll(left, 1, 0), pltpu.roll(right, 15, 0))
        side = jnp.transpose(jnp.concatenate([both, jnp.zeros((LANES - 16, LANES), F32)], axis=0))
        side = jnp.concatenate(
            [pltpu.roll(side, LANES - 1 - 2 * i, 1) for i in range(8)], axis=0
        ).reshape(BRICK, BRICK, LANES)
        return low_y, high_y, low_z, high_z, side

    def shifts(values, halo):
        low_y, high_y, low_z, high_z, side = halo
        lane = lax.broadcasted_iota(jnp.int32, values.shape, 2)
        yield jnp.concatenate([low_z[None], values[:-1]], axis=0)
        yield jnp.concatenate([values[1:], high_z[None]], axis=0)
        yield jnp.concatenate([low_y[:, None, :], values[:, :-1]], axis=1)
        yield jnp.concatenate([values[:, 1:], high_y[:, None, :]], axis=1)
        yield jnp.where(lane == 0, side, pltpu.roll(values, 1, 2))
        yield jnp.where(lane == LANES - 1, side, pltpu.roll(values, LANES - 1, 2))

    def a_pack(s, c):
        slot = s * 3 + c
        if s == 0:
            values = load[c]
            w[slot, 0:BRICK, 0:BRICK, :] = values
        else:
            values = w[slot, 0:BRICK, 0:BRICK, :]
        ys[slot, 0] = values[:, 0:MARGIN, :]
        ys[slot, 1] = values[:, BRICK - MARGIN:BRICK, :]

    def a_send(s, c):
        slot = s * 3 + c
        ends = (pl.ds(0, MARGIN), pl.ds(BRICK - MARGIN, MARGIN))
        send_corners(slot, [ys.at[slot, y, ends[z]] for z, y in QUARTERS], MARGIN)
        send(slot, AY, (ys.at[slot, 0], yr.at[slot, 1]), (ys.at[slot, 1], yr.at[slot, 0]))
        own = pl.ds(0, BRICK)
        send(
            slot, AZ,
            (w.at[slot, ends[0], own], w.at[slot, pl.ds(BRICK + MARGIN, MARGIN), own]),
            (w.at[slot, ends[1], own], w.at[slot, pl.ds(BRICK, MARGIN), own]),
        )

    def a_x(s, c):
        slot = s * 3 + c
        arrive(slot, AY)
        low = keep(has_lower["gy"], yr[slot, 0])
        high = keep(has_upper["gy"], yr[slot, 1])
        w[slot, 0:BRICK, BRICK:LENGTH, :] = jnp.concatenate([low, high], axis=1)
        blocks = arrive_corners(slot, MARGIN)
        arrive(slot, AZ)
        for z, flag in ((0, has_lower["gz"]), (1, has_upper["gz"])):
            planes = slice(BRICK + z * MARGIN, BRICK + (z + 1) * MARGIN)
            w[slot, planes, 0:BRICK, :] = keep(flag, w[slot, planes, 0:BRICK, :])
            w[slot, planes, BRICK:LENGTH, :] = jnp.concatenate([blocks[2 * z], blocks[2 * z + 1]], axis=1)
        rows = flat(w, slot)
        total = jnp.zeros((LANES, LANES), F32)
        for i in range(CHUNKS):
            part = pltpu.roll(rows[i * LANES:(i + 1) * LANES, :], 8 * i + MARGIN, 1)
            total = jnp.where((lanes >= 8 * i) & (lanes < 8 * i + 8), part, total)
        total = jnp.transpose(total)[:CHUNKS * 8].reshape(CHUNKS, 8, LANES)
        xs[slot, 0] = total[:, MARGIN:]
        xs[slot, 1] = total[:, :MARGIN]
        send(slot, AX, (xs.at[slot, 0], xr.at[slot, 1]), (xs.at[slot, 1], xr.at[slot, 0]))

    one, two = (b1a, b1b), (b2a, b2b)

    def transform(matrix, source, target, strided, scale=None):
        def body(i, carry):
            outs = []
            for k in range(UNROLL):
                at = pl.ds(pl.multiple_of((i * UNROLL + k) * 2 * LENGTH, 8), 2 * LENGTH)
                values = jnp.concatenate([source[0][at, :], source[1][at, :]], axis=1)
                outs.append(dot(matrix[...], triple(values)))
            for k in range(UNROLL):
                at = pl.ds(pl.multiple_of((i * UNROLL + k) * 2 * LENGTH, 8), 2 * LENGTH)
                out = outs[k]
                if scale is not None:
                    out = out * scale[at, :]
                for half in range(2):
                    part = out[:, half * LANES:(half + 1) * LANES]
                    if strided:
                        for which in range(2):
                            spot = pl.ds((i * UNROLL + k) * 2 + which, LENGTH, stride=LENGTH)
                            target[half][spot, :] = part[which * LENGTH:(which + 1) * LENGTH]
                    else:
                        target[half][at, :] = part
            return carry

        lax.fori_loop(0, LENGTH // 2 // UNROLL, body, 0)

    def s1(s, c):
        slot = s * 3 + c
        arrive(slot, AX)

        rows = flat(w, slot)
        near = jnp.concatenate([keep(has_lower["gx"], xr[slot, 0]), keep(has_upper["gx"], xr[slot, 1])], axis=1)
        high = near.astype(BF16).astype(F32)
        near = jnp.concatenate([high, near - high, high], axis=1)
        sides = []
        for first in range(0, CHUNKS, 5):
            group = near[first:first + 5].reshape(-1, LANES)
            blank = jnp.zeros((LANES - group.shape[0], LANES), F32)
            sides.append(jnp.transpose(jnp.concatenate([group, blank], axis=0)))
        for i in range(CHUNKS):
            at = pl.ds(i * LANES, LANES)
            side = sides[i // 5]
            if i % 5:
                side = pltpu.roll(side, LANES - 24 * (i % 5), 1)
            high, low = halves(rows[at, :])
            out = dot(jnp.concatenate([high, low], axis=1), into_1[...])
            out += dot(jnp.concatenate([high, side.astype(BF16)], axis=1), into_2[...])
            b1a[at, :] = out[:, :LANES]
            b1b[at, :] = out[:, LANES:]

        transform(fwd, one, two, True)

    def s2(s, c):
        transform(fwd, two, one, False, rinv.at[c])
        transform(bwd, one, two, True)

    def s3(s, c):
        slot = s * 3 + c
        transform(bwd, two, one, False)

        rows = flat(zb, slot)
        margin = jnp.zeros((LANES, LANES), F32)
        for i in range(CHUNKS):
            at = pl.ds(i * LANES, LANES)
            high, low = halves(b1a[at, :])
            tail = b1b[at, :]
            tail_high = tail.astype(BF16).astype(F32)
            packed = tail_high + pltpu.roll(tail - tail_high, 32, 1) + pltpu.roll(tail_high, 64, 1)
            out = dot(jnp.concatenate([high, low], axis=1), out_1[...])
            out += dot(jnp.concatenate([high, packed.astype(BF16)], axis=1), out_2[...])
            rows[at, :] = out[:, :LANES]
            part = out[:, LANES:]
            margin += pltpu.roll(part, 8 * i, 1) if i else part
        margin = jnp.transpose(margin)[:CHUNKS * 8].reshape(CHUNKS, 8, LANES)
        fs[slot, 0] = margin[:, :MARGIN]
        fs[slot, 1] = margin[:, MARGIN:]
        send(slot, BX, (fs.at[slot, 0], fr.at[slot, 1]), (fs.at[slot, 1], fr.at[slot, 0]))

    def b_x(s, c):
        slot = s * 3 + c
        arrive(slot, BX)

        near = jnp.concatenate([keep(has_upper["gx"], fr[slot, 1]), keep(has_lower["gx"], fr[slot, 0])], axis=1)
        blank = jnp.zeros((LANES - CHUNKS * 8, LANES), F32)
        side = jnp.transpose(jnp.concatenate([near.reshape(CHUNKS * 8, LANES), blank], axis=0))
        rows = flat(zb, slot)
        edge = (lanes < MARGIN) | (lanes >= LANES - MARGIN)
        for i in range(CHUNKS):
            at = pl.ds(i * LANES, LANES)
            rows[at, :] += jnp.where(edge, pltpu.roll(side, LANES - 8 * i - MARGIN, 1), 0.0)

        other = slot + 3 * SWEEPS
        rows = zb[slot, :LENGTH, BRICK:LENGTH, :]
        values = zb[slot, :LENGTH, 0:BRICK, :]
        for quarter, (z, y) in enumerate(QUARTERS):
            planes = slice(BRICK + z * MARGIN, BRICK + (z + 1) * MARGIN)
            de[slot, quarter, 0:MARGIN] = rows[planes, y * MARGIN:(y + 1) * MARGIN]
            de[slot, quarter, MARGIN] = values[planes, y * (BRICK - 1)]
        ys[other, 0] = rows[:BRICK, :MARGIN]
        ys[other, 1] = rows[:BRICK, MARGIN:]
        y_pack(slot, values[:BRICK])
        send_corners(other, [de.at[slot, quarter] for quarter in range(4)], MARGIN + 1)
        send(slot, BY, (ys.at[other, 0], yr.at[other, 1]), (ys.at[other, 1], yr.at[other, 0]))
        y_send(slot)
        send(
            slot, BZ,
            (zb.at[slot, pl.ds(BRICK, MARGIN)], zr.at[slot, 1]),
            (zb.at[slot, pl.ds(BRICK + MARGIN, MARGIN)], zr.at[slot, 0]),
        )

    def c_start(s, c):
        slot = s * 3 + c
        other = slot + 3 * SWEEPS
        arrive(slot, BZ)
        zb[slot, 0:MARGIN] += keep(has_lower["gz"], zr[slot, 0])
        zb[slot, BRICK - MARGIN:BRICK] += keep(has_upper["gz"], zr[slot, 1])
        arrive(slot, BY)
        arrive(slot, CY)
        blocks = arrive_corners(other, MARGIN + 1)
        margins = zb[slot, 0:BRICK, BRICK:LENGTH, :]

        def joined(y, flag):
            near, far = blocks[y], blocks[2 + y]
            rows = keep(flag, yr[other, y])
            rows = jnp.concatenate([
                rows[:MARGIN] + near[:MARGIN], rows[MARGIN:BRICK - MARGIN], rows[BRICK - MARGIN:] + far[:MARGIN]
            ], axis=0)
            face = keep(flag, cyr[slot, y] + margins[:, MARGIN - 1 + y, :])
            blank = jnp.zeros((BRICK - 2 * MARGIN, LANES), F32)
            return rows, face + jnp.concatenate([near[MARGIN], blank, far[MARGIN]], axis=0)

        low, face = joined(0, has_lower["gy"])
        cyr[slot, 0] = face
        high, face = joined(1, has_upper["gy"])
        cyr[slot, 1] = face
        own = zb[slot, 0:BRICK, 0:BRICK, :]
        blank = jnp.zeros((BRICK, MARGIN, LANES), F32)
        own = jnp.concatenate([
            own[:, :8] + jnp.concatenate([low, blank], axis=1),
            own[:, 8:24],
            own[:, 24:] + jnp.concatenate([blank, high], axis=1),
        ], axis=1)
        corr[slot] = own
        xz_pack(slot, own)
        xz_send(slot)
        if s == SWEEPS - 1:
            total = own
            for before in range(s):
                total = corr[before * 3 + c] + total
            disp[c] = total

    def update(s, c):
        slot = s * 3 + c
        halo = halo_get(slot, cyr[slot, 0], cyr[slot, 1])
        values = corr[slot]
        total = SIGMA_SHIFT * modulus[...] * values
        for number, moved in enumerate(shifts(values, halo)):
            total = total + (ratio(c, number // 2) * 0.5) * faces[number] * (values - moved)
        if s == SWEEPS - 1:
            resid[c] = w[slot, 0:BRICK, 0:BRICK, :] - total
        else:
            w[slot + 3, 0:BRICK, 0:BRICK, :] = w[slot, 0:BRICK, 0:BRICK, :] - total
            a_pack(s + 1, c)
            a_send(s + 1, c)

    def stiff(s, c):
        arrive(6, CY)
        own = modulus[...]
        low, high = keep(has_lower["gy"], cyr[6, 0]), keep(has_upper["gy"], cyr[6, 1])
        for number, moved in enumerate(shifts(own, halo_get(6, low, high))):
            faces[number] = own + moved

    for c in range(3):
        a_pack(0, c)
    for slot in range(6):
        w[slot, LENGTH:] = jnp.zeros((PLANES - LENGTH, LENGTH, LANES), F32)

    def look(z, carry):
        picked = labels[z]
        value = jnp.zeros(picked.shape, F32)
        for number in range(table.shape[0]):
            value = jnp.where(picked == number, table[number], value)
        modulus[z] = jnp.where(mask[z] == 1, value, VOID_MODULUS)
        return carry

    lax.fori_loop(0, BRICK, look, 0)
    y_pack(6, modulus[...])
    xz_pack(6, modulus[...])

    for c in range(3):
        def invert(y, carry, c=c):
            at = pl.ds(pl.multiple_of(y * LENGTH, 8), LENGTH)
            rinv[c, at, :] = 1.0 / (REF_MODULUS * (
                ratio(c, 0) * eigen_rows[...]
                + ratio(c, 1) * eigen_rows[pl.ds(y, 1), :]
                + ratio(c, 2) * eigen_x[...]
                + SIGMA_SHIFT
            ))
            return carry

        lax.fori_loop(0, LENGTH, invert, 0)

    pl.semaphore_wait(barrier, 10)
    for c in range(3):
        a_send(0, c)
    y_send(6)
    xz_send(6)

    stages = dict(a_x=a_x, s1=s1, s2=s2, s3=s3, b_x=b_x, c_start=c_start, update=update,
                  stiff=stiff)
    for s, c, name in ORDER:
        stages[name](s, c)

    for made in pending.values():
        for copy in made:
            copy.wait_send()


def local(load, labels, mask, table):
    tables = constants()
    vmem = pl.BlockSpec(memory_space=pltpu.VMEM)
    smem = pl.BlockSpec(memory_space=pltpu.SMEM)
    slots = 3 * SWEEPS
    field = jax.ShapeDtypeStruct(load.shape, F32)
    block = (BRICK, BRICK, LANES)
    return pl.pallas_call(
        kernel,
        out_shape=(field, field),
        in_specs=[vmem, vmem, vmem, smem] + [vmem] * len(tables),
        out_specs=(vmem, vmem),
        scratch_shapes=[
            pltpu.VMEM(block, F32),
            pltpu.VMEM((6,) + block, F32),
            pltpu.VMEM((slots, PLANES, LENGTH, LANES), F32),
            pltpu.VMEM((slots, 2, CHUNKS, MARGIN, LANES), F32),
            pltpu.VMEM((slots, 2, CHUNKS, MARGIN, LANES), F32),
            pltpu.VMEM((PADDED, LANES), F32),
            pltpu.VMEM((PADDED, LANES), F32),
            pltpu.VMEM((PADDED, LANES), F32),
            pltpu.VMEM((PADDED, LANES), F32),
            pltpu.VMEM((slots, PLANES, LENGTH, LANES), F32),
            pltpu.VMEM((slots, 2, CHUNKS, MARGIN, LANES), F32),
            pltpu.VMEM((slots, 2, CHUNKS, MARGIN, LANES), F32),
            pltpu.VMEM((slots, 2, MARGIN, LENGTH, LANES), F32),
            pltpu.VMEM((2 * slots, 2, BRICK, MARGIN, LANES), F32),
            pltpu.VMEM((2 * slots, 2, BRICK, MARGIN, LANES), F32),
            pltpu.VMEM((slots,) + block, F32),
            pltpu.VMEM((3, ROWS, WIDE), F32),
            pltpu.VMEM((slots + 1, 2, BRICK, LANES), F32),
            pltpu.VMEM((slots + 1, 2, BRICK, LANES), F32),
            pltpu.VMEM((slots + 1, 2, BRICK, LANES), F32),
            pltpu.VMEM((slots + 1, 2, BRICK, LANES), F32),
            pltpu.VMEM((slots + 1, 16, LANES), F32),
            pltpu.VMEM((slots + 1, 2, 16, LANES), F32),
            pltpu.VMEM((slots, 4, MARGIN + 1, MARGIN, LANES), F32),
            pltpu.VMEM((2 * slots, 4, MARGIN + 1, MARGIN, LANES), F32),
            pltpu.SemaphoreType.DMA(((slots + 1) * PHASES * 2,)),
            pltpu.SemaphoreType.DMA(((slots + 1) * PHASES * 2,)),
            pltpu.SemaphoreType.DMA((2 * slots * 4,)),
            pltpu.SemaphoreType.DMA((2 * slots * 4,)),
        ],
        compiler_params=pltpu.CompilerParams(
            collective_id=0, has_side_effects=True, vmem_limit_bytes=36 * 1024 * 1024
        ),
    )(load, labels, mask, table, *tables)


def solution(mesh):
    placed = (P(None, "gz", "gy", "gx"), P("gz", "gy", "gx"), P("gz", "gy", "gx"), P())
    return jax.shard_map(
        local,
        mesh=mesh,
        in_specs=placed,
        out_specs=(P(None, "gz", "gy", "gx"), P(None, "gz", "gy", "gx")),
        check_vma=False,
    )
```

```python
import jax
import jax.numpy as jnp
import numpy as np
from jax import lax
from jax.experimental import pallas as pl
from jax.experimental.pallas import tpu as pltpu
from jax.sharding import PartitionSpec as P

BRICK = 32
MARGIN = 4
SWEEPS = 2
LENGTH = BRICK + 2 * MARGIN
LANES = 128
WIDE = 256
ROWS = LENGTH * LENGTH
PADDED = 1664
CHUNKS = PADDED // LANES
OWNED = BRICK * LENGTH
LAMBDA_RATIO = 2.0
SIGMA_SHIFT = 0.1
REF_MODULUS = 1.5
VOID_MODULUS = 0.1
MESH = pl.DeviceIdType.MESH
UNROLL = 5
PHASES = 10
AY, AZ, AE, AX, BX, BZ, BY, CY, CZ, CX = range(PHASES)
AXIS = ("gy", "gz", "gz", "gx", "gx", "gz", "gy", "gy", "gz", "gx")
PLANES = 42
TABLES = 8
ORDER = (
    (0, 0, "a_z"), (0, 1, "a_z"), (0, 0, "a_x"), (0, 2, "a_z"), (0, 1, "a_x"), (0, 0, "s1"), (0, 0, "s2"),
    (0, 0, "s3"), (0, 1, "s1"), (0, 2, "a_x"), (0, 0, "stiff"), (0, 0, "b_z"), (0, 1, "s2"), (0, 1, "s3"),
    (0, 0, "b_y"), (0, 2, "s1"), (0, 1, "b_z"), (0, 2, "s2"), (0, 2, "s3"), (0, 0, "c_start"), (0, 1, "b_y"),
    (0, 2, "b_z"), (0, 0, "update"), (0, 1, "c_start"), (0, 2, "b_y"), (1, 0, "a_z"), (0, 1, "update"),
    (1, 0, "a_x"), (0, 2, "c_start"), (1, 1, "a_z"), (0, 2, "update"), (1, 0, "s1"), (1, 1, "a_x"), (1, 0, "s2"),
    (1, 0, "s3"), (1, 2, "a_z"), (1, 1, "s1"), (1, 1, "s2"), (1, 2, "a_x"), (1, 0, "b_z"), (1, 1, "s3"),
    (1, 2, "s1"), (1, 2, "s2"), (1, 1, "b_z"), (1, 2, "s3"), (1, 0, "b_y"), (1, 2, "b_z"), (1, 1, "b_y"),
    (1, 2, "b_y"), (1, 0, "c_start"), (1, 1, "c_start"), (1, 2, "c_start"), (1, 0, "update"), (1, 1, "update"),
    (1, 2, "update"),
)
F32 = jnp.float32
BF16 = jnp.bfloat16


def ratio(component, direction):
    return LAMBDA_RATIO if component == direction else 1.0


def halves(values):
    high = values.astype(BF16)
    return high, (values - high.astype(F32)).astype(BF16)


def constants():
    grid = np.arange(1, LENGTH + 1, dtype=np.float64)
    sine = np.sqrt(2.0 / (LENGTH + 1)) * np.sin(np.pi * grid[:, None] * grid[None, :] / (LENGTH + 1))
    eigen = 2.0 - 2.0 * np.cos(np.pi * grid / (LENGTH + 1))
    spot = np.arange(LENGTH, dtype=np.float64)
    ramp = np.minimum(np.minimum((spot + 0.5) / (2 * MARGIN), (LENGTH - 0.5 - spot) / (2 * MARGIN)), 1.0)
    ramped = ramp[:, None] * sine
    place = np.concatenate([np.arange(MARGIN, MARGIN + BRICK), np.arange(MARGIN), np.arange(MARGIN + BRICK, LENGTH)])
    forward = ramped[place].T
    backward = sine.T[place]
    count = LANES // BRICK
    wide_x = LANES + 2 * MARGIN
    forward_x = np.zeros((wide_x, WIDE))
    backward_x = np.zeros((WIDE, wide_x))
    for brick in range(count):
        rows = slice(brick * BRICK, brick * BRICK + LENGTH)
        columns = slice(brick * LENGTH, (brick + 1) * LENGTH)
        forward_x[rows, columns] = ramped
        backward_x[columns, rows] = sine
    edge = slice(LANES, LANES + 2 * MARGIN)
    into = forward_x[MARGIN:MARGIN + LANES]
    into_edge = np.concatenate([forward_x[:MARGIN], forward_x[MARGIN + LANES:]])
    out = np.zeros((WIDE, WIDE))
    out[:, :LANES] = backward_x[:, MARGIN:MARGIN + LANES]
    out[:, edge] = np.concatenate([backward_x[:, :MARGIN], backward_x[:, MARGIN + LANES:]], axis=1)
    rest = count * LENGTH - LANES
    eigen_x = np.zeros((1, WIDE))
    eigen_x[0, : count * LENGTH] = np.tile(eigen, count)
    eigen_lanes = np.broadcast_to(eigen[:, None], (LENGTH, WIDE))

    def high(matrix):
        return matrix.astype(np.float32).astype(BF16).astype(np.float64)

    def low(matrix):
        return matrix - high(matrix)

    def pair(matrix):
        zero = np.zeros((LENGTH, LENGTH))
        both = np.block([[matrix, zero], [zero, matrix]])
        return np.concatenate([high(both), high(both), low(both)], axis=1)

    def tall(*parts):
        blank = np.zeros((2 * LANES - sum(p.shape[0] for p in parts), WIDE))
        return np.concatenate(parts + (blank,))

    head, tail = out[:LANES], out[LANES:LANES + rest]
    return [m.astype(BF16) for m in (
        pair(forward),
        pair(backward),
        tall(high(into), high(into)),
        tall(low(into), high(into_edge), high(into_edge), low(into_edge)),
        tall(high(head), high(head)),
        tall(low(head), high(tail), high(tail), low(tail)),
    )] + [eigen_x.astype(np.float32), np.ascontiguousarray(eigen_lanes).astype(np.float32)]


def dot(a, b):
    return jnp.dot(a, b, preferred_element_type=F32)


def triple(values):
    high, low = halves(values)
    return jnp.concatenate([high, low, high], axis=0)


def kernel(
    load_in, labels_in, mask_in, table_in, *rest,
):
    tables = rest[:TABLES]
    (
        disp, resid, modulus, faces, w, xs, xr, b1a, b1b, b2a, b2b, zb, fs, fr, zr, ys, yr, corr, rinv,
        cys, cyr, czs, czr, cxs, cxr, send_sem, recv_sem, in_sem,
        load, labels, mask, table, fwd, bwd, into_1, into_2, out_1, out_2, eigen_x, eigen_rows,
    ) = rest[TABLES:]
    index = {a: lax.axis_index(a) for a in ("gx", "gy", "gz")}
    count = {a: lax.axis_size(a) for a in ("gx", "gy", "gz")}
    lower = {a: lax.rem(index[a] + count[a] - 1, count[a]) for a in index}
    upper = {a: lax.rem(index[a] + 1, count[a]) for a in index}
    has_lower = {a: index[a] > 0 for a in index}
    has_upper = {a: index[a] < count[a] - 1 for a in index}

    barrier = pltpu.get_barrier_semaphore()
    for a in ("gx", "gy", "gz"):
        pl.semaphore_signal(barrier, inc=1, device_id={a: lower[a]}, device_id_type=MESH)
        pl.semaphore_signal(barrier, inc=1, device_id={a: upper[a]}, device_id_type=MESH)

    sources = (load_in, labels_in, mask_in, table_in, *tables)
    targets = (load, labels, mask, table, fwd, bwd, into_1, into_2, out_1, out_2, eigen_x, eigen_rows)
    fetched = [
        pltpu.make_async_copy(source, target, in_sem.at[number])
        for number, (source, target) in enumerate(zip(sources, targets))
    ]
    for copy in fetched:
        copy.start()

    def copies(slot, phase, down, up):
        a = AXIS[phase]
        made = []
        for side, (source, target), device in ((0, down, lower[a]), (1, up, upper[a])):
            number = (slot * PHASES + phase) * 2 + side
            made.append(pltpu.make_async_remote_copy(
                src_ref=source, dst_ref=target,
                send_sem=send_sem.at[number], recv_sem=recv_sem.at[number],
                device_id={a: device}, device_id_type=MESH,
            ))
        return made

    pending = {}

    def send(slot, phase, down, up):
        made = copies(slot, phase, down, up)
        for copy, there in zip(made, (has_lower, has_upper)):
            pl.when(there[AXIS[phase]])(copy.start)
        pending[slot, phase] = made

    def arrive(slot, phase):
        for copy, there in zip(pending[slot, phase], (has_upper, has_lower)):
            pl.when(there[AXIS[phase]])(copy.wait_recv)

    def flat(ref, slot):
        return ref.at[slot].reshape(PLANES * LENGTH, LANES)

    def keep(flag, values):
        return jnp.where(flag, values, 0.0)

    lanes = lax.broadcasted_iota(jnp.int32, (LANES, LANES), 1)

    def face_columns(values):
        flat = values.reshape(BRICK * BRICK, LANES)
        total = jnp.zeros((LANES, LANES), F32)
        for i in range(8):
            part = pltpu.roll(flat[i * LANES:(i + 1) * LANES], 2 * i + 1, 1)
            total = jnp.where((lanes == 2 * i) | (lanes == 2 * i + 1), part, total)
        return jnp.transpose(total)[:16]

    def y_pack(slot, values):
        cys[slot, 0] = values[:, 0, :]
        cys[slot, 1] = values[:, BRICK - 1, :]

    def y_send(slot):
        send(slot, CY, (cys.at[slot, 0], cyr.at[slot, 1]), (cys.at[slot, 1], cyr.at[slot, 0]))

    def xz_pack(slot, values):
        czs[slot, 0] = values[0]
        czs[slot, 1] = values[BRICK - 1]
        cxs[slot] = face_columns(values)

    def xz_send(slot):
        send(slot, CZ, (czs.at[slot, 0], czr.at[slot, 1]), (czs.at[slot, 1], czr.at[slot, 0]))
        send(slot, CX, (cxs.at[slot], cxr.at[slot, 1]), (cxs.at[slot], cxr.at[slot, 0]))

    def halo_get(slot, low_y, high_y):
        for phase in (CZ, CX):
            arrive(slot, phase)
        low_z = keep(has_lower["gz"], czr[slot, 0])
        high_z = keep(has_upper["gz"], czr[slot, 1])
        left = keep(has_lower["gx"], cxr[slot, 0])
        right = keep(has_upper["gx"], cxr[slot, 1])
        odd = lax.rem(lax.broadcasted_iota(jnp.int32, (16, LANES), 0), 2) == 1
        both = jnp.where(odd, pltpu.roll(left, 1, 0), pltpu.roll(right, 15, 0))
        side = jnp.transpose(jnp.concatenate([both, jnp.zeros((LANES - 16, LANES), F32)], axis=0))
        side = jnp.concatenate(
            [pltpu.roll(side, LANES - 1 - 2 * i, 1) for i in range(8)], axis=0
        ).reshape(BRICK, BRICK, LANES)
        return low_y, high_y, low_z, high_z, side

    def shifts(values, halo):
        low_y, high_y, low_z, high_z, side = halo
        lane = lax.broadcasted_iota(jnp.int32, values.shape, 2)
        yield jnp.concatenate([low_z[None], values[:-1]], axis=0)
        yield jnp.concatenate([values[1:], high_z[None]], axis=0)
        yield jnp.concatenate([low_y[:, None, :], values[:, :-1]], axis=1)
        yield jnp.concatenate([values[:, 1:], high_y[:, None, :]], axis=1)
        yield jnp.where(lane == 0, side, pltpu.roll(values, 1, 2))
        yield jnp.where(lane == LANES - 1, side, pltpu.roll(values, LANES - 1, 2))

    def a_pack(s, c):
        slot = s * 3 + c
        if s == 0:
            values = load[c]
            w[slot, 0:BRICK, 0:BRICK, :] = values
        else:
            values = w[slot, 0:BRICK, 0:BRICK, :]
        ys[slot, 0] = values[:, 0:MARGIN, :]
        ys[slot, 1] = values[:, BRICK - MARGIN:BRICK, :]

    def z_planes(ref, slot, rows):
        def at(first):
            return ref.at[slot, pl.ds(first, MARGIN), rows]

        return (at(0), at(BRICK + MARGIN)), (at(BRICK - MARGIN), at(BRICK))

    def a_send(s, c):
        slot = s * 3 + c
        send(slot, AY, (ys.at[slot, 0], yr.at[slot, 1]), (ys.at[slot, 1], yr.at[slot, 0]))
        send(slot, AZ, *z_planes(w, slot, pl.ds(0, BRICK)))

    def a_z(s, c):
        slot = s * 3 + c
        arrive(slot, AY)
        low = keep(has_lower["gy"], yr[slot, 0])
        high = keep(has_upper["gy"], yr[slot, 1])
        w[slot, 0:BRICK, BRICK:LENGTH, :] = jnp.concatenate([low, high], axis=1)
        send(slot, AE, *z_planes(w, slot, pl.ds(BRICK, 2 * MARGIN)))

    def a_x(s, c):
        slot = s * 3 + c
        arrive(slot, AZ)
        arrive(slot, AE)
        low = w[slot, BRICK:BRICK + MARGIN]
        w[slot, BRICK:BRICK + MARGIN] = keep(has_lower["gz"], low)
        high = w[slot, BRICK + MARGIN:LENGTH]
        w[slot, BRICK + MARGIN:LENGTH] = keep(has_upper["gz"], high)
        rows = flat(w, slot)
        total = jnp.zeros((LANES, LANES), F32)
        for i in range(CHUNKS):
            part = pltpu.roll(rows[i * LANES:(i + 1) * LANES, :], 8 * i + MARGIN, 1)
            total = jnp.where((lanes >= 8 * i) & (lanes < 8 * i + 8), part, total)
        total = jnp.transpose(total)[:CHUNKS * 8].reshape(CHUNKS, 8, LANES)
        xs[slot, 0] = total[:, MARGIN:]
        xs[slot, 1] = total[:, :MARGIN]
        send(slot, AX, (xs.at[slot, 0], xr.at[slot, 1]), (xs.at[slot, 1], xr.at[slot, 0]))

    one, two = (b1a, b1b), (b2a, b2b)

    def transform(matrix, source, target, strided, scale=None):
        def body(i, carry):
            outs = []
            for k in range(UNROLL):
                at = pl.ds(pl.multiple_of((i * UNROLL + k) * 2 * LENGTH, 8), 2 * LENGTH)
                values = jnp.concatenate([source[0][at, :], source[1][at, :]], axis=1)
                outs.append(dot(matrix[...], triple(values)))
            for k in range(UNROLL):
                at = pl.ds(pl.multiple_of((i * UNROLL + k) * 2 * LENGTH, 8), 2 * LENGTH)
                out = outs[k]
                if scale is not None:
                    out = out * scale[at, :]
                for half in range(2):
                    part = out[:, half * LANES:(half + 1) * LANES]
                    if strided:
                        for which in range(2):
                            spot = pl.ds((i * UNROLL + k) * 2 + which, LENGTH, stride=LENGTH)
                            target[half][spot, :] = part[which * LENGTH:(which + 1) * LENGTH]
                    else:
                        target[half][at, :] = part
            return carry

        lax.fori_loop(0, LENGTH // 2 // UNROLL, body, 0)

    def s1(s, c):
        slot = s * 3 + c
        arrive(slot, AX)

        rows = flat(w, slot)
        near = jnp.concatenate([keep(has_lower["gx"], xr[slot, 0]), keep(has_upper["gx"], xr[slot, 1])], axis=1)
        high = near.astype(BF16).astype(F32)
        near = jnp.concatenate([high, near - high, high], axis=1)
        sides = []
        for first in range(0, CHUNKS, 5):
            group = near[first:first + 5].reshape(-1, LANES)
            blank = jnp.zeros((LANES - group.shape[0], LANES), F32)
            sides.append(jnp.transpose(jnp.concatenate([group, blank], axis=0)))
        for i in range(CHUNKS):
            at = pl.ds(i * LANES, LANES)
            side = sides[i // 5]
            if i % 5:
                side = pltpu.roll(side, LANES - 24 * (i % 5), 1)
            high, low = halves(rows[at, :])
            out = dot(jnp.concatenate([high, low], axis=1), into_1[...])
            out += dot(jnp.concatenate([high, side.astype(BF16)], axis=1), into_2[...])
            b1a[at, :] = out[:, :LANES]
            b1b[at, :] = out[:, LANES:]

        transform(fwd, one, two, True)

    def s2(s, c):
        transform(fwd, two, one, False, rinv.at[c])
        transform(bwd, one, two, True)

    def s3(s, c):
        slot = s * 3 + c
        transform(bwd, two, one, False)

        rows = flat(zb, slot)
        margin = jnp.zeros((LANES, LANES), F32)
        for i in range(CHUNKS):
            at = pl.ds(i * LANES, LANES)
            high, low = halves(b1a[at, :])
            tail = b1b[at, :]
            tail_high = tail.astype(BF16).astype(F32)
            packed = tail_high + pltpu.roll(tail - tail_high, 32, 1) + pltpu.roll(tail_high, 64, 1)
            out = dot(jnp.concatenate([high, low], axis=1), out_1[...])
            out += dot(jnp.concatenate([high, packed.astype(BF16)], axis=1), out_2[...])
            rows[at, :] = out[:, :LANES]
            part = out[:, LANES:]
            margin += pltpu.roll(part, 8 * i, 1) if i else part
        margin = jnp.transpose(margin)[:CHUNKS * 8].reshape(CHUNKS, 8, LANES)
        fs[slot, 0] = margin[:, :MARGIN]
        fs[slot, 1] = margin[:, MARGIN:]
        send(slot, BX, (fs.at[slot, 0], fr.at[slot, 1]), (fs.at[slot, 1], fr.at[slot, 0]))

    def b_z(s, c):
        slot = s * 3 + c
        arrive(slot, BX)

        near = jnp.concatenate([keep(has_upper["gx"], fr[slot, 1]), keep(has_lower["gx"], fr[slot, 0])], axis=1)
        blank = jnp.zeros((LANES - CHUNKS * 8, LANES), F32)
        side = jnp.transpose(jnp.concatenate([near.reshape(CHUNKS * 8, LANES), blank], axis=0))
        rows = flat(zb, slot)
        edge = (lanes < MARGIN) | (lanes >= LANES - MARGIN)
        for i in range(CHUNKS):
            at = pl.ds(i * LANES, LANES)
            rows[at, :] += jnp.where(edge, pltpu.roll(side, LANES - 8 * i - MARGIN, 1), 0.0)

        send(
            slot, BZ,
            (zb.at[slot, pl.ds(BRICK, MARGIN)], zr.at[slot, 1]),
            (zb.at[slot, pl.ds(BRICK + MARGIN, MARGIN)], zr.at[slot, 0]),
        )

    def b_y(s, c):
        slot = s * 3 + c
        arrive(slot, BZ)
        zb[slot, 0:MARGIN] += keep(has_lower["gz"], zr[slot, 0])
        zb[slot, BRICK - MARGIN:BRICK] += keep(has_upper["gz"], zr[slot, 1])
        other = slot + 3 * SWEEPS
        rows = zb[slot, 0:BRICK, BRICK:LENGTH, :]
        ys[other, 0] = rows[:, :MARGIN]
        ys[other, 1] = rows[:, MARGIN:]
        y_pack(slot, zb[slot, 0:BRICK, 0:BRICK, :])
        send(slot, BY, (ys.at[other, 0], yr.at[other, 1]), (ys.at[other, 1], yr.at[other, 0]))
        y_send(slot)

    def c_start(s, c):
        slot = s * 3 + c
        arrive(slot, BY)
        other = slot + 3 * SWEEPS
        low = keep(has_lower["gy"], yr[other, 0])
        high = keep(has_upper["gy"], yr[other, 1])
        own = zb[slot, 0:BRICK, 0:BRICK, :]
        blank = jnp.zeros((BRICK, MARGIN, LANES), F32)
        own = jnp.concatenate([
            own[:, :8] + jnp.concatenate([low, blank], axis=1),
            own[:, 8:24],
            own[:, 24:] + jnp.concatenate([blank, high], axis=1),
        ], axis=1)
        corr[slot] = own
        xz_pack(slot, own)
        xz_send(slot)
        if s == SWEEPS - 1:
            total = own
            for before in range(s):
                total = corr[before * 3 + c] + total
            disp[c] = total

    def update(s, c):
        slot = s * 3 + c
        arrive(slot, CY)
        margins = zb[slot, 0:BRICK, BRICK:LENGTH, :]
        halo = halo_get(
            slot,
            keep(has_lower["gy"], cyr[slot, 0] + margins[:, MARGIN - 1, :]),
            keep(has_upper["gy"], cyr[slot, 1] + margins[:, MARGIN, :]),
        )
        values = corr[slot]
        total = SIGMA_SHIFT * modulus[...] * values
        for number, moved in enumerate(shifts(values, halo)):
            total = total + (ratio(c, number // 2) * 0.5) * faces[number] * (values - moved)
        if s == SWEEPS - 1:
            resid[c] = w[slot, 0:BRICK, 0:BRICK, :] - total
        else:
            w[slot + 3, 0:BRICK, 0:BRICK, :] = w[slot, 0:BRICK, 0:BRICK, :] - total
            a_pack(s + 1, c)
            a_send(s + 1, c)

    def stiff(s, c):
        arrive(6, CY)
        own = modulus[...]
        low, high = keep(has_lower["gy"], cyr[6, 0]), keep(has_upper["gy"], cyr[6, 1])
        for number, moved in enumerate(shifts(own, halo_get(6, low, high))):
            faces[number] = own + moved

    fetched[0].wait()
    for c in range(3):
        a_pack(0, c)
    for slot in range(6):
        w[slot, LENGTH:] = jnp.zeros((PLANES - LENGTH, LENGTH, LANES), F32)

    for copy in fetched[1:]:
        copy.wait()

    def look(z, carry):
        picked = labels[z]
        value = jnp.zeros(picked.shape, F32)
        for number in range(table.shape[0]):
            value = jnp.where(picked == number, table[number], value)
        modulus[z] = jnp.where(mask[z] == 1, value, VOID_MODULUS)
        return carry

    lax.fori_loop(0, BRICK, look, 0)
    y_pack(6, modulus[...])
    xz_pack(6, modulus[...])

    for c in range(3):
        def invert(y, carry, c=c):
            at = pl.ds(pl.multiple_of(y * LENGTH, 8), LENGTH)
            rinv[c, at, :] = 1.0 / (REF_MODULUS * (
                ratio(c, 0) * eigen_rows[...]
                + ratio(c, 1) * eigen_rows[pl.ds(y, 1), :]
                + ratio(c, 2) * eigen_x[...]
                + SIGMA_SHIFT
            ))
            return carry

        lax.fori_loop(0, LENGTH, invert, 0)

    pl.semaphore_wait(barrier, 6)
    for c in range(3):
        a_send(0, c)
    y_send(6)
    xz_send(6)

    stages = dict(a_z=a_z, a_x=a_x, s1=s1, s2=s2, s3=s3, b_z=b_z, b_y=b_y, c_start=c_start, update=update,
                  stiff=stiff)
    for s, c, name in ORDER:
        stages[name](s, c)

    for (_, phase), made in pending.items():
        for copy, there in zip(made, (has_lower, has_upper)):
            pl.when(there[AXIS[phase]])(copy.wait_send)


def local(load, labels, mask, table):
    tables = constants()
    vmem = pl.BlockSpec(memory_space=pltpu.VMEM)
    hbm = pl.BlockSpec(memory_space=pltpu.HBM)
    slots = 3 * SWEEPS
    field = jax.ShapeDtypeStruct(load.shape, F32)
    block = (BRICK, BRICK, LANES)
    return pl.pallas_call(
        kernel,
        out_shape=(field, field),
        in_specs=[hbm] * (4 + len(tables)),
        out_specs=(vmem, vmem),
        scratch_shapes=[
            pltpu.VMEM(block, F32),
            pltpu.VMEM((6,) + block, F32),
            pltpu.VMEM((slots, PLANES, LENGTH, LANES), F32),
            pltpu.VMEM((slots, 2, CHUNKS, MARGIN, LANES), F32),
            pltpu.VMEM((slots, 2, CHUNKS, MARGIN, LANES), F32),
            pltpu.VMEM((PADDED, LANES), F32),
            pltpu.VMEM((PADDED, LANES), F32),
            pltpu.VMEM((PADDED, LANES), F32),
            pltpu.VMEM((PADDED, LANES), F32),
            pltpu.VMEM((slots, PLANES, LENGTH, LANES), F32),
            pltpu.VMEM((slots, 2, CHUNKS, MARGIN, LANES), F32),
            pltpu.VMEM((slots, 2, CHUNKS, MARGIN, LANES), F32),
            pltpu.VMEM((slots, 2, MARGIN, LENGTH, LANES), F32),
            pltpu.VMEM((2 * slots, 2, BRICK, MARGIN, LANES), F32),
            pltpu.VMEM((2 * slots, 2, BRICK, MARGIN, LANES), F32),
            pltpu.VMEM((slots,) + block, F32),
            pltpu.VMEM((3, ROWS, WIDE), F32),
            pltpu.VMEM((slots + 1, 2, BRICK, LANES), F32),
            pltpu.VMEM((slots + 1, 2, BRICK, LANES), F32),
            pltpu.VMEM((slots + 1, 2, BRICK, LANES), F32),
            pltpu.VMEM((slots + 1, 2, BRICK, LANES), F32),
            pltpu.VMEM((slots + 1, 16, LANES), F32),
            pltpu.VMEM((slots + 1, 2, 16, LANES), F32),
            pltpu.SemaphoreType.DMA(((slots + 1) * PHASES * 2,)),
            pltpu.SemaphoreType.DMA(((slots + 1) * PHASES * 2,)),
            pltpu.SemaphoreType.DMA((4 + len(tables),)),
            pltpu.VMEM(load.shape, F32),
            pltpu.VMEM(block, jnp.int32),
            pltpu.VMEM(block, jnp.int32),
            pltpu.SMEM(table.shape, F32),
        ] + [pltpu.VMEM(t.shape, t.dtype) for t in tables] + [
        ],
        compiler_params=pltpu.CompilerParams(
            collective_id=0, has_side_effects=True, vmem_limit_bytes=44 * 1024 * 1024
        ),
    )(*(pltpu.with_memory_space_constraint(v, pltpu.HBM) for v in (load, labels, mask, table, *map(jnp.asarray, tables))))


def solution(mesh):
    placed = (P(None, "gz", "gy", "gx"), P("gz", "gy", "gx"), P("gz", "gy", "gx"), P())
    return jax.shard_map(
        local,
        mesh=mesh,
        in_specs=placed,
        out_specs=(P(None, "gz", "gy", "gx"), P(None, "gz", "gy", "gx")),
        check_vma=False,
    )
```

```python
import jax
import jax.numpy as jnp
import numpy as np
from jax import lax
from jax.experimental import pallas as pl
from jax.experimental.pallas import tpu as pltpu
from jax.sharding import PartitionSpec as P

BRICK = 32
MARGIN = 4
SWEEPS = 2
LENGTH = BRICK + 2 * MARGIN
LANES = 128
WIDE = 256
ROWS = LENGTH * LENGTH
PADDED = 1664
CHUNKS = PADDED // LANES
OWNED = BRICK * LENGTH
LAMBDA_RATIO = 2.0
SIGMA_SHIFT = 0.1
REF_MODULUS = 1.5
VOID_MODULUS = 0.1
MESH = pl.DeviceIdType.MESH
UNROLL = 10
GROUPS = ((0, 4), (4, 8), (8, 13))
PHASES = 10
AY, AZ, AE, AX, BX, BZ, BY, CY, CZ, CX = range(PHASES)
AXIS = ("gy", "gz", "gz", "gx", "gx", "gz", "gy", "gy", "gz", "gx")
PLANES = 42
TABLES = 6
ORDER = (
    (0, 0, "a_z"), (0, 1, "a_z"), (0, 0, "a_x"), (0, 2, "a_z"), (0, 1, "a_x"), (0, 0, "s1"), (0, 0, "s2"),
    (0, 0, "s3"), (0, 1, "s1"), (0, 2, "a_x"), (0, 1, "s2"), (0, 1, "s3"), (0, 0, "stiff"), (0, 0, "b_z"),
    (0, 2, "s1"), (0, 2, "s2"), (0, 1, "b_z"), (0, 2, "s3"), (0, 0, "b_y"), (0, 2, "b_z"), (0, 1, "b_y"),
    (0, 0, "c_start"), (0, 2, "b_y"), (0, 1, "c_start"), (0, 0, "update"), (0, 1, "update"), (1, 0, "a_z"),
    (0, 2, "c_start"), (1, 1, "a_z"), (1, 0, "a_x"), (0, 2, "update"), (1, 1, "a_x"), (1, 0, "s1"), (1, 0, "s2"),
    (1, 0, "s3"), (1, 2, "a_z"), (1, 1, "s1"), (1, 1, "s2"), (1, 2, "a_x"), (1, 0, "b_z"), (1, 1, "s3"),
    (1, 2, "s1"), (1, 2, "s2"), (1, 1, "b_z"), (1, 2, "s3"), (1, 0, "b_y"), (1, 2, "b_z"), (1, 1, "b_y"),
    (1, 2, "b_y"), (1, 0, "c_start"), (1, 1, "c_start"), (1, 2, "c_start"), (1, 1, "update"), (1, 0, "update"),
    (1, 2, "update"),
)
F32 = jnp.float32
BF16 = jnp.bfloat16


def ratio(component, direction):
    return LAMBDA_RATIO if component == direction else 1.0


def halves(values):
    high = values.astype(BF16)
    return high, (values - high.astype(F32)).astype(BF16)


def constants():
    grid = np.arange(1, LENGTH + 1, dtype=np.float64)
    sine = np.sqrt(2.0 / (LENGTH + 1)) * np.sin(np.pi * grid[:, None] * grid[None, :] / (LENGTH + 1))
    eigen = 2.0 - 2.0 * np.cos(np.pi * grid / (LENGTH + 1))
    spot = np.arange(LENGTH, dtype=np.float64)
    ramp = np.minimum(np.minimum((spot + 0.5) / (2 * MARGIN), (LENGTH - 0.5 - spot) / (2 * MARGIN)), 1.0)
    ramped = ramp[:, None] * sine
    place = np.concatenate([np.arange(MARGIN, MARGIN + BRICK), np.arange(MARGIN), np.arange(MARGIN + BRICK, LENGTH)])
    forward = ramped[place].T
    backward = sine.T[place]
    count = LANES // BRICK
    wide_x = LANES + 2 * MARGIN
    forward_x = np.zeros((wide_x, WIDE))
    backward_x = np.zeros((WIDE, wide_x))
    for brick in range(count):
        rows = slice(brick * BRICK, brick * BRICK + LENGTH)
        columns = slice(brick * LENGTH, (brick + 1) * LENGTH)
        forward_x[rows, columns] = ramped
        backward_x[columns, rows] = sine
    edge = slice(LANES, LANES + 2 * MARGIN)
    into = forward_x[MARGIN:MARGIN + LANES]
    into_edge = np.concatenate([forward_x[:MARGIN], forward_x[MARGIN + LANES:]])
    out = np.zeros((WIDE, WIDE))
    out[:, :LANES] = backward_x[:, MARGIN:MARGIN + LANES]
    out[:, edge] = np.concatenate([backward_x[:, :MARGIN], backward_x[:, MARGIN + LANES:]], axis=1)
    rest = count * LENGTH - LANES
    eigen_x = np.zeros((1, WIDE))
    eigen_x[0, : count * LENGTH] = np.tile(eigen, count)
    eigen_lanes = np.broadcast_to(eigen[:, None], (LENGTH, WIDE))

    def high(matrix):
        return matrix.astype(np.float32).astype(BF16).astype(np.float64)

    def low(matrix):
        return matrix - high(matrix)

    def pair(matrix):
        zero = np.zeros((LENGTH, LENGTH))
        both = np.block([[matrix, zero], [zero, matrix]])
        return np.concatenate([high(both), high(both), low(both)], axis=1)

    def tall(*parts):
        blank = np.zeros((4 * LANES - sum(p.shape[0] for p in parts), WIDE))
        return np.concatenate(parts + (blank,))

    head, tail = out[:LANES], out[LANES:LANES + rest]
    return [m.astype(BF16) for m in (
        pair(forward),
        pair(backward),
        tall(high(into), high(into), low(into), high(into_edge), high(into_edge), low(into_edge)),
        tall(high(head), high(head), low(head), high(tail), high(tail), low(tail)),
    )] + [eigen_x.astype(np.float32), np.ascontiguousarray(eigen_lanes).astype(np.float32)]


def dot(a, b):
    return jnp.dot(a, b, preferred_element_type=F32)


def triple(values):
    high, low = halves(values)
    return jnp.concatenate([high, low, high], axis=0)


def kernel(
    load_in, labels_in, mask_in, table_in, *rest,
):
    tables = rest[:TABLES]
    (
        disp, resid, modulus, faces, centre, w, xs, xr, b1a, b1b, b2a, b2b, zb, fs, fr, zr, ys, yr, corr, rinv,
        cys, cyr, czs, czr, cxs, cxr, send_sem, recv_sem, in_sem,
        load, labels, mask, table, fwd, bwd, into, out_of, eigen_x, eigen_rows,
    ) = rest[TABLES:]
    index = {a: lax.axis_index(a) for a in ("gx", "gy", "gz")}
    count = {a: lax.axis_size(a) for a in ("gx", "gy", "gz")}
    lower = {a: lax.rem(index[a] + count[a] - 1, count[a]) for a in index}
    upper = {a: lax.rem(index[a] + 1, count[a]) for a in index}
    has_lower = {a: index[a] > 0 for a in index}
    has_upper = {a: index[a] < count[a] - 1 for a in index}

    barrier = pltpu.get_barrier_semaphore()
    for a in ("gx", "gy", "gz"):
        pl.semaphore_signal(barrier, inc=1, device_id={a: lower[a]}, device_id_type=MESH)
        pl.semaphore_signal(barrier, inc=1, device_id={a: upper[a]}, device_id_type=MESH)

    sources = (load_in, labels_in, mask_in, table_in, *tables)
    targets = (load, labels, mask, table, fwd, bwd, into, out_of, eigen_x, eigen_rows)
    fetched = [
        pltpu.make_async_copy(source, target, in_sem.at[number])
        for number, (source, target) in enumerate(zip(sources, targets))
    ]
    for copy in fetched:
        copy.start()

    def copies(slot, phase, down, up):
        a = AXIS[phase]
        made = []
        for side, (source, target), device in ((0, down, lower[a]), (1, up, upper[a])):
            number = (slot * PHASES + phase) * 2 + side
            made.append(pltpu.make_async_remote_copy(
                src_ref=source, dst_ref=target,
                send_sem=send_sem.at[number], recv_sem=recv_sem.at[number],
                device_id={a: device}, device_id_type=MESH,
            ))
        return made

    pending = {}

    def send(slot, phase, down, up):
        made = copies(slot, phase, down, up)
        for copy, there in zip(made, (has_lower, has_upper)):
            pl.when(there[AXIS[phase]])(copy.start)
        pending[slot, phase] = made

    def arrive(slot, phase):
        for copy, there in zip(pending[slot, phase], (has_upper, has_lower)):
            pl.when(there[AXIS[phase]])(copy.wait_recv)

    def flat(ref, slot):
        return ref.at[slot].reshape(PLANES * LENGTH, LANES)

    def keep(flag, values):
        return jnp.where(flag, values, 0.0)

    lanes = lax.broadcasted_iota(jnp.int32, (LANES, LANES), 1)

    def face_columns(values):
        flat = values.reshape(BRICK * BRICK, LANES)
        total = jnp.zeros((LANES, LANES), F32)
        for i in range(8):
            part = pltpu.roll(flat[i * LANES:(i + 1) * LANES], 2 * i + 1, 1)
            total = jnp.where((lanes == 2 * i) | (lanes == 2 * i + 1), part, total)
        return jnp.transpose(total)[:16]

    def y_pack(slot, values):
        cys[slot, 0] = values[:, 0, :]
        cys[slot, 1] = values[:, BRICK - 1, :]

    def y_send(slot):
        send(slot, CY, (cys.at[slot, 0], cyr.at[slot, 1]), (cys.at[slot, 1], cyr.at[slot, 0]))

    def xz_pack(slot, values):
        czs[slot, 0] = values[0]
        czs[slot, 1] = values[BRICK - 1]
        cxs[slot] = face_columns(values)

    def xz_send(slot):
        send(slot, CZ, (czs.at[slot, 0], czr.at[slot, 1]), (czs.at[slot, 1], czr.at[slot, 0]))
        send(slot, CX, (cxs.at[slot], cxr.at[slot, 1]), (cxs.at[slot], cxr.at[slot, 0]))

    def halo_get(slot, low_y, high_y):
        for phase in (CZ, CX):
            arrive(slot, phase)
        low_z = keep(has_lower["gz"], czr[slot, 0])
        high_z = keep(has_upper["gz"], czr[slot, 1])
        left = keep(has_lower["gx"], cxr[slot, 0])
        right = keep(has_upper["gx"], cxr[slot, 1])
        odd = lax.rem(lax.broadcasted_iota(jnp.int32, (16, LANES), 0), 2) == 1
        both = jnp.where(odd, pltpu.roll(left, 1, 0), pltpu.roll(right, 15, 0))
        side = jnp.transpose(jnp.concatenate([both, jnp.zeros((LANES - 16, LANES), F32)], axis=0))
        side = jnp.concatenate(
            [pltpu.roll(side, LANES - 1 - 2 * i, 1) for i in range(8)], axis=0
        ).reshape(BRICK, BRICK, LANES)
        return low_y, high_y, low_z, high_z, side

    def shifts(values, halo):
        low_y, high_y, low_z, high_z, side = halo
        lane = lax.broadcasted_iota(jnp.int32, values.shape, 2)
        yield jnp.concatenate([low_z[None], values[:-1]], axis=0)
        yield jnp.concatenate([values[1:], high_z[None]], axis=0)
        yield jnp.concatenate([low_y[:, None, :], values[:, :-1]], axis=1)
        yield jnp.concatenate([values[:, 1:], high_y[:, None, :]], axis=1)
        yield jnp.where(lane == 0, side, pltpu.roll(values, 1, 2))
        yield jnp.where(lane == LANES - 1, side, pltpu.roll(values, LANES - 1, 2))

    def a_pack(s, c):
        slot = s * 3 + c
        if s == 0:
            values = load[c]
            w[slot, 0:BRICK, 0:BRICK, :] = values
        else:
            values = w[slot, 0:BRICK, 0:BRICK, :]
        ys[slot, 0] = values[:, 0:MARGIN, :]
        ys[slot, 1] = values[:, BRICK - MARGIN:BRICK, :]

    def z_planes(ref, slot, rows):
        def at(first):
            return ref.at[slot, pl.ds(first, MARGIN), rows]

        return (at(0), at(BRICK + MARGIN)), (at(BRICK - MARGIN), at(BRICK))

    def a_send(s, c):
        slot = s * 3 + c
        send(slot, AY, (ys.at[slot, 0], yr.at[slot, 1]), (ys.at[slot, 1], yr.at[slot, 0]))
        send(slot, AZ, *z_planes(w, slot, pl.ds(0, BRICK)))

    def a_z(s, c):
        slot = s * 3 + c
        arrive(slot, AY)
        low = keep(has_lower["gy"], yr[slot, 0])
        high = keep(has_upper["gy"], yr[slot, 1])
        w[slot, 0:BRICK, BRICK:LENGTH, :] = jnp.concatenate([low, high], axis=1)
        send(slot, AE, *z_planes(w, slot, pl.ds(BRICK, 2 * MARGIN)))

    def a_x(s, c):
        slot = s * 3 + c
        arrive(slot, AZ)
        arrive(slot, AE)
        low = w[slot, BRICK:BRICK + MARGIN]
        w[slot, BRICK:BRICK + MARGIN] = keep(has_lower["gz"], low)
        high = w[slot, BRICK + MARGIN:LENGTH]
        w[slot, BRICK + MARGIN:LENGTH] = keep(has_upper["gz"], high)
        rows = flat(w, slot)
        total = jnp.zeros((LANES, LANES), F32)
        for i in range(CHUNKS):
            part = pltpu.roll(rows[i * LANES:(i + 1) * LANES, :], 8 * i + MARGIN, 1)
            total = jnp.where((lanes >= 8 * i) & (lanes < 8 * i + 8), part, total)
        total = jnp.transpose(total)[:CHUNKS * 8].reshape(CHUNKS, 8, LANES)
        xs[slot, 0] = total[:, MARGIN:]
        xs[slot, 1] = total[:, :MARGIN]
        send(slot, AX, (xs.at[slot, 0], xr.at[slot, 1]), (xs.at[slot, 1], xr.at[slot, 0]))

    one, two = (b1a, b1b), (b2a, b2b)

    def transform(matrix, source, target, strided, scale=None):
        def body(i, carry):
            outs = []
            for k in range(UNROLL):
                at = pl.ds(pl.multiple_of((i * UNROLL + k) * 2 * LENGTH, 8), 2 * LENGTH)
                values = jnp.concatenate([source[0][at, :], source[1][at, :]], axis=1)
                outs.append(dot(matrix[...], triple(values)))
            for k in range(UNROLL):
                at = pl.ds(pl.multiple_of((i * UNROLL + k) * 2 * LENGTH, 8), 2 * LENGTH)
                out = outs[k]
                if scale is not None:
                    out = out * scale[at, :]
                for half in range(2):
                    part = out[:, half * LANES:(half + 1) * LANES]
                    if strided:
                        for which in range(2):
                            spot = pl.ds((i * UNROLL + k) * 2 + which, LENGTH, stride=LENGTH)
                            target[half][spot, :] = part[which * LENGTH:(which + 1) * LENGTH]
                    else:
                        target[half][at, :] = part
            return carry

        lax.fori_loop(0, LENGTH // 2 // UNROLL, body, 0)

    def s1(s, c):
        slot = s * 3 + c
        arrive(slot, AX)

        rows = flat(w, slot)
        near = jnp.concatenate([keep(has_lower["gx"], xr[slot, 0]), keep(has_upper["gx"], xr[slot, 1])], axis=1)
        high = near.astype(BF16).astype(F32)
        near = jnp.concatenate([high, near - high, high], axis=1)
        sides = []
        for first in range(0, CHUNKS, 5):
            group = near[first:first + 5].reshape(-1, LANES)
            blank = jnp.zeros((LANES - group.shape[0], LANES), F32)
            sides.append(jnp.transpose(jnp.concatenate([group, blank], axis=0)))
        for first, last in GROUPS:
            parts = []
            for i in range(first, last):
                side = sides[i // 5]
                if i % 5:
                    side = pltpu.roll(side, LANES - 24 * (i % 5), 1)
                high, low = halves(rows[i * LANES:(i + 1) * LANES, :])
                parts.append(jnp.concatenate([high, low, high, side.astype(BF16)], axis=1))
            out = dot(jnp.concatenate(parts, axis=0), into[...])
            b1a[first * LANES:last * LANES, :] = out[:, :LANES]
            b1b[first * LANES:last * LANES, :] = out[:, LANES:]

        transform(fwd, one, two, True)

    def s2(s, c):
        transform(fwd, two, one, False, rinv.at[c])
        transform(bwd, one, two, True)

    def s3(s, c):
        slot = s * 3 + c
        transform(bwd, two, one, False)

        rows = flat(zb, slot)
        margin = jnp.zeros((LANES, LANES), F32)
        for first, last in GROUPS:
            parts = []
            for i in range(first, last):
                at = pl.ds(i * LANES, LANES)
                high, low = halves(b1a[at, :])
                tail = b1b[at, :]
                tail_high = tail.astype(BF16).astype(F32)
                packed = tail_high + pltpu.roll(tail - tail_high, 32, 1) + pltpu.roll(tail_high, 64, 1)
                parts.append(jnp.concatenate([high, low, high, packed.astype(BF16)], axis=1))
            out = dot(jnp.concatenate(parts, axis=0), out_of[...])
            rows[first * LANES:last * LANES, :] = out[:, :LANES]
            for i in range(first, last):
                part = out[(i - first) * LANES:(i - first + 1) * LANES, LANES:]
                margin += pltpu.roll(part, 8 * i, 1) if i else part
        margin = jnp.transpose(margin)[:CHUNKS * 8].reshape(CHUNKS, 8, LANES)
        fs[slot, 0] = margin[:, :MARGIN]
        fs[slot, 1] = margin[:, MARGIN:]
        send(slot, BX, (fs.at[slot, 0], fr.at[slot, 1]), (fs.at[slot, 1], fr.at[slot, 0]))

    def b_z(s, c):
        slot = s * 3 + c
        arrive(slot, BX)

        near = jnp.concatenate([keep(has_upper["gx"], fr[slot, 1]), keep(has_lower["gx"], fr[slot, 0])], axis=1)
        blank = jnp.zeros((LANES - CHUNKS * 8, LANES), F32)
        side = jnp.transpose(jnp.concatenate([near.reshape(CHUNKS * 8, LANES), blank], axis=0))
        rows = flat(zb, slot)
        edge = (lanes < MARGIN) | (lanes >= LANES - MARGIN)
        for i in range(CHUNKS):
            at = pl.ds(i * LANES, LANES)
            rows[at, :] += jnp.where(edge, pltpu.roll(side, LANES - 8 * i - MARGIN, 1), 0.0)

        send(
            slot, BZ,
            (zb.at[slot, pl.ds(BRICK, MARGIN)], zr.at[slot, 1]),
            (zb.at[slot, pl.ds(BRICK + MARGIN, MARGIN)], zr.at[slot, 0]),
        )

    def b_y(s, c):
        slot = s * 3 + c
        arrive(slot, BZ)
        zb[slot, 0:MARGIN] += keep(has_lower["gz"], zr[slot, 0])
        zb[slot, BRICK - MARGIN:BRICK] += keep(has_upper["gz"], zr[slot, 1])
        other = slot + 3 * SWEEPS
        rows = zb[slot, 0:BRICK, BRICK:LENGTH, :]
        ys[other, 0] = rows[:, :MARGIN]
        ys[other, 1] = rows[:, MARGIN:]
        y_pack(slot, zb[slot, 0:BRICK, 0:BRICK, :])
        send(slot, BY, (ys.at[other, 0], yr.at[other, 1]), (ys.at[other, 1], yr.at[other, 0]))
        y_send(slot)

    def c_start(s, c):
        slot = s * 3 + c
        arrive(slot, BY)
        other = slot + 3 * SWEEPS
        low = keep(has_lower["gy"], yr[other, 0])
        high = keep(has_upper["gy"], yr[other, 1])
        own = zb[slot, 0:BRICK, 0:BRICK, :]
        blank = jnp.zeros((BRICK, MARGIN, LANES), F32)
        own = jnp.concatenate([
            own[:, :8] + jnp.concatenate([low, blank], axis=1),
            own[:, 8:24],
            own[:, 24:] + jnp.concatenate([blank, high], axis=1),
        ], axis=1)
        corr[slot] = own
        xz_pack(slot, own)
        xz_send(slot)
        if s == SWEEPS - 1:
            total = own
            for before in range(s):
                total = corr[before * 3 + c] + total
            disp[c] = total

    def update(s, c):
        slot = s * 3 + c
        arrive(slot, CY)
        margins = zb[slot, 0:BRICK, BRICK:LENGTH, :]
        halo = halo_get(
            slot,
            keep(has_lower["gy"], cyr[slot, 0] + margins[:, MARGIN - 1, :]),
            keep(has_upper["gy"], cyr[slot, 1] + margins[:, MARGIN, :]),
        )
        values = corr[slot]
        total = centre[c] * values
        moved = list(shifts(values, halo))
        for k in range(3):
            part = faces[2 * k] * moved[2 * k] + faces[2 * k + 1] * moved[2 * k + 1]
            total = total - (part * ratio(c, k) if ratio(c, k) != 1.0 else part)
        if s == SWEEPS - 1:
            resid[c] = w[slot, 0:BRICK, 0:BRICK, :] - total
        else:
            w[slot + 3, 0:BRICK, 0:BRICK, :] = w[slot, 0:BRICK, 0:BRICK, :] - total
            a_pack(s + 1, c)
            a_send(s + 1, c)

    def stiff(s, c):
        arrive(6, CY)
        own = modulus[...]
        low, high = keep(has_lower["gy"], cyr[6, 0]), keep(has_upper["gy"], cyr[6, 1])
        for number, moved in enumerate(shifts(own, halo_get(6, low, high))):
            faces[number] = 0.5 * (own + moved)
        sums = [faces[2 * k] + faces[2 * k + 1] for k in range(3)]
        for component in range(3):
            total = SIGMA_SHIFT * own
            for k in range(3):
                total = total + ratio(component, k) * sums[k]
            centre[component] = total

    fetched[0].wait()
    for c in range(3):
        a_pack(0, c)
    for slot in range(6):
        w[slot, LENGTH:] = jnp.zeros((PLANES - LENGTH, LENGTH, LANES), F32)

    for copy in fetched[1:]:
        copy.wait()

    def look(z, carry):
        picked = labels[z]
        value = jnp.zeros(picked.shape, F32)
        for number in range(table.shape[0]):
            value = jnp.where(picked == number, table[number], value)
        modulus[z] = jnp.where(mask[z] == 1, value, VOID_MODULUS)
        return carry

    lax.fori_loop(0, BRICK, look, 0)
    y_pack(6, modulus[...])
    xz_pack(6, modulus[...])

    for c in range(3):
        def invert(y, carry, c=c):
            at = pl.ds(pl.multiple_of(y * LENGTH, 8), LENGTH)
            rinv[c, at, :] = 1.0 / (REF_MODULUS * (
                ratio(c, 0) * eigen_rows[...]
                + ratio(c, 1) * eigen_rows[pl.ds(y, 1), :]
                + ratio(c, 2) * eigen_x[...]
                + SIGMA_SHIFT
            ))
            return carry

        lax.fori_loop(0, LENGTH, invert, 0)

    pl.semaphore_wait(barrier, 6)
    for c in range(3):
        a_send(0, c)
    y_send(6)
    xz_send(6)

    stages = dict(a_z=a_z, a_x=a_x, s1=s1, s2=s2, s3=s3, b_z=b_z, b_y=b_y, c_start=c_start, update=update,
                  stiff=stiff)
    for s, c, name in ORDER:
        stages[name](s, c)

    for (_, phase), made in pending.items():
        for copy, there in zip(made, (has_lower, has_upper)):
            pl.when(there[AXIS[phase]])(copy.wait_send)


def local(load, labels, mask, table):
    tables = constants()
    vmem = pl.BlockSpec(memory_space=pltpu.VMEM)
    hbm = pl.BlockSpec(memory_space=pltpu.HBM)
    slots = 3 * SWEEPS
    field = jax.ShapeDtypeStruct(load.shape, F32)
    block = (BRICK, BRICK, LANES)
    return pl.pallas_call(
        kernel,
        out_shape=(field, field),
        in_specs=[hbm] * (4 + len(tables)),
        out_specs=(vmem, vmem),
        scratch_shapes=[
            pltpu.VMEM(block, F32),
            pltpu.VMEM((6,) + block, F32),
            pltpu.VMEM((3,) + block, F32),
            pltpu.VMEM((slots, PLANES, LENGTH, LANES), F32),
            pltpu.VMEM((slots, 2, CHUNKS, MARGIN, LANES), F32),
            pltpu.VMEM((slots, 2, CHUNKS, MARGIN, LANES), F32),
            pltpu.VMEM((PADDED, LANES), F32),
            pltpu.VMEM((PADDED, LANES), F32),
            pltpu.VMEM((PADDED, LANES), F32),
            pltpu.VMEM((PADDED, LANES), F32),
            pltpu.VMEM((slots, PLANES, LENGTH, LANES), F32),
            pltpu.VMEM((slots, 2, CHUNKS, MARGIN, LANES), F32),
            pltpu.VMEM((slots, 2, CHUNKS, MARGIN, LANES), F32),
            pltpu.VMEM((slots, 2, MARGIN, LENGTH, LANES), F32),
            pltpu.VMEM((2 * slots, 2, BRICK, MARGIN, LANES), F32),
            pltpu.VMEM((2 * slots, 2, BRICK, MARGIN, LANES), F32),
            pltpu.VMEM((slots,) + block, F32),
            pltpu.VMEM((3, ROWS, WIDE), F32),
            pltpu.VMEM((slots + 1, 2, BRICK, LANES), F32),
            pltpu.VMEM((slots + 1, 2, BRICK, LANES), F32),
            pltpu.VMEM((slots + 1, 2, BRICK, LANES), F32),
            pltpu.VMEM((slots + 1, 2, BRICK, LANES), F32),
            pltpu.VMEM((slots + 1, 16, LANES), F32),
            pltpu.VMEM((slots + 1, 2, 16, LANES), F32),
            pltpu.SemaphoreType.DMA(((slots + 1) * PHASES * 2,)),
            pltpu.SemaphoreType.DMA(((slots + 1) * PHASES * 2,)),
            pltpu.SemaphoreType.DMA((4 + len(tables),)),
            pltpu.VMEM(load.shape, F32),
            pltpu.VMEM(block, jnp.int32),
            pltpu.VMEM(block, jnp.int32),
            pltpu.SMEM(table.shape, F32),
        ] + [pltpu.VMEM(t.shape, t.dtype) for t in tables] + [
        ],
        compiler_params=pltpu.CompilerParams(
            collective_id=0, has_side_effects=True, vmem_limit_bytes=44 * 1024 * 1024
        ),
    )(*(pltpu.with_memory_space_constraint(v, pltpu.HBM) for v in (load, labels, mask, table, *map(jnp.asarray, tables))))


def solution(mesh):
    placed = (P(None, "gz", "gy", "gx"), P("gz", "gy", "gx"), P("gz", "gy", "gx"), P())
    return jax.shard_map(
        local,
        mesh=mesh,
        in_specs=placed,
        out_specs=(P(None, "gz", "gy", "gx"), P(None, "gz", "gy", "gx")),
        check_vma=False,
    )
```

```python
import jax
import jax.numpy as jnp
import numpy as np
from jax import lax
from jax.experimental import pallas as pl
from jax.experimental.pallas import tpu as pltpu
from jax.sharding import PartitionSpec as P

BRICK = 32
MARGIN = 4
SWEEPS = 2
LENGTH = BRICK + 2 * MARGIN
LANES = 128
WIDE = 256
ROWS = LENGTH * LENGTH
PADDED = 1664
CHUNKS = PADDED // LANES
OWNED = BRICK * LENGTH
LAMBDA_RATIO = 2.0
SIGMA_SHIFT = 0.1
REF_MODULUS = 1.5
VOID_MODULUS = 0.1
MESH = pl.DeviceIdType.MESH
UNROLL = 10
GROUPS = ((0, 4), (4, 8), (8, 13))
PHASES = 10
AY, AZ, AE, AX, BX, BZ, BY, CY, CZ, CX = range(PHASES)
AXIS = ("gy", "gz", "gz", "gx", "gx", "gz", "gy", "gy", "gz", "gx")
PLANES = 42
TABLES = 6
ORDER = (
    (0, 0, "a_z"), (0, 1, "a_z"), (0, 0, "a_x"), (0, 2, "a_z"), (0, 1, "a_x"), (0, 0, "s1"), (0, 0, "s2"),
    (0, 0, "s3"), (0, 2, "a_x"), (0, 1, "s1"), (0, 0, "b_z"), (0, 1, "s2"), (0, 1, "s3"), (0, 0, "b_y"),
    (0, 2, "s1"), (0, 1, "b_z"), (0, 2, "s2"), (0, 2, "s3"), (0, 0, "c_start"), (0, 1, "b_y"), (0, 0, "stiff"),
    (0, 2, "b_z"), (0, 0, "update"), (0, 1, "c_start"), (0, 2, "b_y"), (0, 1, "update"), (1, 0, "a_z"),
    (0, 2, "c_start"), (1, 0, "a_x"), (1, 1, "a_z"), (0, 2, "update"), (1, 0, "s1"), (1, 1, "a_x"), (1, 0, "s2"),
    (1, 0, "s3"), (1, 2, "a_z"), (1, 1, "s1"), (1, 1, "s2"), (1, 2, "a_x"), (1, 0, "b_z"), (1, 1, "s3"),
    (1, 2, "s1"), (1, 2, "s2"), (1, 1, "b_z"), (1, 2, "s3"), (1, 0, "b_y"), (1, 1, "b_y"), (1, 2, "b_z"),
    (1, 2, "b_y"), (1, 0, "c_start"), (1, 1, "c_start"), (1, 2, "c_start"), (1, 1, "update"), (1, 0, "update"),
    (1, 2, "update"),
)
F32 = jnp.float32
BF16 = jnp.bfloat16


def ratio(component, direction):
    return LAMBDA_RATIO if component == direction else 1.0


def halves(values):
    high = values.astype(BF16)
    return high, (values - high.astype(F32)).astype(BF16)


def constants():
    grid = np.arange(1, LENGTH + 1, dtype=np.float64)
    sine = np.sqrt(2.0 / (LENGTH + 1)) * np.sin(np.pi * grid[:, None] * grid[None, :] / (LENGTH + 1))
    eigen = 2.0 - 2.0 * np.cos(np.pi * grid / (LENGTH + 1))
    spot = np.arange(LENGTH, dtype=np.float64)
    ramp = np.minimum(np.minimum((spot + 0.5) / (2 * MARGIN), (LENGTH - 0.5 - spot) / (2 * MARGIN)), 1.0)
    ramped = ramp[:, None] * sine
    place = np.concatenate([np.arange(MARGIN, MARGIN + BRICK), np.arange(MARGIN), np.arange(MARGIN + BRICK, LENGTH)])
    forward = ramped[place].T
    backward = sine.T[place]
    count = LANES // BRICK
    wide_x = LANES + 2 * MARGIN
    forward_x = np.zeros((wide_x, WIDE))
    backward_x = np.zeros((WIDE, wide_x))
    for brick in range(count):
        rows = slice(brick * BRICK, brick * BRICK + LENGTH)
        columns = slice(brick * LENGTH, (brick + 1) * LENGTH)
        forward_x[rows, columns] = ramped
        backward_x[columns, rows] = sine
    edge = slice(LANES, LANES + 2 * MARGIN)
    into = forward_x[MARGIN:MARGIN + LANES]
    into_edge = np.concatenate([forward_x[:MARGIN], forward_x[MARGIN + LANES:]])
    out = np.zeros((WIDE, WIDE))
    out[:, :LANES] = backward_x[:, MARGIN:MARGIN + LANES]
    out[:, edge] = np.concatenate([backward_x[:, :MARGIN], backward_x[:, MARGIN + LANES:]], axis=1)
    rest = count * LENGTH - LANES
    eigen_x = np.zeros((1, WIDE))
    eigen_x[0, : count * LENGTH] = np.tile(eigen, count)
    eigen_lanes = np.broadcast_to(eigen[:, None], (LENGTH, WIDE))

    def high(matrix):
        return matrix.astype(np.float32).astype(BF16).astype(np.float64)

    def low(matrix):
        return matrix - high(matrix)

    def pair(matrix):
        zero = np.zeros((LENGTH, LENGTH))
        both = np.block([[matrix, zero], [zero, matrix]])
        return np.concatenate([high(both), high(both), low(both)], axis=1)

    def tall(*parts):
        blank = np.zeros((4 * LANES - sum(p.shape[0] for p in parts), WIDE))
        return np.concatenate(parts + (blank,))

    head, tail = out[:LANES], out[LANES:LANES + rest]
    return [m.astype(BF16) for m in (
        pair(forward),
        pair(backward),
        tall(high(into), high(into), low(into), high(into_edge), high(into_edge), low(into_edge)),
        tall(high(head), high(head), low(head), high(tail), high(tail), low(tail)),
    )] + [eigen_x.astype(np.float32), np.ascontiguousarray(eigen_lanes).astype(np.float32)]


def dot(a, b):
    return jnp.dot(a, b, preferred_element_type=F32)


def triple(values):
    high, low = halves(values)
    return jnp.concatenate([high, low, high], axis=0)


def kernel(
    load_in, labels_in, mask_in, table_in, *rest,
):
    tables = rest[:TABLES]
    (
        disp, resid, modulus, faces, centre, w, xs, xr, b1a, b1b, b2a, b2b, zb, fs, fr, zr, ys, yr, corr, rinv,
        cys, cyr, czs, czr, cxs, cxr, send_sem, recv_sem, in_sem,
        load, labels, mask, table, fwd, bwd, into, out_of, eigen_x, eigen_rows,
    ) = rest[TABLES:]
    index = {a: lax.axis_index(a) for a in ("gx", "gy", "gz")}
    count = {a: lax.axis_size(a) for a in ("gx", "gy", "gz")}
    lower = {a: lax.rem(index[a] + count[a] - 1, count[a]) for a in index}
    upper = {a: lax.rem(index[a] + 1, count[a]) for a in index}
    has_lower = {a: index[a] > 0 for a in index}
    has_upper = {a: index[a] < count[a] - 1 for a in index}

    barrier = pltpu.get_barrier_semaphore()
    for a in ("gx", "gy", "gz"):
        pl.semaphore_signal(barrier, inc=1, device_id={a: lower[a]}, device_id_type=MESH)
        pl.semaphore_signal(barrier, inc=1, device_id={a: upper[a]}, device_id_type=MESH)

    sources = (*(load_in.at[c] for c in range(3)), labels_in, mask_in, table_in, *tables)
    targets = (*(load.at[c] for c in range(3)), labels, mask, table, fwd, bwd, into, out_of, eigen_x, eigen_rows)
    fetched = [
        pltpu.make_async_copy(source, target, in_sem.at[number])
        for number, (source, target) in enumerate(zip(sources, targets))
    ]
    for copy in fetched:
        copy.start()

    def copies(slot, phase, down, up):
        a = AXIS[phase]
        made = []
        for side, (source, target), device in ((0, down, lower[a]), (1, up, upper[a])):
            number = (slot * PHASES + phase) * 2 + side
            made.append(pltpu.make_async_remote_copy(
                src_ref=source, dst_ref=target,
                send_sem=send_sem.at[number], recv_sem=recv_sem.at[number],
                device_id={a: device}, device_id_type=MESH,
            ))
        return made

    pending = {}

    def send(slot, phase, down, up):
        made = copies(slot, phase, down, up)
        for copy, there in zip(made, (has_lower, has_upper)):
            pl.when(there[AXIS[phase]])(copy.start)
        pending[slot, phase] = made

    def arrive(slot, phase):
        for copy, there in zip(pending[slot, phase], (has_upper, has_lower)):
            pl.when(there[AXIS[phase]])(copy.wait_recv)

    def flat(ref, slot):
        return ref.at[slot].reshape(PLANES * LENGTH, LANES)

    def keep(flag, values):
        return jnp.where(flag, values, 0.0)

    lanes = lax.broadcasted_iota(jnp.int32, (LANES, LANES), 1)

    def face_columns(values):
        flat = values.reshape(BRICK * BRICK, LANES)
        total = jnp.zeros((LANES, LANES), F32)
        for i in range(8):
            part = pltpu.roll(flat[i * LANES:(i + 1) * LANES], 2 * i + 1, 1)
            total = jnp.where((lanes == 2 * i) | (lanes == 2 * i + 1), part, total)
        return jnp.transpose(total)[:16]

    def y_pack(slot, values):
        cys[slot, 0] = values[:, 0, :]
        cys[slot, 1] = values[:, BRICK - 1, :]

    def y_send(slot):
        send(slot, CY, (cys.at[slot, 0], cyr.at[slot, 1]), (cys.at[slot, 1], cyr.at[slot, 0]))

    def xz_pack(slot, values):
        czs[slot, 0] = values[0]
        czs[slot, 1] = values[BRICK - 1]
        cxs[slot] = face_columns(values)

    def xz_send(slot):
        send(slot, CZ, (czs.at[slot, 0], czr.at[slot, 1]), (czs.at[slot, 1], czr.at[slot, 0]))
        send(slot, CX, (cxs.at[slot], cxr.at[slot, 1]), (cxs.at[slot], cxr.at[slot, 0]))

    def halo_get(slot, low_y, high_y):
        for phase in (CZ, CX):
            arrive(slot, phase)
        low_z = keep(has_lower["gz"], czr[slot, 0])
        high_z = keep(has_upper["gz"], czr[slot, 1])
        left = keep(has_lower["gx"], cxr[slot, 0])
        right = keep(has_upper["gx"], cxr[slot, 1])
        odd = lax.rem(lax.broadcasted_iota(jnp.int32, (16, LANES), 0), 2) == 1
        both = jnp.where(odd, pltpu.roll(left, 1, 0), pltpu.roll(right, 15, 0))
        side = jnp.transpose(jnp.concatenate([both, jnp.zeros((LANES - 16, LANES), F32)], axis=0))
        side = jnp.concatenate(
            [pltpu.roll(side, LANES - 1 - 2 * i, 1) for i in range(8)], axis=0
        ).reshape(BRICK, BRICK, LANES)
        return low_y, high_y, low_z, high_z, side

    def shifts(values, halo):
        low_y, high_y, low_z, high_z, side = halo
        lane = lax.broadcasted_iota(jnp.int32, values.shape, 2)
        yield jnp.concatenate([low_z[None], values[:-1]], axis=0)
        yield jnp.concatenate([values[1:], high_z[None]], axis=0)
        yield jnp.concatenate([low_y[:, None, :], values[:, :-1]], axis=1)
        yield jnp.concatenate([values[:, 1:], high_y[:, None, :]], axis=1)
        yield jnp.where(lane == 0, side, pltpu.roll(values, 1, 2))
        yield jnp.where(lane == LANES - 1, side, pltpu.roll(values, LANES - 1, 2))

    def a_pack(s, c):
        slot = s * 3 + c
        if s == 0:
            values = load[c]
            w[slot, 0:BRICK, 0:BRICK, :] = values
        else:
            values = w[slot, 0:BRICK, 0:BRICK, :]
        ys[slot, 0] = values[:, 0:MARGIN, :]
        ys[slot, 1] = values[:, BRICK - MARGIN:BRICK, :]

    def z_planes(ref, slot, rows):
        def at(first):
            return ref.at[slot, pl.ds(first, MARGIN), rows]

        return (at(0), at(BRICK + MARGIN)), (at(BRICK - MARGIN), at(BRICK))

    def a_send(s, c):
        slot = s * 3 + c
        send(slot, AY, (ys.at[slot, 0], yr.at[slot, 1]), (ys.at[slot, 1], yr.at[slot, 0]))
        send(slot, AZ, *z_planes(w, slot, pl.ds(0, BRICK)))

    def a_z(s, c):
        slot = s * 3 + c
        arrive(slot, AY)
        low = keep(has_lower["gy"], yr[slot, 0])
        high = keep(has_upper["gy"], yr[slot, 1])
        w[slot, 0:BRICK, BRICK:LENGTH, :] = jnp.concatenate([low, high], axis=1)
        send(slot, AE, *z_planes(w, slot, pl.ds(BRICK, 2 * MARGIN)))

    def a_x(s, c):
        slot = s * 3 + c
        arrive(slot, AZ)
        arrive(slot, AE)
        low = w[slot, BRICK:BRICK + MARGIN]
        w[slot, BRICK:BRICK + MARGIN] = keep(has_lower["gz"], low)
        high = w[slot, BRICK + MARGIN:LENGTH]
        w[slot, BRICK + MARGIN:LENGTH] = keep(has_upper["gz"], high)
        rows = flat(w, slot)
        total = jnp.zeros((LANES, LANES), F32)
        for i in range(CHUNKS):
            part = pltpu.roll(rows[i * LANES:(i + 1) * LANES, :], 8 * i + MARGIN, 1)
            total = jnp.where((lanes >= 8 * i) & (lanes < 8 * i + 8), part, total)
        total = jnp.transpose(total)[:CHUNKS * 8].reshape(CHUNKS, 8, LANES)
        xs[slot, 0] = total[:, MARGIN:]
        xs[slot, 1] = total[:, :MARGIN]
        send(slot, AX, (xs.at[slot, 0], xr.at[slot, 1]), (xs.at[slot, 1], xr.at[slot, 0]))

    one, two = (b1a, b1b), (b2a, b2b)

    def transform(matrix, source, target, strided, scale=None):
        def body(i, carry):
            outs = []
            for k in range(UNROLL):
                at = pl.ds(pl.multiple_of((i * UNROLL + k) * 2 * LENGTH, 8), 2 * LENGTH)
                values = jnp.concatenate([source[0][at, :], source[1][at, :]], axis=1)
                outs.append(dot(matrix[...], triple(values)))
            for k in range(UNROLL):
                at = pl.ds(pl.multiple_of((i * UNROLL + k) * 2 * LENGTH, 8), 2 * LENGTH)
                out = outs[k]
                if scale is not None:
                    out = out * scale[at, :]
                for half in range(2):
                    part = out[:, half * LANES:(half + 1) * LANES]
                    if strided:
                        for which in range(2):
                            spot = pl.ds((i * UNROLL + k) * 2 + which, LENGTH, stride=LENGTH)
                            target[half][spot, :] = part[which * LENGTH:(which + 1) * LENGTH]
                    else:
                        target[half][at, :] = part
            return carry

        lax.fori_loop(0, LENGTH // 2 // UNROLL, body, 0)

    def s1(s, c):
        slot = s * 3 + c
        arrive(slot, AX)

        rows = flat(w, slot)
        near = jnp.concatenate([keep(has_lower["gx"], xr[slot, 0]), keep(has_upper["gx"], xr[slot, 1])], axis=1)
        high = near.astype(BF16).astype(F32)
        near = jnp.concatenate([high, near - high, high], axis=1)
        sides = []
        for first in range(0, CHUNKS, 5):
            group = near[first:first + 5].reshape(-1, LANES)
            blank = jnp.zeros((LANES - group.shape[0], LANES), F32)
            sides.append(jnp.transpose(jnp.concatenate([group, blank], axis=0)))
        for first, last in GROUPS:
            parts = []
            for i in range(first, last):
                side = sides[i // 5]
                if i % 5:
                    side = pltpu.roll(side, LANES - 24 * (i % 5), 1)
                high, low = halves(rows[i * LANES:(i + 1) * LANES, :])
                parts.append(jnp.concatenate([high, low, high, side.astype(BF16)], axis=1))
            out = dot(jnp.concatenate(parts, axis=0), into[...])
            b1a[first * LANES:last * LANES, :] = out[:, :LANES]
            b1b[first * LANES:last * LANES, :] = out[:, LANES:]

        transform(fwd, one, two, True)

    def s2(s, c):
        transform(fwd, two, one, False, rinv.at[c])
        transform(bwd, one, two, True)

    def s3(s, c):
        slot = s * 3 + c
        transform(bwd, two, one, False)

        rows = flat(zb, slot)
        margin = jnp.zeros((LANES, LANES), F32)
        for first, last in GROUPS:
            parts = []
            for i in range(first, last):
                at = pl.ds(i * LANES, LANES)
                high, low = halves(b1a[at, :])
                tail = b1b[at, :]
                tail_high = tail.astype(BF16).astype(F32)
                packed = tail_high + pltpu.roll(tail - tail_high, 32, 1) + pltpu.roll(tail_high, 64, 1)
                parts.append(jnp.concatenate([high, low, high, packed.astype(BF16)], axis=1))
            out = dot(jnp.concatenate(parts, axis=0), out_of[...])
            rows[first * LANES:last * LANES, :] = out[:, :LANES]
            for i in range(first, last):
                part = out[(i - first) * LANES:(i - first + 1) * LANES, LANES:]
                margin += pltpu.roll(part, 8 * i, 1) if i else part
        margin = jnp.transpose(margin)[:CHUNKS * 8].reshape(CHUNKS, 8, LANES)
        fs[slot, 0] = margin[:, :MARGIN]
        fs[slot, 1] = margin[:, MARGIN:]
        send(slot, BX, (fs.at[slot, 0], fr.at[slot, 1]), (fs.at[slot, 1], fr.at[slot, 0]))

    def b_z(s, c):
        slot = s * 3 + c
        arrive(slot, BX)

        near = jnp.concatenate([keep(has_upper["gx"], fr[slot, 1]), keep(has_lower["gx"], fr[slot, 0])], axis=1)
        blank = jnp.zeros((LANES - CHUNKS * 8, LANES), F32)
        side = jnp.transpose(jnp.concatenate([near.reshape(CHUNKS * 8, LANES), blank], axis=0))
        rows = flat(zb, slot)
        edge = (lanes < MARGIN) | (lanes >= LANES - MARGIN)
        for i in range(CHUNKS):
            at = pl.ds(i * LANES, LANES)
            rows[at, :] += jnp.where(edge, pltpu.roll(side, LANES - 8 * i - MARGIN, 1), 0.0)

        send(
            slot, BZ,
            (zb.at[slot, pl.ds(BRICK, MARGIN)], zr.at[slot, 1]),
            (zb.at[slot, pl.ds(BRICK + MARGIN, MARGIN)], zr.at[slot, 0]),
        )

    def b_y(s, c):
        slot = s * 3 + c
        arrive(slot, BZ)
        zb[slot, 0:MARGIN] += keep(has_lower["gz"], zr[slot, 0])
        zb[slot, BRICK - MARGIN:BRICK] += keep(has_upper["gz"], zr[slot, 1])
        other = slot + 3 * SWEEPS
        rows = zb[slot, 0:BRICK, BRICK:LENGTH, :]
        ys[other, 0] = rows[:, :MARGIN]
        ys[other, 1] = rows[:, MARGIN:]
        y_pack(slot, zb[slot, 0:BRICK, 0:BRICK, :])
        send(slot, BY, (ys.at[other, 0], yr.at[other, 1]), (ys.at[other, 1], yr.at[other, 0]))
        y_send(slot)

    def c_start(s, c):
        slot = s * 3 + c
        arrive(slot, BY)
        other = slot + 3 * SWEEPS
        low = keep(has_lower["gy"], yr[other, 0])
        high = keep(has_upper["gy"], yr[other, 1])
        own = zb[slot, 0:BRICK, 0:BRICK, :]
        blank = jnp.zeros((BRICK, MARGIN, LANES), F32)
        own = jnp.concatenate([
            own[:, :8] + jnp.concatenate([low, blank], axis=1),
            own[:, 8:24],
            own[:, 24:] + jnp.concatenate([blank, high], axis=1),
        ], axis=1)
        corr[slot] = own
        xz_pack(slot, own)
        xz_send(slot)
        if s == SWEEPS - 1:
            total = own
            for before in range(s):
                total = corr[before * 3 + c] + total
            disp[c] = total

    def update(s, c):
        slot = s * 3 + c
        arrive(slot, CY)
        margins = zb[slot, 0:BRICK, BRICK:LENGTH, :]
        halo = halo_get(
            slot,
            keep(has_lower["gy"], cyr[slot, 0] + margins[:, MARGIN - 1, :]),
            keep(has_upper["gy"], cyr[slot, 1] + margins[:, MARGIN, :]),
        )
        values = corr[slot]
        total = centre[c] * values
        moved = list(shifts(values, halo))
        for k in range(3):
            part = faces[2 * k] * moved[2 * k] + faces[2 * k + 1] * moved[2 * k + 1]
            total = total - (part * ratio(c, k) if ratio(c, k) != 1.0 else part)
        if s == SWEEPS - 1:
            resid[c] = w[slot, 0:BRICK, 0:BRICK, :] - total
        else:
            w[slot + 3, 0:BRICK, 0:BRICK, :] = w[slot, 0:BRICK, 0:BRICK, :] - total
            a_pack(s + 1, c)
            a_send(s + 1, c)

    def stiff(s, c):
        arrive(6, CY)
        own = modulus[...]
        low, high = keep(has_lower["gy"], cyr[6, 0]), keep(has_upper["gy"], cyr[6, 1])
        for number, moved in enumerate(shifts(own, halo_get(6, low, high))):
            faces[number] = 0.5 * (own + moved)
        sums = [faces[2 * k] + faces[2 * k + 1] for k in range(3)]
        for component in range(3):
            total = SIGMA_SHIFT * own
            for k in range(3):
                total = total + ratio(component, k) * sums[k]
            centre[component] = total

    for c in range(3):
        fetched[c].wait()
        a_pack(0, c)
        if c == 0:
            pl.semaphore_wait(barrier, 6)
        a_send(0, c)
    for slot in range(6):
        w[slot, LENGTH:] = jnp.zeros((PLANES - LENGTH, LENGTH, LANES), F32)

    for copy in fetched[3:]:
        copy.wait()

    def look(z, carry):
        picked = labels[z]
        value = jnp.zeros(picked.shape, F32)
        for number in range(table.shape[0]):
            value = jnp.where(picked == number, table[number], value)
        modulus[z] = jnp.where(mask[z] == 1, value, VOID_MODULUS)
        return carry

    lax.fori_loop(0, BRICK, look, 0)
    y_pack(6, modulus[...])
    xz_pack(6, modulus[...])
    y_send(6)
    xz_send(6)

    for c in range(3):
        def invert(y, carry, c=c):
            at = pl.ds(pl.multiple_of(y * LENGTH, 8), LENGTH)
            rinv[c, at, :] = 1.0 / (REF_MODULUS * (
                ratio(c, 0) * eigen_rows[...]
                + ratio(c, 1) * eigen_rows[pl.ds(y, 1), :]
                + ratio(c, 2) * eigen_x[...]
                + SIGMA_SHIFT
            ))
            return carry

        lax.fori_loop(0, LENGTH, invert, 0)

    stages = dict(a_z=a_z, a_x=a_x, s1=s1, s2=s2, s3=s3, b_z=b_z, b_y=b_y, c_start=c_start, update=update,
                  stiff=stiff)
    for s, c, name in ORDER:
        stages[name](s, c)

    for (_, phase), made in pending.items():
        for copy, there in zip(made, (has_lower, has_upper)):
            pl.when(there[AXIS[phase]])(copy.wait_send)


def local(load, labels, mask, table):
    tables = constants()
    vmem = pl.BlockSpec(memory_space=pltpu.VMEM)
    hbm = pl.BlockSpec(memory_space=pltpu.HBM)
    slots = 3 * SWEEPS
    field = jax.ShapeDtypeStruct(load.shape, F32)
    block = (BRICK, BRICK, LANES)
    return pl.pallas_call(
        kernel,
        out_shape=(field, field),
        in_specs=[hbm] * (4 + len(tables)),
        out_specs=(vmem, vmem),
        scratch_shapes=[
            pltpu.VMEM(block, F32),
            pltpu.VMEM((6,) + block, F32),
            pltpu.VMEM((3,) + block, F32),
            pltpu.VMEM((slots, PLANES, LENGTH, LANES), F32),
            pltpu.VMEM((slots, 2, CHUNKS, MARGIN, LANES), F32),
            pltpu.VMEM((slots, 2, CHUNKS, MARGIN, LANES), F32),
            pltpu.VMEM((PADDED, LANES), F32),
            pltpu.VMEM((PADDED, LANES), F32),
            pltpu.VMEM((PADDED, LANES), F32),
            pltpu.VMEM((PADDED, LANES), F32),
            pltpu.VMEM((slots, PLANES, LENGTH, LANES), F32),
            pltpu.VMEM((slots, 2, CHUNKS, MARGIN, LANES), F32),
            pltpu.VMEM((slots, 2, CHUNKS, MARGIN, LANES), F32),
            pltpu.VMEM((slots, 2, MARGIN, LENGTH, LANES), F32),
            pltpu.VMEM((2 * slots, 2, BRICK, MARGIN, LANES), F32),
            pltpu.VMEM((2 * slots, 2, BRICK, MARGIN, LANES), F32),
            pltpu.VMEM((slots,) + block, F32),
            pltpu.VMEM((3, ROWS, WIDE), F32),
            pltpu.VMEM((slots + 1, 2, BRICK, LANES), F32),
            pltpu.VMEM((slots + 1, 2, BRICK, LANES), F32),
            pltpu.VMEM((slots + 1, 2, BRICK, LANES), F32),
            pltpu.VMEM((slots + 1, 2, BRICK, LANES), F32),
            pltpu.VMEM((slots + 1, 16, LANES), F32),
            pltpu.VMEM((slots + 1, 2, 16, LANES), F32),
            pltpu.SemaphoreType.DMA(((slots + 1) * PHASES * 2,)),
            pltpu.SemaphoreType.DMA(((slots + 1) * PHASES * 2,)),
            pltpu.SemaphoreType.DMA((6 + len(tables),)),
            pltpu.VMEM(load.shape, F32),
            pltpu.VMEM(block, jnp.int32),
            pltpu.VMEM(block, jnp.int32),
            pltpu.SMEM(table.shape, F32),
        ] + [pltpu.VMEM(t.shape, t.dtype) for t in tables] + [
        ],
        compiler_params=pltpu.CompilerParams(
            collective_id=0, has_side_effects=True, vmem_limit_bytes=44 * 1024 * 1024
        ),
    )(*(pltpu.with_memory_space_constraint(v, pltpu.HBM) for v in (load, labels, mask, table, *map(jnp.asarray, tables))))


def solution(mesh):
    placed = (P(None, "gz", "gy", "gx"), P("gz", "gy", "gx"), P("gz", "gy", "gx"), P())
    return jax.shard_map(
        local,
        mesh=mesh,
        in_specs=placed,
        out_specs=(P(None, "gz", "gy", "gx"), P(None, "gz", "gy", "gx")),
        check_vma=False,
    )
```

```python
import jax
import jax.numpy as jnp
import numpy as np
from jax import lax
from jax.experimental import pallas as pl
from jax.experimental.pallas import tpu as pltpu
from jax.sharding import PartitionSpec as P

BRICK = 32
MARGIN = 4
SWEEPS = 2
LENGTH = BRICK + 2 * MARGIN
LANES = 128
WIDE = 256
ROWS = LENGTH * LENGTH
PADDED = 1664
CHUNKS = PADDED // LANES
OWNED = BRICK * LENGTH
LAMBDA_RATIO = 2.0
SIGMA_SHIFT = 0.1
REF_MODULUS = 1.5
VOID_MODULUS = 0.1
MESH = pl.DeviceIdType.MESH
UNROLL = 10
GROUPS = ((0, 4), (4, 8), (8, 13))
PHASES = 10
AY, AZ, AE, AX, BX, BZ, BY, CY, CZ, CX = range(PHASES)
AXIS = ("gy", "gz", "gz", "gx", "gx", "gz", "gy", "gy", "gz", "gx")
PLANES = 42
TABLES = 6
ORDER = (
    (0, 0, "a_z"), (0, 1, "a_z"), (0, 0, "a_x"), (0, 2, "a_z"), (0, 1, "a_x"), (0, 0, "s1"), (0, 0, "s2"),
    (0, 0, "s3"), (0, 2, "a_x"), (0, 1, "s1"), (0, 0, "b_z"), (0, 1, "s2"), (0, 1, "s3"), (0, 0, "b_y"),
    (0, 0, "stiff"), (0, 2, "s1"), (0, 1, "b_z"), (0, 2, "s2"), (0, 2, "s3"), (0, 0, "c_start"), (0, 1, "b_y"),
    (0, 2, "b_z"), (0, 0, "update"), (0, 1, "c_start"), (0, 2, "b_y"), (1, 0, "a_z"), (0, 1, "update"),
    (0, 2, "c_start"), (1, 0, "a_x"), (1, 1, "a_z"), (0, 2, "update"), (1, 0, "s1"), (1, 1, "a_x"), (1, 0, "s2"),
    (1, 0, "s3"), (1, 2, "a_z"), (1, 1, "s1"), (1, 1, "s2"), (1, 2, "a_x"), (1, 0, "b_z"), (1, 1, "s3"),
    (1, 2, "s1"), (1, 0, "b_y"), (1, 2, "s2"), (1, 1, "b_z"), (1, 2, "s3"), (1, 1, "b_y"), (1, 2, "b_z"),
    (1, 0, "c_start"), (1, 2, "b_y"), (1, 1, "c_start"), (1, 0, "update"), (1, 2, "c_start"), (1, 1, "update"),
    (1, 2, "update"),
)
F32 = jnp.float32
BF16 = jnp.bfloat16


def ratio(component, direction):
    return LAMBDA_RATIO if component == direction else 1.0


def halves(values):
    high = values.astype(BF16)
    return high, (values - high.astype(F32)).astype(BF16)


def constants():
    grid = np.arange(1, LENGTH + 1, dtype=np.float64)
    sine = np.sqrt(2.0 / (LENGTH + 1)) * np.sin(np.pi * grid[:, None] * grid[None, :] / (LENGTH + 1))
    eigen = 2.0 - 2.0 * np.cos(np.pi * grid / (LENGTH + 1))
    spot = np.arange(LENGTH, dtype=np.float64)
    ramp = np.minimum(np.minimum((spot + 0.5) / (2 * MARGIN), (LENGTH - 0.5 - spot) / (2 * MARGIN)), 1.0)
    ramped = ramp[:, None] * sine
    place = np.concatenate([np.arange(MARGIN, MARGIN + BRICK), np.arange(MARGIN), np.arange(MARGIN + BRICK, LENGTH)])
    forward = ramped[place].T
    backward = sine.T[place]
    count = LANES // BRICK
    wide_x = LANES + 2 * MARGIN
    forward_x = np.zeros((wide_x, WIDE))
    backward_x = np.zeros((WIDE, wide_x))
    for brick in range(count):
        rows = slice(brick * BRICK, brick * BRICK + LENGTH)
        columns = slice(brick * LENGTH, (brick + 1) * LENGTH)
        forward_x[rows, columns] = ramped
        backward_x[columns, rows] = sine
    edge = slice(LANES, LANES + 2 * MARGIN)
    into = forward_x[MARGIN:MARGIN + LANES]
    into_edge = np.concatenate([forward_x[:MARGIN], forward_x[MARGIN + LANES:]])
    out = np.zeros((WIDE, WIDE))
    out[:, :LANES] = backward_x[:, MARGIN:MARGIN + LANES]
    out[:, edge] = np.concatenate([backward_x[:, :MARGIN], backward_x[:, MARGIN + LANES:]], axis=1)
    rest = count * LENGTH - LANES
    eigen_x = np.zeros((1, WIDE))
    eigen_x[0, : count * LENGTH] = np.tile(eigen, count)
    eigen_lanes = np.broadcast_to(eigen[:, None], (LENGTH, WIDE))

    def high(matrix):
        return matrix.astype(np.float32).astype(BF16).astype(np.float64)

    def low(matrix):
        return matrix - high(matrix)

    def pair(matrix):
        zero = np.zeros((LENGTH, LENGTH))
        both = np.block([[matrix, zero], [zero, matrix]])
        return np.concatenate([high(both), high(both), low(both)], axis=1)

    def tall(*parts):
        blank = np.zeros((4 * LANES - sum(p.shape[0] for p in parts), WIDE))
        return np.concatenate(parts + (blank,))

    head, tail = out[:LANES], out[LANES:LANES + rest]
    return [m.astype(BF16) for m in (
        pair(forward),
        pair(backward),
        tall(high(into), high(into), low(into), high(into_edge), high(into_edge), low(into_edge)),
        tall(high(head), high(head), low(head), high(tail), high(tail), low(tail)),
    )] + [eigen_x.astype(np.float32), np.ascontiguousarray(eigen_lanes).astype(np.float32)]


def dot(a, b):
    return jnp.dot(a, b, preferred_element_type=F32)


def triple(values):
    high, low = halves(values)
    return jnp.concatenate([high, low, high], axis=0)


def kernel(
    load_in, labels_in, mask_in, table_in, *rest,
):
    tables = rest[:TABLES]
    (
        disp, resid, modulus, faces, centre, w, xs, xr, b1a, b1b, b2a, b2b, zb, fs, fr, zr, ys, yr, corr, rinv,
        cys, cyr, czs, czr, cxs, cxr, send_sem, recv_sem, in_sem,
        load, labels, mask, table, fwd, bwd, into, out_of, eigen_x, eigen_rows,
    ) = rest[TABLES:]
    index = {a: lax.axis_index(a) for a in ("gx", "gy", "gz")}
    count = {a: lax.axis_size(a) for a in ("gx", "gy", "gz")}
    lower = {a: lax.rem(index[a] + count[a] - 1, count[a]) for a in index}
    upper = {a: lax.rem(index[a] + 1, count[a]) for a in index}
    has_lower = {a: index[a] > 0 for a in index}
    has_upper = {a: index[a] < count[a] - 1 for a in index}

    barrier = pltpu.get_barrier_semaphore()
    for a in ("gx", "gy", "gz"):
        pl.semaphore_signal(barrier, inc=1, device_id={a: lower[a]}, device_id_type=MESH)
        pl.semaphore_signal(barrier, inc=1, device_id={a: upper[a]}, device_id_type=MESH)

    sources = (*(load_in.at[c] for c in range(3)), labels_in, mask_in, table_in, *tables)
    targets = (*(load.at[c] for c in range(3)), labels, mask, table, fwd, bwd, into, out_of, eigen_x, eigen_rows)
    fetched = [
        pltpu.make_async_copy(source, target, in_sem.at[number])
        for number, (source, target) in enumerate(zip(sources, targets))
    ]
    for copy in fetched:
        copy.start()

    def copies(slot, phase, down, up):
        a = AXIS[phase]
        made = []
        for side, (source, target), device in ((0, down, lower[a]), (1, up, upper[a])):
            number = (slot * PHASES + phase) * 2 + side
            made.append(pltpu.make_async_remote_copy(
                src_ref=source, dst_ref=target,
                send_sem=send_sem.at[number], recv_sem=recv_sem.at[number],
                device_id={a: device}, device_id_type=MESH,
            ))
        return made

    pending = {}

    def send(slot, phase, down, up):
        made = copies(slot, phase, down, up)
        for copy, there in zip(made, (has_lower, has_upper)):
            pl.when(there[AXIS[phase]])(copy.start)
        pending[slot, phase] = made

    def arrive(slot, phase):
        for copy, there in zip(pending[slot, phase], (has_upper, has_lower)):
            pl.when(there[AXIS[phase]])(copy.wait_recv)

    def flat(ref, slot):
        return ref.at[slot].reshape(PLANES * LENGTH, LANES)

    def keep(flag, values):
        return jnp.where(flag, values, 0.0)

    lanes = lax.broadcasted_iota(jnp.int32, (LANES, LANES), 1)

    def face_columns(values):
        flat = values.reshape(BRICK * BRICK, LANES)
        total = jnp.zeros((LANES, LANES), F32)
        for i in range(8):
            part = pltpu.roll(flat[i * LANES:(i + 1) * LANES], 2 * i + 1, 1)
            total = jnp.where((lanes == 2 * i) | (lanes == 2 * i + 1), part, total)
        return jnp.transpose(total)[:16]

    def y_pack(slot, values):
        cys[slot, 0] = values[:, 0, :]
        cys[slot, 1] = values[:, BRICK - 1, :]

    def y_send(slot):
        send(slot, CY, (cys.at[slot, 0], cyr.at[slot, 1]), (cys.at[slot, 1], cyr.at[slot, 0]))

    def xz_pack(slot, values):
        czs[slot, 0] = values[0]
        czs[slot, 1] = values[BRICK - 1]
        cxs[slot] = face_columns(values)

    def xz_send(slot):
        send(slot, CZ, (czs.at[slot, 0], czr.at[slot, 1]), (czs.at[slot, 1], czr.at[slot, 0]))
        send(slot, CX, (cxs.at[slot], cxr.at[slot, 1]), (cxs.at[slot], cxr.at[slot, 0]))

    def halo_get(slot, low_y, high_y):
        for phase in (CZ, CX):
            arrive(slot, phase)
        low_z = keep(has_lower["gz"], czr[slot, 0])
        high_z = keep(has_upper["gz"], czr[slot, 1])
        left = keep(has_lower["gx"], cxr[slot, 0])
        right = keep(has_upper["gx"], cxr[slot, 1])
        odd = lax.rem(lax.broadcasted_iota(jnp.int32, (16, LANES), 0), 2) == 1
        both = jnp.where(odd, pltpu.roll(left, 1, 0), pltpu.roll(right, 15, 0))
        side = jnp.transpose(jnp.concatenate([both, jnp.zeros((LANES - 16, LANES), F32)], axis=0))
        side = jnp.concatenate(
            [pltpu.roll(side, LANES - 1 - 2 * i, 1) for i in range(8)], axis=0
        ).reshape(BRICK, BRICK, LANES)
        return low_y, high_y, low_z, high_z, side

    def shifts(values, halo):
        low_y, high_y, low_z, high_z, side = halo
        lane = lax.broadcasted_iota(jnp.int32, values.shape, 2)
        yield jnp.concatenate([low_z[None], values[:-1]], axis=0)
        yield jnp.concatenate([values[1:], high_z[None]], axis=0)
        yield jnp.concatenate([low_y[:, None, :], values[:, :-1]], axis=1)
        yield jnp.concatenate([values[:, 1:], high_y[:, None, :]], axis=1)
        yield jnp.where(lane == 0, side, pltpu.roll(values, 1, 2))
        yield jnp.where(lane == LANES - 1, side, pltpu.roll(values, LANES - 1, 2))

    def a_pack(s, c):
        slot = s * 3 + c
        if s == 0:
            values = load[c]
            w[slot, 0:BRICK, 0:BRICK, :] = values
        else:
            values = w[slot, 0:BRICK, 0:BRICK, :]
        ys[slot, 0] = values[:, 0:MARGIN, :]
        ys[slot, 1] = values[:, BRICK - MARGIN:BRICK, :]

    def z_planes(ref, slot, rows):
        def at(first):
            return ref.at[slot, pl.ds(first, MARGIN), rows]

        return (at(0), at(BRICK + MARGIN)), (at(BRICK - MARGIN), at(BRICK))

    def a_send(s, c):
        slot = s * 3 + c
        send(slot, AY, (ys.at[slot, 0], yr.at[slot, 1]), (ys.at[slot, 1], yr.at[slot, 0]))
        send(slot, AZ, *z_planes(w, slot, pl.ds(0, BRICK)))

    def a_z(s, c):
        slot = s * 3 + c
        arrive(slot, AY)
        low = keep(has_lower["gy"], yr[slot, 0])
        high = keep(has_upper["gy"], yr[slot, 1])
        w[slot, 0:BRICK, BRICK:LENGTH, :] = jnp.concatenate([low, high], axis=1)
        send(slot, AE, *z_planes(w, slot, pl.ds(BRICK, 2 * MARGIN)))

    def a_x(s, c):
        slot = s * 3 + c
        arrive(slot, AZ)
        arrive(slot, AE)
        low = w[slot, BRICK:BRICK + MARGIN]
        w[slot, BRICK:BRICK + MARGIN] = keep(has_lower["gz"], low)
        high = w[slot, BRICK + MARGIN:LENGTH]
        w[slot, BRICK + MARGIN:LENGTH] = keep(has_upper["gz"], high)
        rows = flat(w, slot)
        total = jnp.zeros((LANES, LANES), F32)
        for i in range(CHUNKS):
            part = pltpu.roll(rows[i * LANES:(i + 1) * LANES, :], 8 * i + MARGIN, 1)
            total = jnp.where((lanes >= 8 * i) & (lanes < 8 * i + 8), part, total)
        total = jnp.transpose(total)[:CHUNKS * 8].reshape(CHUNKS, 8, LANES)
        xs[slot, 0] = total[:, MARGIN:]
        xs[slot, 1] = total[:, :MARGIN]
        send(slot, AX, (xs.at[slot, 0], xr.at[slot, 1]), (xs.at[slot, 1], xr.at[slot, 0]))

    one, two = (b1a, b1b), (b2a, b2b)

    def transform(matrix, source, target, strided, scale=None):
        def body(i, carry):
            outs = []
            for k in range(UNROLL):
                at = pl.ds(pl.multiple_of((i * UNROLL + k) * 2 * LENGTH, 8), 2 * LENGTH)
                values = jnp.concatenate([source[0][at, :], source[1][at, :]], axis=1)
                outs.append(dot(matrix[...], triple(values)))
            for k in range(UNROLL):
                at = pl.ds(pl.multiple_of((i * UNROLL + k) * 2 * LENGTH, 8), 2 * LENGTH)
                out = outs[k]
                if scale is not None:
                    out = out * scale[at, :]
                for half in range(2):
                    part = out[:, half * LANES:(half + 1) * LANES]
                    if strided:
                        for which in range(2):
                            spot = pl.ds((i * UNROLL + k) * 2 + which, LENGTH, stride=LENGTH)
                            target[half][spot, :] = part[which * LENGTH:(which + 1) * LENGTH]
                    else:
                        target[half][at, :] = part
            return carry

        lax.fori_loop(0, LENGTH // 2 // UNROLL, body, 0)

    def s1(s, c):
        slot = s * 3 + c
        arrive(slot, AX)

        rows = flat(w, slot)
        near = jnp.concatenate([keep(has_lower["gx"], xr[slot, 0]), keep(has_upper["gx"], xr[slot, 1])], axis=1)
        high = near.astype(BF16).astype(F32)
        near = jnp.concatenate([high, near - high, high], axis=1)
        sides = []
        for first in range(0, CHUNKS, 5):
            group = near[first:first + 5].reshape(-1, LANES)
            blank = jnp.zeros((LANES - group.shape[0], LANES), F32)
            sides.append(jnp.transpose(jnp.concatenate([group, blank], axis=0)))
        for first, last in GROUPS:
            parts = []
            for i in range(first, last):
                side = sides[i // 5]
                if i % 5:
                    side = pltpu.roll(side, LANES - 24 * (i % 5), 1)
                high, low = halves(rows[i * LANES:(i + 1) * LANES, :])
                parts.append(jnp.concatenate([high, low, high, side.astype(BF16)], axis=1))
            out = dot(jnp.concatenate(parts, axis=0), into[...])
            b1a[first * LANES:last * LANES, :] = out[:, :LANES]
            b1b[first * LANES:last * LANES, :] = out[:, LANES:]

        transform(fwd, one, two, True)

    def s2(s, c):
        transform(fwd, two, one, False, rinv.at[c])
        transform(bwd, one, two, True)

    def s3(s, c):
        slot = s * 3 + c
        transform(bwd, two, one, False)

        rows = flat(zb, slot)
        margin = jnp.zeros((LANES, LANES), F32)
        for first, last in GROUPS:
            parts = []
            for i in range(first, last):
                at = pl.ds(i * LANES, LANES)
                high, low = halves(b1a[at, :])
                tail = b1b[at, :]
                tail_high = tail.astype(BF16).astype(F32)
                packed = tail_high + pltpu.roll(tail - tail_high, 32, 1) + pltpu.roll(tail_high, 64, 1)
                parts.append(jnp.concatenate([high, low, high, packed.astype(BF16)], axis=1))
            out = dot(jnp.concatenate(parts, axis=0), out_of[...])
            rows[first * LANES:last * LANES, :] = out[:, :LANES]
            for i in range(first, last):
                part = out[(i - first) * LANES:(i - first + 1) * LANES, LANES:]
                margin += pltpu.roll(part, 8 * i, 1) if i else part
        margin = jnp.transpose(margin)[:CHUNKS * 8].reshape(CHUNKS, 8, LANES)
        fs[slot, 0] = margin[:, :MARGIN]
        fs[slot, 1] = margin[:, MARGIN:]
        send(slot, BX, (fs.at[slot, 0], fr.at[slot, 1]), (fs.at[slot, 1], fr.at[slot, 0]))

    def b_z(s, c):
        slot = s * 3 + c
        arrive(slot, BX)

        near = jnp.concatenate([keep(has_upper["gx"], fr[slot, 1]), keep(has_lower["gx"], fr[slot, 0])], axis=1)
        blank = jnp.zeros((LANES - CHUNKS * 8, LANES), F32)
        side = jnp.transpose(jnp.concatenate([near.reshape(CHUNKS * 8, LANES), blank], axis=0))
        rows = flat(zb, slot)
        edge = (lanes < MARGIN) | (lanes >= LANES - MARGIN)

        def add(first, last):
            for i in range(first, last):
                at = pl.ds(i * LANES, LANES)
                rows[at, :] += jnp.where(edge, pltpu.roll(side, LANES - 8 * i - MARGIN, 1), 0.0)

        whole = OWNED // LANES
        add(whole, CHUNKS)
        send(
            slot, BZ,
            (zb.at[slot, pl.ds(BRICK, MARGIN)], zr.at[slot, 1]),
            (zb.at[slot, pl.ds(BRICK + MARGIN, MARGIN)], zr.at[slot, 0]),
        )
        add(0, whole)

    def b_y(s, c):
        slot = s * 3 + c
        arrive(slot, BZ)
        zb[slot, 0:MARGIN] += keep(has_lower["gz"], zr[slot, 0])
        zb[slot, BRICK - MARGIN:BRICK] += keep(has_upper["gz"], zr[slot, 1])
        other = slot + 3 * SWEEPS
        rows = zb[slot, 0:BRICK, BRICK:LENGTH, :]
        ys[other, 0] = rows[:, :MARGIN]
        ys[other, 1] = rows[:, MARGIN:]
        y_pack(slot, zb[slot, 0:BRICK, 0:BRICK, :])
        send(slot, BY, (ys.at[other, 0], yr.at[other, 1]), (ys.at[other, 1], yr.at[other, 0]))
        y_send(slot)

    def c_start(s, c):
        slot = s * 3 + c
        arrive(slot, BY)
        other = slot + 3 * SWEEPS
        low = keep(has_lower["gy"], yr[other, 0])
        high = keep(has_upper["gy"], yr[other, 1])
        own = zb[slot, 0:BRICK, 0:BRICK, :]
        blank = jnp.zeros((BRICK, MARGIN, LANES), F32)
        own = jnp.concatenate([
            own[:, :8] + jnp.concatenate([low, blank], axis=1),
            own[:, 8:24],
            own[:, 24:] + jnp.concatenate([blank, high], axis=1),
        ], axis=1)
        corr[slot] = own
        xz_pack(slot, own)
        xz_send(slot)
        if s == SWEEPS - 1:
            total = own
            for before in range(s):
                total = corr[before * 3 + c] + total
            disp[c] = total

    def update(s, c):
        slot = s * 3 + c
        arrive(slot, CY)
        margins = zb[slot, 0:BRICK, BRICK:LENGTH, :]
        halo = halo_get(
            slot,
            keep(has_lower["gy"], cyr[slot, 0] + margins[:, MARGIN - 1, :]),
            keep(has_upper["gy"], cyr[slot, 1] + margins[:, MARGIN, :]),
        )
        values = corr[slot]
        total = centre[c] * values
        moved = list(shifts(values, halo))
        for k in range(3):
            part = faces[2 * k] * moved[2 * k] + faces[2 * k + 1] * moved[2 * k + 1]
            total = total - (part * ratio(c, k) if ratio(c, k) != 1.0 else part)
        if s == SWEEPS - 1:
            resid[c] = w[slot, 0:BRICK, 0:BRICK, :] - total
        else:
            w[slot + 3, 0:BRICK, 0:BRICK, :] = w[slot, 0:BRICK, 0:BRICK, :] - total
            a_pack(s + 1, c)
            a_send(s + 1, c)

    def stiff(s, c):
        arrive(6, CY)
        own = modulus[...]
        low, high = keep(has_lower["gy"], cyr[6, 0]), keep(has_upper["gy"], cyr[6, 1])
        for number, moved in enumerate(shifts(own, halo_get(6, low, high))):
            faces[number] = 0.5 * (own + moved)
        sums = [faces[2 * k] + faces[2 * k + 1] for k in range(3)]
        for component in range(3):
            total = SIGMA_SHIFT * own
            for k in range(3):
                total = total + ratio(component, k) * sums[k]
            centre[component] = total

    for c in range(3):
        fetched[c].wait()
        a_pack(0, c)
        if c == 0:
            pl.semaphore_wait(barrier, 6)
        a_send(0, c)
    for slot in range(6):
        w[slot, LENGTH:] = jnp.zeros((PLANES - LENGTH, LENGTH, LANES), F32)

    for copy in fetched[3:]:
        copy.wait()

    def look(z, carry):
        picked = labels[z]
        value = jnp.zeros(picked.shape, F32)
        for number in range(table.shape[0]):
            value = jnp.where(picked == number, table[number], value)
        modulus[z] = jnp.where(mask[z] == 1, value, VOID_MODULUS)
        return carry

    lax.fori_loop(0, BRICK, look, 0)
    y_pack(6, modulus[...])
    xz_pack(6, modulus[...])
    y_send(6)
    xz_send(6)

    for c in range(3):
        def invert(y, carry, c=c):
            at = pl.ds(pl.multiple_of(y * LENGTH, 8), LENGTH)
            rinv[c, at, :] = 1.0 / (REF_MODULUS * (
                ratio(c, 0) * eigen_rows[...]
                + ratio(c, 1) * eigen_rows[pl.ds(y, 1), :]
                + ratio(c, 2) * eigen_x[...]
                + SIGMA_SHIFT
            ))
            return carry

        lax.fori_loop(0, LENGTH, invert, 0)

    stages = dict(a_z=a_z, a_x=a_x, s1=s1, s2=s2, s3=s3, b_z=b_z, b_y=b_y, c_start=c_start, update=update,
                  stiff=stiff)
    for s, c, name in ORDER:
        stages[name](s, c)

    for (_, phase), made in pending.items():
        for copy, there in zip(made, (has_lower, has_upper)):
            pl.when(there[AXIS[phase]])(copy.wait_send)


def local(load, labels, mask, table):
    tables = constants()
    vmem = pl.BlockSpec(memory_space=pltpu.VMEM)
    hbm = pl.BlockSpec(memory_space=pltpu.HBM)
    slots = 3 * SWEEPS
    field = jax.ShapeDtypeStruct(load.shape, F32)
    block = (BRICK, BRICK, LANES)
    return pl.pallas_call(
        kernel,
        out_shape=(field, field),
        in_specs=[hbm] * (4 + len(tables)),
        out_specs=(vmem, vmem),
        scratch_shapes=[
            pltpu.VMEM(block, F32),
            pltpu.VMEM((6,) + block, F32),
            pltpu.VMEM((3,) + block, F32),
            pltpu.VMEM((slots, PLANES, LENGTH, LANES), F32),
            pltpu.VMEM((slots, 2, CHUNKS, MARGIN, LANES), F32),
            pltpu.VMEM((slots, 2, CHUNKS, MARGIN, LANES), F32),
            pltpu.VMEM((PADDED, LANES), F32),
            pltpu.VMEM((PADDED, LANES), F32),
            pltpu.VMEM((PADDED, LANES), F32),
            pltpu.VMEM((PADDED, LANES), F32),
            pltpu.VMEM((slots, PLANES, LENGTH, LANES), F32),
            pltpu.VMEM((slots, 2, CHUNKS, MARGIN, LANES), F32),
            pltpu.VMEM((slots, 2, CHUNKS, MARGIN, LANES), F32),
            pltpu.VMEM((slots, 2, MARGIN, LENGTH, LANES), F32),
            pltpu.VMEM((2 * slots, 2, BRICK, MARGIN, LANES), F32),
            pltpu.VMEM((2 * slots, 2, BRICK, MARGIN, LANES), F32),
            pltpu.VMEM((slots,) + block, F32),
            pltpu.VMEM((3, ROWS, WIDE), F32),
            pltpu.VMEM((slots + 1, 2, BRICK, LANES), F32),
            pltpu.VMEM((slots + 1, 2, BRICK, LANES), F32),
            pltpu.VMEM((slots + 1, 2, BRICK, LANES), F32),
            pltpu.VMEM((slots + 1, 2, BRICK, LANES), F32),
            pltpu.VMEM((slots + 1, 16, LANES), F32),
            pltpu.VMEM((slots + 1, 2, 16, LANES), F32),
            pltpu.SemaphoreType.DMA(((slots + 1) * PHASES * 2,)),
            pltpu.SemaphoreType.DMA(((slots + 1) * PHASES * 2,)),
            pltpu.SemaphoreType.DMA((6 + len(tables),)),
            pltpu.VMEM(load.shape, F32),
            pltpu.VMEM(block, jnp.int32),
            pltpu.VMEM(block, jnp.int32),
            pltpu.SMEM(table.shape, F32),
        ] + [pltpu.VMEM(t.shape, t.dtype) for t in tables] + [
        ],
        compiler_params=pltpu.CompilerParams(
            collective_id=0, has_side_effects=True, vmem_limit_bytes=44 * 1024 * 1024
        ),
    )(*(pltpu.with_memory_space_constraint(v, pltpu.HBM) for v in (load, labels, mask, table, *map(jnp.asarray, tables))))


def solution(mesh):
    placed = (P(None, "gz", "gy", "gx"), P("gz", "gy", "gx"), P("gz", "gy", "gx"), P())
    return jax.shard_map(
        local,
        mesh=mesh,
        in_specs=placed,
        out_specs=(P(None, "gz", "gy", "gx"), P(None, "gz", "gy", "gx")),
        check_vma=False,
    )
```

```python
import jax
import jax.numpy as jnp
import numpy as np
from jax import lax
from jax.experimental import pallas as pl
from jax.experimental.pallas import tpu as pltpu
from jax.sharding import PartitionSpec as P

BRICK = 32
MARGIN = 4
SWEEPS = 2
LENGTH = BRICK + 2 * MARGIN
LANES = 128
WIDE = 256
ROWS = LENGTH * LENGTH
PADDED = 1664
CHUNKS = PADDED // LANES
OWNED = BRICK * LENGTH
LAMBDA_RATIO = 2.0
SIGMA_SHIFT = 0.1
REF_MODULUS = 1.5
VOID_MODULUS = 0.1
MESH = pl.DeviceIdType.MESH
UNROLL = 20
GROUPS = ((0, 4), (4, 8), (8, 13))
PHASES = 10
AY, AZ, AE, AX, BX, BZ, BY, CY, CZ, CX = range(PHASES)
AXIS = ("gy", "gz", "gz", "gx", "gx", "gz", "gy", "gy", "gz", "gx")
PLANES = 42
TABLES = 6
ORDER = (
    (0, 0, "a_z"), (0, 1, "a_z"), (0, 0, "a_x"), (0, 2, "a_z"), (0, 1, "a_x"), (0, 0, "s1"), (0, 0, "s2"),
    (0, 0, "s3"), (0, 2, "a_x"), (0, 1, "s1"), (0, 0, "b_z"), (0, 1, "s2"), (0, 1, "s3"), (0, 0, "b_y"),
    (0, 2, "s1"), (0, 1, "b_z"), (0, 2, "s2"), (0, 2, "s3"), (0, 0, "c_start"), (0, 1, "b_y"), (0, 0, "stiff"),
    (0, 2, "b_z"), (0, 0, "update"), (0, 1, "c_start"), (0, 2, "b_y"), (0, 1, "update"), (1, 0, "a_z"),
    (0, 2, "c_start"), (1, 0, "a_x"), (1, 1, "a_z"), (0, 2, "update"), (1, 0, "s1"), (1, 1, "a_x"), (1, 0, "s2"),
    (1, 0, "s3"), (1, 2, "a_z"), (1, 1, "s1"), (1, 1, "s2"), (1, 2, "a_x"), (1, 0, "b_z"), (1, 1, "s3"),
    (1, 2, "s1"), (1, 2, "s2"), (1, 1, "b_z"), (1, 2, "s3"), (1, 0, "b_y"), (1, 1, "b_y"), (1, 2, "b_z"),
    (1, 2, "b_y"), (1, 0, "c_start"), (1, 1, "c_start"), (1, 2, "c_start"), (1, 1, "update"), (1, 0, "update"),
    (1, 2, "update"),
)
F32 = jnp.float32
BF16 = jnp.bfloat16


def ratio(component, direction):
    return LAMBDA_RATIO if component == direction else 1.0


def halves(values):
    high = values.astype(BF16)
    return high, (values - high.astype(F32)).astype(BF16)


def constants():
    grid = np.arange(1, LENGTH + 1, dtype=np.float64)
    sine = np.sqrt(2.0 / (LENGTH + 1)) * np.sin(np.pi * grid[:, None] * grid[None, :] / (LENGTH + 1))
    eigen = 2.0 - 2.0 * np.cos(np.pi * grid / (LENGTH + 1))
    spot = np.arange(LENGTH, dtype=np.float64)
    ramp = np.minimum(np.minimum((spot + 0.5) / (2 * MARGIN), (LENGTH - 0.5 - spot) / (2 * MARGIN)), 1.0)
    ramped = ramp[:, None] * sine
    place = np.concatenate([np.arange(MARGIN, MARGIN + BRICK), np.arange(MARGIN), np.arange(MARGIN + BRICK, LENGTH)])
    forward = ramped[place].T
    backward = sine.T[place]
    count = LANES // BRICK
    wide_x = LANES + 2 * MARGIN
    forward_x = np.zeros((wide_x, WIDE))
    backward_x = np.zeros((WIDE, wide_x))
    for brick in range(count):
        rows = slice(brick * BRICK, brick * BRICK + LENGTH)
        columns = slice(brick * LENGTH, (brick + 1) * LENGTH)
        forward_x[rows, columns] = ramped
        backward_x[columns, rows] = sine
    edge = slice(LANES, LANES + 2 * MARGIN)
    into = forward_x[MARGIN:MARGIN + LANES]
    into_edge = np.concatenate([forward_x[:MARGIN], forward_x[MARGIN + LANES:]])
    out = np.zeros((WIDE, WIDE))
    out[:, :LANES] = backward_x[:, MARGIN:MARGIN + LANES]
    out[:, edge] = np.concatenate([backward_x[:, :MARGIN], backward_x[:, MARGIN + LANES:]], axis=1)
    rest = count * LENGTH - LANES
    eigen_x = np.zeros((1, WIDE))
    eigen_x[0, : count * LENGTH] = np.tile(eigen, count)
    eigen_lanes = np.broadcast_to(eigen[:, None], (LENGTH, WIDE))

    def high(matrix):
        return matrix.astype(np.float32).astype(BF16).astype(np.float64)

    def low(matrix):
        return matrix - high(matrix)

    def pair(matrix):
        zero = np.zeros((LENGTH, LENGTH))
        both = np.block([[matrix, zero], [zero, matrix]])
        return np.concatenate([high(both), high(both), low(both)], axis=1)

    def tall(*parts):
        blank = np.zeros((4 * LANES - sum(p.shape[0] for p in parts), WIDE))
        return np.concatenate(parts + (blank,))

    head, tail = out[:LANES], out[LANES:LANES + rest]
    return [m.astype(BF16) for m in (
        pair(forward),
        pair(backward),
        tall(high(into), high(into), low(into), high(into_edge), high(into_edge), low(into_edge)),
        tall(high(head), high(head), low(head), high(tail), high(tail), low(tail)),
    )] + [eigen_x.astype(np.float32), np.ascontiguousarray(eigen_lanes).astype(np.float32)]


def dot(a, b):
    return jnp.dot(a, b, preferred_element_type=F32)


def triple(values):
    high, low = halves(values)
    return jnp.concatenate([high, low, high], axis=0)


def kernel(
    load_in, labels_in, mask_in, table_in, *rest,
):
    tables = rest[:TABLES]
    (
        disp, resid, modulus, faces, centre, w, xs, xr, b1a, b1b, b2a, b2b, zb, fs, fr, zr, ys, yr, corr, rinv,
        cys, cyr, czs, czr, cxs, cxr, send_sem, recv_sem, in_sem,
        load, labels, mask, table, fwd, bwd, into, out_of, eigen_x, eigen_rows,
    ) = rest[TABLES:]
    index = {a: lax.axis_index(a) for a in ("gx", "gy", "gz")}
    count = {a: lax.axis_size(a) for a in ("gx", "gy", "gz")}
    lower = {a: lax.rem(index[a] + count[a] - 1, count[a]) for a in index}
    upper = {a: lax.rem(index[a] + 1, count[a]) for a in index}
    has_lower = {a: index[a] > 0 for a in index}
    has_upper = {a: index[a] < count[a] - 1 for a in index}

    barrier = pltpu.get_barrier_semaphore()
    for a in ("gx", "gy", "gz"):
        pl.semaphore_signal(barrier, inc=1, device_id={a: lower[a]}, device_id_type=MESH)
        pl.semaphore_signal(barrier, inc=1, device_id={a: upper[a]}, device_id_type=MESH)

    sources = (*(load_in.at[c] for c in range(3)), labels_in, mask_in, table_in, *tables)
    targets = (*(load.at[c] for c in range(3)), labels, mask, table, fwd, bwd, into, out_of, eigen_x, eigen_rows)
    fetched = [
        pltpu.make_async_copy(source, target, in_sem.at[number])
        for number, (source, target) in enumerate(zip(sources, targets))
    ]
    for copy in fetched:
        copy.start()

    def copies(slot, phase, down, up):
        a = AXIS[phase]
        made = []
        for side, (source, target), device in ((0, down, lower[a]), (1, up, upper[a])):
            number = (slot * PHASES + phase) * 2 + side
            made.append(pltpu.make_async_remote_copy(
                src_ref=source, dst_ref=target,
                send_sem=send_sem.at[number], recv_sem=recv_sem.at[number],
                device_id={a: device}, device_id_type=MESH,
            ))
        return made

    pending = {}

    def send(slot, phase, down, up):
        made = copies(slot, phase, down, up)
        for copy, there in zip(made, (has_lower, has_upper)):
            pl.when(there[AXIS[phase]])(copy.start)
        pending[slot, phase] = made

    def arrive(slot, phase):
        for copy, there in zip(pending[slot, phase], (has_upper, has_lower)):
            pl.when(there[AXIS[phase]])(copy.wait_recv)

    def flat(ref, slot):
        return ref.at[slot].reshape(PLANES * LENGTH, LANES)

    def keep(flag, values):
        return jnp.where(flag, values, 0.0)

    lanes = lax.broadcasted_iota(jnp.int32, (LANES, LANES), 1)

    def face_columns(values):
        flat = values.reshape(BRICK * BRICK, LANES)
        total = jnp.zeros((LANES, LANES), F32)
        for i in range(8):
            part = pltpu.roll(flat[i * LANES:(i + 1) * LANES], 2 * i + 1, 1)
            total = jnp.where((lanes == 2 * i) | (lanes == 2 * i + 1), part, total)
        return jnp.transpose(total)[:16]

    def y_pack(slot, values):
        cys[slot, 0] = values[:, 0, :]
        cys[slot, 1] = values[:, BRICK - 1, :]

    def y_send(slot):
        send(slot, CY, (cys.at[slot, 0], cyr.at[slot, 1]), (cys.at[slot, 1], cyr.at[slot, 0]))

    def xz_pack(slot, values):
        czs[slot, 0] = values[0]
        czs[slot, 1] = values[BRICK - 1]
        cxs[slot] = face_columns(values)

    def xz_send(slot):
        send(slot, CZ, (czs.at[slot, 0], czr.at[slot, 1]), (czs.at[slot, 1], czr.at[slot, 0]))
        send(slot, CX, (cxs.at[slot], cxr.at[slot, 1]), (cxs.at[slot], cxr.at[slot, 0]))

    def halo_get(slot, low_y, high_y):
        for phase in (CZ, CX):
            arrive(slot, phase)
        low_z = keep(has_lower["gz"], czr[slot, 0])
        high_z = keep(has_upper["gz"], czr[slot, 1])
        left = keep(has_lower["gx"], cxr[slot, 0])
        right = keep(has_upper["gx"], cxr[slot, 1])
        odd = lax.rem(lax.broadcasted_iota(jnp.int32, (16, LANES), 0), 2) == 1
        both = jnp.where(odd, pltpu.roll(left, 1, 0), pltpu.roll(right, 15, 0))
        side = jnp.transpose(jnp.concatenate([both, jnp.zeros((LANES - 16, LANES), F32)], axis=0))
        side = jnp.concatenate(
            [pltpu.roll(side, LANES - 1 - 2 * i, 1) for i in range(8)], axis=0
        ).reshape(BRICK, BRICK, LANES)
        return low_y, high_y, low_z, high_z, side

    def shifts(values, halo):
        low_y, high_y, low_z, high_z, side = halo
        lane = lax.broadcasted_iota(jnp.int32, values.shape, 2)
        yield jnp.concatenate([low_z[None], values[:-1]], axis=0)
        yield jnp.concatenate([values[1:], high_z[None]], axis=0)
        yield jnp.concatenate([low_y[:, None, :], values[:, :-1]], axis=1)
        yield jnp.concatenate([values[:, 1:], high_y[:, None, :]], axis=1)
        yield jnp.where(lane == 0, side, pltpu.roll(values, 1, 2))
        yield jnp.where(lane == LANES - 1, side, pltpu.roll(values, LANES - 1, 2))

    def a_pack(s, c):
        slot = s * 3 + c
        if s == 0:
            values = load[c]
            w[slot, 0:BRICK, 0:BRICK, :] = values
        else:
            values = w[slot, 0:BRICK, 0:BRICK, :]
        ys[slot, 0] = values[:, 0:MARGIN, :]
        ys[slot, 1] = values[:, BRICK - MARGIN:BRICK, :]

    def z_planes(ref, slot, rows):
        def at(first):
            return ref.at[slot, pl.ds(first, MARGIN), rows]

        return (at(0), at(BRICK + MARGIN)), (at(BRICK - MARGIN), at(BRICK))

    def a_send(s, c):
        slot = s * 3 + c
        send(slot, AY, (ys.at[slot, 0], yr.at[slot, 1]), (ys.at[slot, 1], yr.at[slot, 0]))
        send(slot, AZ, *z_planes(w, slot, pl.ds(0, BRICK)))

    def a_z(s, c):
        slot = s * 3 + c
        arrive(slot, AY)
        low = keep(has_lower["gy"], yr[slot, 0])
        high = keep(has_upper["gy"], yr[slot, 1])
        w[slot, 0:BRICK, BRICK:LENGTH, :] = jnp.concatenate([low, high], axis=1)
        send(slot, AE, *z_planes(w, slot, pl.ds(BRICK, 2 * MARGIN)))

    def a_x(s, c):
        slot = s * 3 + c
        arrive(slot, AZ)
        arrive(slot, AE)
        low = w[slot, BRICK:BRICK + MARGIN]
        w[slot, BRICK:BRICK + MARGIN] = keep(has_lower["gz"], low)
        high = w[slot, BRICK + MARGIN:LENGTH]
        w[slot, BRICK + MARGIN:LENGTH] = keep(has_upper["gz"], high)
        rows = flat(w, slot)
        total = jnp.zeros((LANES, LANES), F32)
        for i in range(CHUNKS):
            part = pltpu.roll(rows[i * LANES:(i + 1) * LANES, :], 8 * i + MARGIN, 1)
            total = jnp.where((lanes >= 8 * i) & (lanes < 8 * i + 8), part, total)
        total = jnp.transpose(total)[:CHUNKS * 8].reshape(CHUNKS, 8, LANES)
        xs[slot, 0] = total[:, MARGIN:]
        xs[slot, 1] = total[:, :MARGIN]
        send(slot, AX, (xs.at[slot, 0], xr.at[slot, 1]), (xs.at[slot, 1], xr.at[slot, 0]))

    one, two = (b1a, b1b), (b2a, b2b)

    def transform(matrix, source, target, strided, scale=None):
        def body(i, carry):
            outs = []
            for k in range(UNROLL):
                at = pl.ds(pl.multiple_of((i * UNROLL + k) * 2 * LENGTH, 8), 2 * LENGTH)
                values = jnp.concatenate([source[0][at, :], source[1][at, :]], axis=1)
                outs.append(dot(matrix[...], triple(values)))
            for k in range(UNROLL):
                at = pl.ds(pl.multiple_of((i * UNROLL + k) * 2 * LENGTH, 8), 2 * LENGTH)
                out = outs[k]
                if scale is not None:
                    out = out * scale[at, :]
                for half in range(2):
                    part = out[:, half * LANES:(half + 1) * LANES]
                    if strided:
                        for which in range(2):
                            spot = pl.ds((i * UNROLL + k) * 2 + which, LENGTH, stride=LENGTH)
                            target[half][spot, :] = part[which * LENGTH:(which + 1) * LENGTH]
                    else:
                        target[half][at, :] = part
            return carry

        lax.fori_loop(0, LENGTH // 2 // UNROLL, body, 0)

    def s1(s, c):
        slot = s * 3 + c
        arrive(slot, AX)

        rows = flat(w, slot)
        near = jnp.concatenate([keep(has_lower["gx"], xr[slot, 0]), keep(has_upper["gx"], xr[slot, 1])], axis=1)
        high = near.astype(BF16).astype(F32)
        near = jnp.concatenate([high, near - high, high], axis=1)
        sides = []
        for first in range(0, CHUNKS, 5):
            group = near[first:first + 5].reshape(-1, LANES)
            blank = jnp.zeros((LANES - group.shape[0], LANES), F32)
            sides.append(jnp.transpose(jnp.concatenate([group, blank], axis=0)))
        for first, last in GROUPS:
            parts = []
            for i in range(first, last):
                side = sides[i // 5]
                if i % 5:
                    side = pltpu.roll(side, LANES - 24 * (i % 5), 1)
                high, low = halves(rows[i * LANES:(i + 1) * LANES, :])
                parts.append(jnp.concatenate([high, low, high, side.astype(BF16)], axis=1))
            out = dot(jnp.concatenate(parts, axis=0), into[...])
            b1a[first * LANES:last * LANES, :] = out[:, :LANES]
            b1b[first * LANES:last * LANES, :] = out[:, LANES:]

        transform(fwd, one, two, True)

    def s2(s, c):
        transform(fwd, two, one, False, rinv.at[c])
        transform(bwd, one, two, True)

    def s3(s, c):
        slot = s * 3 + c
        transform(bwd, two, one, False)

        rows = flat(zb, slot)
        margin = jnp.zeros((LANES, LANES), F32)
        for first, last in GROUPS:
            parts = []
            for i in range(first, last):
                at = pl.ds(i * LANES, LANES)
                high, low = halves(b1a[at, :])
                tail = b1b[at, :]
                tail_high = tail.astype(BF16).astype(F32)
                packed = tail_high + pltpu.roll(tail - tail_high, 32, 1) + pltpu.roll(tail_high, 64, 1)
                parts.append(jnp.concatenate([high, low, high, packed.astype(BF16)], axis=1))
            out = dot(jnp.concatenate(parts, axis=0), out_of[...])
            rows[first * LANES:last * LANES, :] = out[:, :LANES]
            for i in range(first, last):
                part = out[(i - first) * LANES:(i - first + 1) * LANES, LANES:]
                margin += pltpu.roll(part, 8 * i, 1) if i else part
        margin = jnp.transpose(margin)[:CHUNKS * 8].reshape(CHUNKS, 8, LANES)
        fs[slot, 0] = margin[:, :MARGIN]
        fs[slot, 1] = margin[:, MARGIN:]
        send(slot, BX, (fs.at[slot, 0], fr.at[slot, 1]), (fs.at[slot, 1], fr.at[slot, 0]))

    def b_z(s, c):
        slot = s * 3 + c
        arrive(slot, BX)

        near = jnp.concatenate([keep(has_upper["gx"], fr[slot, 1]), keep(has_lower["gx"], fr[slot, 0])], axis=1)
        blank = jnp.zeros((LANES - CHUNKS * 8, LANES), F32)
        side = jnp.transpose(jnp.concatenate([near.reshape(CHUNKS * 8, LANES), blank], axis=0))
        rows = flat(zb, slot)
        edge = (lanes < MARGIN) | (lanes >= LANES - MARGIN)

        def add(first, last):
            for i in range(first, last):
                at = pl.ds(i * LANES, LANES)
                rows[at, :] += jnp.where(edge, pltpu.roll(side, LANES - 8 * i - MARGIN, 1), 0.0)

        whole = OWNED // LANES
        add(whole, CHUNKS)
        send(
            slot, BZ,
            (zb.at[slot, pl.ds(BRICK, MARGIN)], zr.at[slot, 1]),
            (zb.at[slot, pl.ds(BRICK + MARGIN, MARGIN)], zr.at[slot, 0]),
        )
        add(0, whole)

    def b_y(s, c):
        slot = s * 3 + c
        arrive(slot, BZ)
        zb[slot, 0:MARGIN] += keep(has_lower["gz"], zr[slot, 0])
        zb[slot, BRICK - MARGIN:BRICK] += keep(has_upper["gz"], zr[slot, 1])
        other = slot + 3 * SWEEPS
        rows = zb[slot, 0:BRICK, BRICK:LENGTH, :]
        ys[other, 0] = rows[:, :MARGIN]
        ys[other, 1] = rows[:, MARGIN:]
        y_pack(slot, zb[slot, 0:BRICK, 0:BRICK, :])
        send(slot, BY, (ys.at[other, 0], yr.at[other, 1]), (ys.at[other, 1], yr.at[other, 0]))
        y_send(slot)

    def c_start(s, c):
        slot = s * 3 + c
        arrive(slot, BY)
        other = slot + 3 * SWEEPS
        low = keep(has_lower["gy"], yr[other, 0])
        high = keep(has_upper["gy"], yr[other, 1])
        own = zb[slot, 0:BRICK, 0:BRICK, :]
        blank = jnp.zeros((BRICK, MARGIN, LANES), F32)
        own = jnp.concatenate([
            own[:, :8] + jnp.concatenate([low, blank], axis=1),
            own[:, 8:24],
            own[:, 24:] + jnp.concatenate([blank, high], axis=1),
        ], axis=1)
        corr[slot] = own
        xz_pack(slot, own)
        xz_send(slot)
        if s == SWEEPS - 1:
            total = own
            for before in range(s):
                total = corr[before * 3 + c] + total
            disp[c] = total

    def update(s, c):
        slot = s * 3 + c
        arrive(slot, CY)
        margins = zb[slot, 0:BRICK, BRICK:LENGTH, :]
        halo = halo_get(
            slot,
            keep(has_lower["gy"], cyr[slot, 0] + margins[:, MARGIN - 1, :]),
            keep(has_upper["gy"], cyr[slot, 1] + margins[:, MARGIN, :]),
        )
        values = corr[slot]
        total = centre[c] * values
        moved = list(shifts(values, halo))
        for k in range(3):
            part = faces[2 * k] * moved[2 * k] + faces[2 * k + 1] * moved[2 * k + 1]
            total = total - (part * ratio(c, k) if ratio(c, k) != 1.0 else part)
        if s == SWEEPS - 1:
            resid[c] = w[slot, 0:BRICK, 0:BRICK, :] - total
        else:
            w[slot + 3, 0:BRICK, 0:BRICK, :] = w[slot, 0:BRICK, 0:BRICK, :] - total
            a_pack(s + 1, c)
            a_send(s + 1, c)

    def stiff(s, c):
        arrive(6, CY)
        own = modulus[...]
        low, high = keep(has_lower["gy"], cyr[6, 0]), keep(has_upper["gy"], cyr[6, 1])
        for number, moved in enumerate(shifts(own, halo_get(6, low, high))):
            faces[number] = 0.5 * (own + moved)
        sums = [faces[2 * k] + faces[2 * k + 1] for k in range(3)]
        for component in range(3):
            total = SIGMA_SHIFT * own
            for k in range(3):
                total = total + ratio(component, k) * sums[k]
            centre[component] = total

    for c in range(3):
        fetched[c].wait()
        a_pack(0, c)
        if c == 0:
            pl.semaphore_wait(barrier, 6)
        a_send(0, c)
    for slot in range(6):
        w[slot, LENGTH:] = jnp.zeros((PLANES - LENGTH, LENGTH, LANES), F32)

    for copy in fetched[3:]:
        copy.wait()

    def look(z, carry):
        picked = labels[z]
        value = jnp.zeros(picked.shape, F32)
        for number in range(table.shape[0]):
            value = jnp.where(picked == number, table[number], value)
        modulus[z] = jnp.where(mask[z] == 1, value, VOID_MODULUS)
        return carry

    lax.fori_loop(0, BRICK, look, 0)
    y_pack(6, modulus[...])
    xz_pack(6, modulus[...])
    y_send(6)
    xz_send(6)

    for c in range(3):
        def invert(y, carry, c=c):
            at = pl.ds(pl.multiple_of(y * LENGTH, 8), LENGTH)
            rinv[c, at, :] = 1.0 / (REF_MODULUS * (
                ratio(c, 0) * eigen_rows[...]
                + ratio(c, 1) * eigen_rows[pl.ds(y, 1), :]
                + ratio(c, 2) * eigen_x[...]
                + SIGMA_SHIFT
            ))
            return carry

        lax.fori_loop(0, LENGTH, invert, 0)

    stages = dict(a_z=a_z, a_x=a_x, s1=s1, s2=s2, s3=s3, b_z=b_z, b_y=b_y, c_start=c_start, update=update,
                  stiff=stiff)
    for s, c, name in ORDER:
        stages[name](s, c)

    for (_, phase), made in pending.items():
        for copy, there in zip(made, (has_lower, has_upper)):
            pl.when(there[AXIS[phase]])(copy.wait_send)


def local(load, labels, mask, table):
    tables = constants()
    vmem = pl.BlockSpec(memory_space=pltpu.VMEM)
    hbm = pl.BlockSpec(memory_space=pltpu.HBM)
    slots = 3 * SWEEPS
    field = jax.ShapeDtypeStruct(load.shape, F32)
    block = (BRICK, BRICK, LANES)
    return pl.pallas_call(
        kernel,
        out_shape=(field, field),
        in_specs=[hbm] * (4 + len(tables)),
        out_specs=(vmem, vmem),
        scratch_shapes=[
            pltpu.VMEM(block, F32),
            pltpu.VMEM((6,) + block, F32),
            pltpu.VMEM((3,) + block, F32),
            pltpu.VMEM((slots, PLANES, LENGTH, LANES), F32),
            pltpu.VMEM((slots, 2, CHUNKS, MARGIN, LANES), F32),
            pltpu.VMEM((slots, 2, CHUNKS, MARGIN, LANES), F32),
            pltpu.VMEM((PADDED, LANES), F32),
            pltpu.VMEM((PADDED, LANES), F32),
            pltpu.VMEM((PADDED, LANES), F32),
            pltpu.VMEM((PADDED, LANES), F32),
            pltpu.VMEM((slots, PLANES, LENGTH, LANES), F32),
            pltpu.VMEM((slots, 2, CHUNKS, MARGIN, LANES), F32),
            pltpu.VMEM((slots, 2, CHUNKS, MARGIN, LANES), F32),
            pltpu.VMEM((slots, 2, MARGIN, LENGTH, LANES), F32),
            pltpu.VMEM((2 * slots, 2, BRICK, MARGIN, LANES), F32),
            pltpu.VMEM((2 * slots, 2, BRICK, MARGIN, LANES), F32),
            pltpu.VMEM((slots,) + block, F32),
            pltpu.VMEM((3, ROWS, WIDE), F32),
            pltpu.VMEM((slots + 1, 2, BRICK, LANES), F32),
            pltpu.VMEM((slots + 1, 2, BRICK, LANES), F32),
            pltpu.VMEM((slots + 1, 2, BRICK, LANES), F32),
            pltpu.VMEM((slots + 1, 2, BRICK, LANES), F32),
            pltpu.VMEM((slots + 1, 16, LANES), F32),
            pltpu.VMEM((slots + 1, 2, 16, LANES), F32),
            pltpu.SemaphoreType.DMA(((slots + 1) * PHASES * 2,)),
            pltpu.SemaphoreType.DMA(((slots + 1) * PHASES * 2,)),
            pltpu.SemaphoreType.DMA((6 + len(tables),)),
            pltpu.VMEM(load.shape, F32),
            pltpu.VMEM(block, jnp.int32),
            pltpu.VMEM(block, jnp.int32),
            pltpu.SMEM(table.shape, F32),
        ] + [pltpu.VMEM(t.shape, t.dtype) for t in tables] + [
        ],
        compiler_params=pltpu.CompilerParams(
            collective_id=0, has_side_effects=True, vmem_limit_bytes=44 * 1024 * 1024
        ),
    )(*(pltpu.with_memory_space_constraint(v, pltpu.HBM) for v in (load, labels, mask, table, *map(jnp.asarray, tables))))


def solution(mesh):
    placed = (P(None, "gz", "gy", "gx"), P("gz", "gy", "gx"), P("gz", "gy", "gx"), P())
    return jax.shard_map(
        local,
        mesh=mesh,
        in_specs=placed,
        out_specs=(P(None, "gz", "gy", "gx"), P(None, "gz", "gy", "gx")),
        check_vma=False,
    )
```
